128 devices in a mesh: mesh: 16 (over y, x), src: 8 (over z, core).
Axes of the slice: x: 4, y: 4, z: 4, core: 2. Of those that a mesh axis runs over, the one named last changes fastest.
Arguments:
- right_side: float32 [262144, 256], P(('mesh', 'src')), may hold values from -6 to 6
- tile_stiff: float32 [32768, 32, 32], P(('mesh', 'src')), as said below
- tile_nodes: int32 [32768, 32], P(('mesh', 'src')), may hold values from 0 to 2304, as said below
- node_shift: float32 [262144], P(('mesh', 'src')), may hold values from 0.5 to 2
- slot_nodes: int32 [16, 32768], P(None, ('mesh', 'src')), may hold values from 0 to 2047
- slot_load: float32 [16, 98304], P(None, ('mesh', 'src')), may hold values from -6 to 6
- dipole_slot: int32 [16384], P(('mesh', 'src')), may hold values from 0 to 255, as said below
Outputs:
- solution: float32 [262144, 256], P(('mesh', 'src'))
- leadfield: float32 [3, 16384, 256], P(None, ('mesh', 'src'))
The draws below stay inside these ranges and needn't reach their ends.
Inputs may be any that keep to these rules, and one draw needn't show every extreme that they name: `tile_stiff`: every tile is symmetric positive definite. `tile_nodes`: the largest value marks a padded slot; every other value is a row of the partition's extended nodes. The live slots of one tile lie within 64 consecutive rows. `dipole_slot`: the 128 entries of one owner are distinct; at most 2 of one owner's entries name one source partition, and each owner has a source partition with exactly 2.
All inputs are finite; a program needn't handle non-finite values.
Results may differ from the reference program's by a relative error of at most 0.00018.
Values sent between devices are 32-bit elements; how exact they have to be, the bound alone decides.
No kernel may reach another device: no remote copies, remote signals or barrier semaphores. Data moves between devices by JAX's collectives and lax.ppermute only.
A program may use at most 128 MiB of HBM per device.

```python
import math
import jax
import jax.numpy as jnp
from jax import lax

E = 256
NODES_DEV = 2048
TILE = 32
HALO = 128
ITERS = 3
SUPPORT = 16
DIP_DEV = 128
TILE_DEV = 256
SLOTS = 256
CAP = 2
NODES = 262144
TILES = 32768
DIPOLES = 16384
DEVICES = 128


def draw_tile_stiff(key, part):
    first_key, second_key = jax.random.split(key)
    mixing = jax.random.normal(first_key, (TILES, TILE, TILE), jnp.float32)
    squared = jnp.einsum('tij,tkj->tik', mixing, mixing) / TILE
    scales = jnp.exp(jax.random.uniform(second_key, (TILES, 1, 1), jnp.float32, math.log(0.1), 0.0))
    return scales * (squared + 0.5 * jnp.eye(TILE, dtype=jnp.float32))


def draw_tile_nodes(key, part):
    ext_rows = NODES_DEV + 2 * HALO
    first_key, second_key, third_key = jax.random.split(key, 3)
    centers = jax.random.randint(first_key, (TILES, 1), 0, ext_rows - 2 * TILE + 1)
    offsets = jax.random.randint(second_key, (TILES, TILE), 0, 2 * TILE)
    live_count = jax.random.randint(third_key, (TILES, 1), 3 * TILE // 4, TILE + 1)
    positions = jnp.arange(TILE, dtype=jnp.int32)[None, :]
    return jnp.where(positions < live_count, centers + offsets, ext_rows).astype(jnp.int32)


def draw_dipole_slot(key, part):
    peer_total = DIPOLES // DIP_DEV
    per_peer = SLOTS // peer_total
    first_key, second_key = jax.random.split(key)
    penalty = jax.random.randint(first_key, (peer_total,), 0, 2 * SLOTS)
    slot_ids = jnp.arange(SLOTS, dtype=jnp.int32)
    sources = slot_ids // per_peer

    def one_owner(owner_key):
        perm_key, pick_key = jax.random.split(owner_key)
        shuffled = jax.random.permutation(perm_key, SLOTS).astype(jnp.int32)
        chosen = jax.random.randint(pick_key, (), 0, peer_total)
        scores = (shuffled + penalty[sources]) * SLOTS + slot_ids
        scores = jnp.where(sources == chosen, slot_ids % per_peer - per_peer, scores)
        return jnp.argsort(scores, stable=True)[:DIP_DEV].astype(jnp.int32)
    owner_keys = jax.random.split(second_key, peer_total)
    return jax.vmap(one_owner)(owner_keys).reshape(-1).astype(jnp.int32)


def touch_ends(result, key, smallest, high):
    index_at = [jax.random.randint(jax.random.fold_in(key, axis), (), 0, length) for axis, length in enumerate(result.shape)]
    longest = result.shape.index(max(result.shape))
    next_to = index_at[:longest] + [(index_at[longest] + 1) % result.shape[longest]] + index_at[longest + 1:]
    return result.at[tuple(index_at)].set(smallest).at[tuple(next_to)].set(high)


def levels(key, shape, pieces, smallest, largest):
    factor_of, own = 1.0, jax.random.fold_in(key, 6)
    for axis_at, parts in pieces:
        steps = jnp.exp(jax.random.uniform(jax.random.fold_in(own, axis_at), (parts,), jnp.float32, smallest / len(pieces), largest / len(pieces)))
        factor_of = factor_of * jnp.repeat(steps, shape[axis_at] // parts).reshape([-1 if axis == axis_at else 1 for axis in range(len(shape))])
    return factor_of


def scatter_about(stream_key, extent, spread, bound, pieces=(), kind=jnp.bfloat16):
    values = spread * jax.random.normal(stream_key, extent, jnp.float32)
    if pieces:
        values = values * levels(stream_key, extent, pieces, -0.22, 0.18)
    return jnp.clip(values, -bound, bound).astype(kind)


def setup_inputs(seed: int = 0) -> dict:
    key_list = jax.random.split(jax.random.key(seed), 8)
    return {
        "right_side": scatter_about(key_list[0], (NODES, E), 1.0, 6.0, ((0, 128),), jnp.float32),
        "tile_stiff": draw_tile_stiff(jax.random.fold_in(key_list[7], 71), 0),
        "tile_nodes": draw_tile_nodes(jax.random.fold_in(key_list[7], 71), 0),
        "node_shift": jnp.clip(jnp.exp(math.log(2.0) - 1.3862944 * jax.random.uniform(key_list[3], (NODES,), jnp.float32) ** levels(key_list[3], (NODES,), ((0, 128),), -0.2, 0.2)), 0.5, 2.0),
        "slot_nodes": touch_ends(jax.random.randint(key_list[4], (SUPPORT, SLOTS * DEVICES), 0, NODES_DEV), jax.random.fold_in(key_list[4], 1), 0, NODES_DEV - 1).astype(jnp.int32),
        "slot_load": scatter_about(key_list[5], (SUPPORT, 3 * SLOTS * DEVICES), 1.0, 6.0, ((1, 128),), jnp.float32),
        "dipole_slot": draw_dipole_slot(jax.random.fold_in(key_list[7], 71), 0),
    }


PRECISE = lax.Precision.HIGHEST

def inner_products(former, latter):
    return jnp.dot(former.T.astype(jnp.float32), latter.astype(jnp.float32), preferred_element_type=jnp.float32, precision=PRECISE)

def times_matrix(former, latter):
    return jnp.dot(former.astype(jnp.float32), latter.astype(jnp.float32), preferred_element_type=jnp.float32, precision=PRECISE)

def solve_spd(matrix, target):
    factor = jnp.linalg.cholesky(matrix)
    halfway = lax.linalg.triangular_solve(factor, target, left_side=True, lower=True)
    return lax.linalg.triangular_solve(factor, halfway, left_side=True, lower=True, transpose_a=True)

def apply_stiffness(vector_in, tile_stiff, tile_nodes, node_shift):
    columns = vector_in.shape[1]
    ext_rows = NODES_DEV + 2 * HALO
    padded = jnp.concatenate([jnp.zeros((HALO, columns), jnp.float32), vector_in, jnp.zeros((HALO + 1, columns), jnp.float32)], axis=0)
    stiffness = tile_stiff.reshape(DEVICES, TILE_DEV, TILE, TILE)
    node_ids = tile_nodes.reshape(DEVICES, TILE_DEV, TILE)
    starts = (jnp.arange(DEVICES, dtype=jnp.int32) * NODES_DEV)[:, None, None]
    global_ids = jnp.where(node_ids == ext_rows, NODES + 2 * HALO, node_ids + starts).astype(jnp.int32)

    def one_part(summed, entries):
        blocks, node_index = entries
        gathered = padded[node_index]
        product = jnp.einsum('tij,tje->tie', blocks, gathered, precision=PRECISE)
        summed = summed.at[node_index.reshape(-1)].add(product.reshape(-1, columns))
        return (summed, None)
    summed, unused = lax.scan(one_part, jnp.zeros_like(padded), (stiffness, global_ids))
    return node_shift[:, None] * vector_in + summed[HALO:HALO + NODES]

def reference(right_side, tile_stiff, tile_nodes, node_shift, slot_nodes, slot_load, dipole_slot):
    solution = jnp.zeros_like(right_side)
    residual = right_side
    direction = right_side
    res_gram = inner_products(residual, residual)
    for iteration in range(ITERS):
        applied = apply_stiffness(direction, tile_stiff, tile_nodes, node_shift)
        alpha_mat = solve_spd(inner_products(direction, applied), res_gram)
        solution = solution + times_matrix(direction, alpha_mat)
        if iteration + 1 < ITERS:
            residual = residual - times_matrix(applied, alpha_mat)
            new_gram = inner_products(residual, residual)
            beta_mat = solve_spd(res_gram, new_gram)
            direction = residual + times_matrix(direction, beta_mat)
            res_gram = new_gram
    loads = slot_load.reshape(SUPPORT, DEVICES, SLOTS, 3)
    supports = slot_nodes.reshape(SUPPORT, DEVICES, SLOTS)

    def one_partition(number):
        local_rows = lax.dynamic_slice_in_dim(solution, number * NODES_DEV, NODES_DEV, 0)
        gathered = local_rows[supports[:, number]]
        return jnp.einsum('sqk,sqe->kqe', loads[:, number], gathered, precision=PRECISE)
    partials = lax.map(one_partition, jnp.arange(DEVICES, dtype=jnp.int32))
    owners = jnp.arange(DIPOLES, dtype=jnp.int32) // DIP_DEV
    sources = (dipole_slot // CAP).astype(jnp.int32)
    places = (owners * CAP + dipole_slot % CAP).astype(jnp.int32)
    picked = partials[sources, :, places, :]
    leadfield = jnp.transpose(picked, (1, 0, 2))
    return (solution, leadfield)
```

```python
import functools
import jax
import jax.numpy as jnp
from jax import lax
from jax.experimental import pallas as pl
from jax.experimental.pallas import tpu as pltpu
from jax.sharding import Mesh
from jax.sharding import PartitionSpec as P

F32 = jnp.float32
BF16 = jnp.bfloat16
AXES = ("row", "column", "depth", "core")
CHIPS = ("row", "column", "depth")
ITERS = 3
HALO = 128
REACH = 64
WIN = 256
STEP = WIN - REACH
SHIFT = 4.5
GUARD = 0.01
SPAN = 72
BATCH = 8
EDGE = 192


def dot(a, b, dims=((1,), (0,))):
    return lax.dot_general(a, b, (dims, ((), ())), preferred_element_type=F32)


def halves(x):
    high = x.astype(BF16)
    return high, (x - high.astype(F32)).astype(BF16)


def dot3(ah, al, bh, bl, dims=((1,), (0,))):
    return dot(ah, bh, dims) + (dot(ah, bl, dims) + dot(al, bh, dims))


def full_dot(a, b):
    return lax.dot_general(
        a, b, (((1,), (0,)), ((), ())), preferred_element_type=F32, precision=lax.Precision.HIGHEST
    )


def iota(shape, dim):
    return lax.broadcasted_iota(jnp.int32, shape, dim)


def in_vmem(count):
    return [pl.BlockSpec(memory_space=pltpu.VMEM)] * count


def assemble_kernel(group_ref, first_ref, stiff_ref, place_ref, offset_ref, diag_ref, out_ref, rows_ref):
    slots, _, tiles = stiff_ref.shape
    windows = out_ref.shape[0]
    eye = iota((WIN, WIN), 0) == iota((WIN, WIN), 1)

    def start(g, carry):
        out_ref[g] = jnp.where(eye, diag_ref[pl.ds(g, 1), :], 0.0)
        return carry

    lax.fori_loop(0, windows, start, 0)

    for i in range(slots):
        plane = stiff_ref[i]
        stacked = jnp.concatenate([plane] * (128 // slots), axis=0)
        rows_ref[pl.ds(i, tiles, stride=slots), :] = stacked.T

    lanes = BATCH * slots
    same = iota((lanes, lanes), 0) // slots == iota((lanes, lanes), 1) // slots
    row_in_window = iota((WIN, lanes), 0)
    row_in_span = iota((SPAN, lanes), 0)
    tile_of_lane = iota((SPAN, lanes), 1) // slots

    def batch(b, carry):
        base = pl.multiple_of(b * lanes, lanes)
        part = rows_ref[pl.ds(base, lanes), :]
        block = jnp.where(same, jnp.concatenate([part] * (lanes // 128), axis=1), 0.0)
        bh, bl = halves(block)
        place = place_ref[pl.ds(b, 1), :]
        hot = (row_in_window == place).astype(F32).astype(BF16)
        nt = ((1,), (1,))
        uh, ul = halves(dot(bh, hot, nt) + dot(bl, hot, nt))
        offset = offset_ref[pl.ds(b, 1), :]
        match = row_in_span == offset
        pick = jnp.concatenate(
            [(match & (tile_of_lane == t)).astype(F32).astype(BF16) for t in range(BATCH)], axis=0
        )
        full = dot(pick, uh) + dot(pick, ul)
        for t in range(BATCH):
            g = group_ref[b * BATCH + t]
            r = pl.multiple_of(first_ref[b * BATCH + t], 8)
            out_ref[g, pl.ds(r, SPAN), :] += full[t * SPAN : (t + 1) * SPAN]
        return carry

    lax.fori_loop(0, tiles // BATCH, batch, 0)


def assemble(tile_stiff, tile_nodes, node_shift):
    tiles, slots = tile_nodes.shape
    ext = node_shift.shape[0] + 2 * HALO
    windows = ext // STEP
    lowest = jnp.min(tile_nodes, axis=1)
    group = jnp.minimum(lowest // STEP, windows - 1)
    first = jnp.minimum((lowest - group * STEP) // 8 * 8, STEP - 8)
    place = jnp.where(tile_nodes == ext, -1, tile_nodes - group[:, None] * STEP)
    offset = jnp.where(tile_nodes == ext, -1, place - first[:, None])
    diag = jnp.pad(node_shift - SHIFT, (HALO, HALO)).reshape(windows, STEP)
    diag = jnp.pad(diag, ((0, 0), (0, WIN - STEP)))
    lanes = BATCH * slots
    smem = pl.BlockSpec(memory_space=pltpu.SMEM)
    return pl.pallas_call(
        assemble_kernel,
        out_shape=jax.ShapeDtypeStruct((windows, WIN, WIN), F32),
        in_specs=[smem, smem] + in_vmem(4),
        out_specs=pl.BlockSpec(memory_space=pltpu.VMEM),
        scratch_shapes=[pltpu.VMEM((tiles * slots, 128), F32)],
        name="assemble",
    )(
        group,
        first,
        jnp.transpose(tile_stiff, (1, 2, 0)),
        place.reshape(-1, lanes),
        offset.reshape(-1, lanes),
        diag,
    )


LOW = 2 * HALO


def powers_kernel(
    valid_ref, own_ref, left_ref, right_ref, band_ref, lband_ref, rband_ref,
    k1_ref, k2_ref, mom_ref,
    bh_ref, bl_ref, lh_ref, ll_ref, rh_ref, rl_ref,
    vh_ref, vl_ref, wh_ref, wl_ref, y_ref,
):
    own, cols = own_ref.shape
    windows = band_ref.shape[0]
    frame = vh_ref.shape[0]
    high = LOW + own

    def split_band(g, carry):
        bh_ref[g], bl_ref[g] = halves(band_ref[g])
        return carry

    lax.fori_loop(0, windows, split_band, 0)
    lh_ref[...], ll_ref[...] = halves(lband_ref[...])
    rh_ref[...], rl_ref[...] = halves(rband_ref[...])

    zero = jnp.zeros((LOW - EDGE, cols), BF16)
    tail = jnp.zeros((frame - high - EDGE, cols), BF16)
    for ref in (vh_ref, vl_ref):
        ref[: LOW - EDGE] = zero
        ref[high + EDGE :] = tail
    vh_ref[LOW - EDGE : LOW], vl_ref[LOW - EDGE : LOW] = halves(left_ref[...])
    vh_ref[high : high + EDGE], vl_ref[high : high + EDGE] = halves(right_ref[...])
    chunk = 256

    def split_own(i, carry):
        at = pl.multiple_of(i * chunk, chunk)
        h, l = halves(own_ref[pl.ds(at, chunk), :])
        vh_ref[pl.ds(LOW + at, chunk), :] = h
        vl_ref[pl.ds(LOW + at, chunk), :] = l
        return carry

    lax.fori_loop(0, own // chunk, split_own, 0)

    def apply(xh_ref, xl_ref):
        y_ref[...] = jnp.zeros_like(y_ref)

        def window(g, carry):
            at = pl.multiple_of(HALO + g * STEP, 64)
            xh = xh_ref[pl.ds(at, WIN), :]
            xl = xl_ref[pl.ds(at, WIN), :]
            y_ref[pl.ds(at, WIN), :] += dot3(bh_ref[g], bl_ref[g], xh, xl)
            return carry

        lax.fori_loop(0, windows, window, 0)

        def extra(h_ref, l_ref, lo, rows, out, at):
            y_ref[out : out + rows] += dot3(
                h_ref[lo : lo + rows], l_ref[lo : lo + rows],
                xh_ref[at : at + WIN], xl_ref[at : at + WIN],
            )

        extra(lh_ref, ll_ref, 0, 128, HALO, 0)
        extra(lh_ref, ll_ref, 128, 192, HALO + 64, HALO + 64)
        extra(rh_ref, rl_ref, 0, 256, own + HALO, own + HALO)
        extra(rh_ref, rl_ref, 256, 64, own + HALO + STEP, own + HALO + STEP)

    def keep(oh_ref, ol_ref):
        oh_ref[:HALO] = jnp.zeros((HALO, cols), BF16)
        ol_ref[:HALO] = jnp.zeros((HALO, cols), BF16)
        oh_ref[high + HALO :] = jnp.zeros((frame - high - HALO, cols), BF16)
        ol_ref[high + HALO :] = jnp.zeros((frame - high - HALO, cols), BF16)
        lower = jnp.where(valid_ref[0] > 0, y_ref[HALO:LOW], 0.0)
        upper = jnp.where(valid_ref[1] > 0, y_ref[high : high + HALO], 0.0)
        oh_ref[HALO:LOW], ol_ref[HALO:LOW] = halves(lower)
        oh_ref[high : high + HALO], ol_ref[high : high + HALO] = halves(upper)

        def split(i, carry):
            at = pl.multiple_of(LOW + i * chunk, chunk)
            h, l = halves(y_ref[pl.ds(at, chunk), :])
            oh_ref[pl.ds(at, chunk), :] = h
            ol_ref[pl.ds(at, chunk), :] = l
            return carry

        lax.fori_loop(0, own // chunk, split, 0)

    tn = ((0,), (0,))

    def square(n, xh_ref, xl_ref):
        xh = xh_ref[LOW:high]
        cross = dot(xh, xl_ref[LOW:high], tn)
        mom_ref[n] = dot(xh, xh, tn) + (cross + cross.T)

    def product(n, xh_ref, xl_ref, zh_ref, zl_ref):
        mom_ref[n] = dot3(xh_ref[LOW:high], xl_ref[LOW:high], zh_ref[LOW:high], zl_ref[LOW:high], tn)

    square(0, vh_ref, vl_ref)
    apply(vh_ref, vl_ref)
    k1_ref[...] = y_ref[LOW:high]
    keep(wh_ref, wl_ref)
    product(1, vh_ref, vl_ref, wh_ref, wl_ref)
    square(2, wh_ref, wl_ref)
    apply(wh_ref, wl_ref)
    k2_ref[...] = y_ref[LOW:high]
    keep(vh_ref, vl_ref)
    product(3, wh_ref, wl_ref, vh_ref, vl_ref)
    square(4, vh_ref, vl_ref)
    apply(vh_ref, vl_ref)
    keep(wh_ref, wl_ref)
    product(5, vh_ref, vl_ref, wh_ref, wl_ref)


def powers(vector, left, right, valid, bands):
    band, lband, rband = bands
    own, cols = vector.shape
    frame = own + 2 * LOW + 64
    full = jax.ShapeDtypeStruct((own, cols), F32)
    wide = pltpu.VMEM((frame, cols), BF16)
    edge = pltpu.VMEM(lband.shape, BF16)
    return pl.pallas_call(
        powers_kernel,
        out_shape=(full, full, jax.ShapeDtypeStruct((2 * ITERS, cols, cols), F32)),
        in_specs=[pl.BlockSpec(memory_space=pltpu.SMEM)] + in_vmem(6),
        out_specs=tuple(in_vmem(3)),
        scratch_shapes=[pltpu.VMEM(band.shape, BF16)] * 2 + [edge] * 4 + [wide] * 4
        + [pltpu.VMEM((frame, cols), F32)],
        name="powers",
    )(valid, vector, left, right, band, lband, rband)


def diagonals(matrix):
    size = matrix.shape[0]
    on = jnp.where(iota((size, size), 0) == iota((size, size), 1), matrix, 0.0)
    return jnp.sum(on, axis=0, keepdims=True), jnp.sum(on, axis=1, keepdims=True)


def inverse_spd(matrix):
    size = matrix.shape[0]
    unit = (iota((size, size), 0) == iota((size, size), 1)).astype(F32)
    along, down = diagonals(matrix)
    scale = lax.rsqrt(along) * lax.rsqrt(down)
    scaled = matrix * scale
    norm = jnp.max(jnp.sum(jnp.abs(scaled), axis=1, keepdims=True))
    factor = jnp.where(norm < 1.9, 1.0, 1.9 / norm)
    rest = unit - factor * scaled

    def going(state):
        k, worst, _, _ = state
        return (k < 40) & (worst > 3e-9)

    def step(state):
        k, _, total, power = state
        both = full_dot(jnp.concatenate([total, power], axis=0), power)
        total = total + both[:size]
        power = both[size:]
        return k + 1, jnp.max(jnp.abs(power)), total, power

    _, worst, total, _ = lax.while_loop(
        going, step, (0, jnp.max(jnp.abs(rest)), unit * factor, rest)
    )
    return total * scale, worst


def ratio(left, whole):
    return jnp.min(diagonals(left)[0] / diagonals(whole)[0])


def galerkin_kernel(mom_ref, out_ref, good_ref):
    m = [mom_ref[n] for n in range(2 * ITERS)]
    m = [0.5 * (x + x.T) for x in m]
    h = [m[n + 1] + SHIFT * m[n] for n in range(2 * ITERS - 1)]
    size = m[0].shape[0]

    def right_of(inverse, *targets):
        wide = full_dot(inverse, jnp.concatenate(targets, axis=1))
        return [wide[:, n * size : (n + 1) * size] for n in range(len(targets))]

    s0, w0 = inverse_spd(h[0])
    z01, z02, z0m = right_of(s0, h[1], h[2], m[0])
    lower = full_dot(
        jnp.concatenate([h[1], h[2]], axis=0), jnp.concatenate([z01, z02, z0m], axis=1)
    )
    first = h[2] - lower[:size, :size]
    cross = h[3] - lower[:size, size : 2 * size]
    m1 = m[1] - lower[:size, 2 * size :]
    last = h[4] - lower[size:, size : 2 * size]
    m2 = m[2] - lower[size:, 2 * size :]
    first = 0.5 * (first + first.T)
    s1, w1 = inverse_spd(first)
    z12, z1m = right_of(s1, cross, m1)
    lower = full_dot(cross.T, jnp.concatenate([z12, z1m], axis=1))
    rest = last - lower[:, :size]
    rest = 0.5 * (rest + rest.T)
    m2 = m2 - lower[:, size:]
    s2, w2 = inverse_spd(rest)
    y2 = full_dot(s2, m2)
    y1 = z1m - full_dot(z12, y2)
    y0 = z0m - full_dot(jnp.concatenate([z01, z02], axis=1), jnp.concatenate([y1, y2], axis=0))
    out_ref[:size] = y0
    out_ref[size : 2 * size] = y1
    out_ref[2 * size :] = y2
    share = jnp.minimum(ratio(first, h[2]), ratio(rest, h[4]))
    worst = jnp.maximum(w0, jnp.maximum(w1, w2))
    good_ref[0] = jnp.where((share > GUARD) & (worst < 1e-7), 1, 0)


def galerkin(moments):
    size = moments.shape[-1]
    return pl.pallas_call(
        galerkin_kernel,
        out_shape=(jax.ShapeDtypeStruct((ITERS * size, size), F32), jax.ShapeDtypeStruct((1,), jnp.int32)),
        in_specs=in_vmem(1),
        out_specs=(pl.BlockSpec(memory_space=pltpu.VMEM), pl.BlockSpec(memory_space=pltpu.SMEM)),
        name="galerkin",
    )(moments)


def solve_kernel(matrix_ref, target_ref, out_ref):
    matrix = matrix_ref[...]
    matrix = 0.5 * (matrix + matrix.T)
    inverse, _ = inverse_spd(matrix)
    guess = full_dot(inverse, target_ref[...])
    out_ref[...] = guess + full_dot(inverse, target_ref[...] - full_dot(matrix, guess))


def solve(matrix, target):
    return pl.pallas_call(
        solve_kernel,
        out_shape=jax.ShapeDtypeStruct(target.shape, F32),
        in_specs=in_vmem(2),
        out_specs=in_vmem(1)[0],
        name="solve",
    )(matrix, target)


def total_of(value):
    shape = value.shape
    lines = value.reshape(-1, 128)
    half = lines.shape[0] // 2
    core = lax.axis_index("core")
    chips = lax.axis_size(CHIPS)
    other = [(0, 1), (1, 0)]
    mine = lax.dynamic_slice_in_dim(lines, core * half, half, 0)
    theirs = lax.dynamic_slice_in_dim(lines, (1 - core) * half, half, 0)
    pair = (mine + lax.ppermute(theirs, "core", other)).reshape(chips, half // chips, 128)
    own = lax.all_to_all(pair, CHIPS, 0, 0, tiled=True).sum(axis=0)
    gathered = lax.all_to_all(jnp.broadcast_to(own[None], pair.shape), CHIPS, 0, 0, tiled=True)
    gathered = gathered.reshape(half, 128)
    partner = lax.ppermute(gathered, "core", other)
    low = jnp.where(core == 0, gathered, partner)
    high = jnp.where(core == 0, partner, gathered)
    return jnp.concatenate([low, high], axis=0).reshape(shape)


def both_ways(to_right, to_left):
    count = lax.axis_size(AXES)
    up = [(i, i + 1) for i in range(count - 1)]
    return lax.ppermute(to_right, AXES, up), lax.ppermute(to_left, AXES, [(b, a) for a, b in up])


def halo_of(vector):
    return both_ways(vector[-EDGE:], vector[:EDGE])


def combine_kernel(k0_ref, k1_ref, k2_ref, c_ref, out_ref):
    size = c_ref.shape[1]
    total = jnp.zeros(out_ref.shape, F32)
    for n, ref in enumerate((k0_ref, k1_ref, k2_ref)):
        ah, al = halves(ref[...])
        bh, bl = halves(c_ref[n * size : (n + 1) * size])
        total = total + dot3(ah, al, bh, bl)
    out_ref[...] = total


def combine(k0, k1, k2, coef):
    rows, cols = k0.shape
    block = pl.BlockSpec((512, cols), lambda i: (i, 0))
    return pl.pallas_call(
        combine_kernel,
        grid=(rows // 512,),
        out_shape=jax.ShapeDtypeStruct((rows, cols), F32),
        in_specs=[block] * 3 + [pl.BlockSpec(coef.shape, lambda i: (0, 0))],
        out_specs=block,
        name="combine",
    )(k0, k1, k2, coef)


def plain_cg(right_side, valid, bands):
    def image_of(vector):
        image, _, moments = powers(vector, *halo_of(vector), valid, bands)
        moments = total_of(moments)
        return image + SHIFT * vector, moments[1] + SHIFT * moments[0], moments[0]

    def times(a, b):
        return jnp.dot(a, b, preferred_element_type=F32, precision=lax.Precision.HIGHEST)

    def step(_, state):
        answer, residual, direction, gram = state
        applied, dir_gram, _ = image_of(direction)
        alpha = solve(dir_gram, gram)
        answer = answer + times(direction, alpha)
        residual = residual - times(applied, alpha)
        new_gram = image_of(residual)[2]
        beta = solve(gram, new_gram)
        return answer, residual, residual + times(direction, beta), new_gram

    gram = image_of(right_side)[2]
    state = (jnp.zeros_like(right_side), right_side, right_side, gram)
    return lax.fori_loop(0, ITERS, step, state)[0]


def loads_kernel(nodes_ref, load_ref, x_ref, out_ref, xh_ref, xl_ref):
    chunk = pl.program_id(0)
    support, slots = nodes_ref.shape[1:] if nodes_ref.ndim == 3 else (nodes_ref.shape[1], nodes_ref.shape[0])
    width = x_ref.shape[0]

    @pl.when(chunk == 0)
    def _():
        out_ref[...] = jnp.zeros_like(out_ref)

    column = iota((slots, width), 1) + chunk * width
    weights = [jnp.zeros((slots, width), F32) for _ in range(3)]
    for s in range(support):
        hit = nodes_ref[:, s : s + 1] == column
        for k in range(3):
            at = s * 3 + k
            weights[k] = weights[k] + jnp.where(hit, load_ref[:, at : at + 1], 0.0)
    xh, xl = halves(x_ref[...])
    for k in range(3):
        wh, wl = halves(weights[k])
        out_ref[k] += dot3(wh, wl, xh, xl)


def load_rows(x, slot_nodes, slot_load):
    rows, cols = x.shape
    support, slots = slot_nodes.shape
    width = 256
    loads = slot_load.reshape(support, slots, 3).transpose(1, 0, 2).reshape(slots, support * 3)
    whole = lambda shape: pl.BlockSpec(shape, lambda i: (0,) * len(shape))
    return pl.pallas_call(
        loads_kernel,
        grid=(rows // width,),
        out_shape=jax.ShapeDtypeStruct((3, slots, cols), F32),
        in_specs=[whole((slots, support)), whole((slots, support * 3)), pl.BlockSpec((width, cols), lambda i: (i, 0))],
        out_specs=whole((3, slots, cols)),
        scratch_shapes=[pltpu.VMEM((8, 128), BF16)] * 2,
        name="loads",
    )(slot_nodes.T, loads, x)


def per_device(right_side, tile_stiff, tile_nodes, node_shift, slot_nodes, slot_load, dipole_slot):
    count = lax.axis_size(AXES)
    index = lax.axis_index(AXES)
    valid = jnp.stack([index > 0, index < count - 1]).astype(jnp.int32)
    left, right = halo_of(right_side)
    band = assemble(tile_stiff, tile_nodes, node_shift)
    to_right = jnp.concatenate([band[-2, 128:], band[-1, :192]], axis=0)
    to_left = jnp.concatenate([band[0], band[1, :64]], axis=0)
    bands = (band, *both_ways(to_right, to_left))
    k1, k2, moments = powers(right_side, left, right, valid, bands)
    coef, good = galerkin(total_of(moments))
    answer = lax.cond(
        good[0] > 0,
        lambda: combine(right_side, k1, k2, coef),
        lambda: plain_cg(right_side, valid, bands),
    )
    slots = slot_nodes.shape[1]
    cols = right_side.shape[1]
    rows = load_rows(answer, slot_nodes, slot_load)
    received = lax.all_to_all(
        rows.reshape(3, count, slots // count, cols), AXES, split_axis=1, concat_axis=1, tiled=True
    )
    leadfield = received.reshape(3, slots, cols)[:, dipole_slot, :]
    return answer, leadfield


def solution(mesh):
    rows, depth = mesh.devices.shape
    outer = 4 if rows % 4 == 0 else 1
    flat = Mesh(mesh.devices.reshape(outer, rows // outer, depth // 2, 2), AXES)
    return jax.shard_map(
        per_device,
        mesh=flat,
        in_specs=(
            P(AXES, None),
            P(AXES, None, None),
            P(AXES, None),
            P(AXES),
            P(None, AXES),
            P(None, AXES),
            P(AXES),
        ),
        out_specs=(P(AXES, None), P(None, AXES, None)),
        check_vma=False,
    )
```

```python
import jax
import jax.numpy as jnp
from jax import lax
from jax.experimental import pallas as pl
from jax.experimental.pallas import tpu as pltpu
from jax.sharding import Mesh
from jax.sharding import PartitionSpec as P


F32 = jnp.float32
BF16 = jnp.bfloat16
AXES = ("row", "column", "depth", "core")
CHIPS = ("row", "column", "depth")
ITERS = 3
HALO = 128
REACH = 64
WIN = 256
STEP = WIN - REACH
SHIFT = 4.5
ROUNDS = 8
GUARD = 0.01
SMALL = 128
SPAN = 80
BATCH = 8
EDGE = 192


def dot(a, b, dims=((1,), (0,))):
    return lax.dot_general(a, b, (dims, ((), ())), preferred_element_type=F32)


def halves(x):
    high = x.astype(BF16)
    return high, (x - high.astype(F32)).astype(BF16)


def dot3(ah, al, bh, bl, dims=((1,), (0,))):
    return dot(ah, bh, dims) + (dot(ah, bl, dims) + dot(al, bh, dims))


def full_dot(a, b):
    return lax.dot_general(
        a, b, (((1,), (0,)), ((), ())), preferred_element_type=F32, precision=lax.Precision.HIGHEST
    )


def iota(shape, dim):
    return lax.broadcasted_iota(jnp.int32, shape, dim)


def in_vmem(count):
    return [pl.BlockSpec(memory_space=pltpu.VMEM)] * count


def assemble_kernel(
    group_ref, first_ref, stiff_ref, place_ref, offset_ref, diag_ref, out_ref,
    rows_ref, small_ref, block_ref, lane_ref,
):
    slots, _, tiles = stiff_ref.shape
    windows = out_ref.shape[0]
    lanes = BATCH * slots
    one = lambda mask: jnp.where(mask, 1.0, 0.0).astype(BF16)
    block_ref[...] = one(iota((lanes, lanes), 0) // slots == iota((lanes, lanes), 1) // slots)
    for t in range(BATCH):
        lane_ref[t * SPAN : (t + 1) * SPAN] = one(iota((SPAN, lanes), 1) // slots == t)

    def clear(g, carry):
        small_ref[g] = jnp.zeros((SMALL, SMALL), F32)
        return carry

    lax.fori_loop(0, small_ref.shape[0], clear, 0)
    for i in range(slots):
        plane = stiff_ref[i]
        stacked = jnp.concatenate([plane] * (128 // slots), axis=0)
        rows_ref[pl.ds(i, tiles, stride=slots), :] = stacked.T

    row_in_window = iota((SMALL, lanes), 0)
    row_in_span = iota((SPAN, lanes), 0)

    def batch(b, carry):
        base = pl.multiple_of(b * lanes, lanes)
        parts = halves(rows_ref[pl.ds(base, lanes), :])
        block = block_ref[...]
        wide = [jnp.concatenate([part] * (lanes // 128), axis=1) * block for part in parts]
        hot = one(row_in_window == place_ref[pl.ds(b, 1), :])
        both = dot(jnp.concatenate(wide, axis=0), hot, ((1,), (1,)))
        uh, ul = halves(both[:lanes] + both[lanes:])
        match = one(row_in_span == offset_ref[pl.ds(b, 1), :])
        pick = jnp.concatenate([match] * BATCH, axis=0) * lane_ref[...]
        full = dot(pick, jnp.concatenate([uh, ul], axis=1))
        full = full[:, :SMALL] + full[:, SMALL:]
        for t in range(BATCH):
            g = group_ref[b * BATCH + t]
            r = pl.multiple_of(first_ref[b * BATCH + t], 16)
            small_ref[g, pl.ds(r, SPAN), :] += full[t * SPAN : (t + 1) * SPAN]
        return carry

    lax.fori_loop(0, tiles // BATCH, batch, 0)

    eye = iota((WIN, WIN), 0) == iota((WIN, WIN), 1)
    gap = jnp.zeros((SMALL, REACH), F32)

    def gather(g, carry):
        out_ref[g] = jnp.where(eye, diag_ref[pl.ds(g, 1), :], 0.0)
        out_ref[g, :SMALL, :SMALL] += small_ref[3 * g]
        middle = jnp.concatenate([gap, small_ref[3 * g + 1], gap], axis=1)
        out_ref[g, REACH : REACH + SMALL, :] += middle
        out_ref[g, SMALL:, SMALL:] += small_ref[3 * g + 2]
        return carry

    lax.fori_loop(0, windows, gather, 0)


def assemble(tile_stiff, tile_nodes, node_shift):
    tiles, slots = tile_nodes.shape
    ext = node_shift.shape[0] + 2 * HALO
    windows = ext // STEP
    smalls = ext // REACH
    lowest = jnp.min(tile_nodes, axis=1)
    group = jnp.minimum(lowest // REACH, smalls - 1)
    first = jnp.minimum((lowest - group * REACH) // 16 * 16, REACH - 16)
    place = jnp.where(tile_nodes == ext, -1, tile_nodes - group[:, None] * REACH)
    offset = jnp.where(tile_nodes == ext, -1, place - first[:, None])
    diag = jnp.pad(node_shift - SHIFT, (HALO, HALO)).reshape(windows, STEP)
    diag = jnp.pad(diag, ((0, 0), (0, WIN - STEP)))
    lanes = BATCH * slots
    smem = pl.BlockSpec(memory_space=pltpu.SMEM)
    return pl.pallas_call(
        assemble_kernel,
        out_shape=jax.ShapeDtypeStruct((windows, WIN, WIN), F32),
        in_specs=[smem, smem] + in_vmem(4),
        out_specs=pl.BlockSpec(memory_space=pltpu.VMEM),
        scratch_shapes=[
            pltpu.VMEM((tiles * slots, 128), F32),
            pltpu.VMEM((smalls, SMALL, SMALL), F32),
            pltpu.VMEM((lanes, lanes), BF16),
            pltpu.VMEM((BATCH * SPAN, lanes), BF16),
        ],
        compiler_params=pltpu.CompilerParams(vmem_limit_bytes=28 << 20),
        name="assemble",
    )(
        group,
        first,
        jnp.transpose(tile_stiff, (1, 2, 0)),
        place.reshape(-1, lanes),
        offset.reshape(-1, lanes),
        diag,
    )


LOW = 2 * HALO


def powers_kernel(
    valid_ref, own_ref, left_ref, right_ref, band_ref, lband_ref, rband_ref,
    k1_ref, k2_ref, mine_ref, theirs_ref,
    bh_ref, bl_ref, lh_ref, ll_ref, rh_ref, rl_ref,
    vh_ref, vl_ref, wh_ref, wl_ref, y_ref,
):
    own, cols = own_ref.shape
    windows = band_ref.shape[0]
    frame = vh_ref.shape[0]
    high = LOW + own

    def split_band(g, carry):
        bh_ref[g], bl_ref[g] = halves(band_ref[g])
        return carry

    lax.fori_loop(0, windows, split_band, 0)
    lh_ref[...], ll_ref[...] = halves(lband_ref[...])
    rh_ref[...], rl_ref[...] = halves(rband_ref[...])

    zero = jnp.zeros((LOW - EDGE, cols), BF16)
    tail = jnp.zeros((frame - high - EDGE, cols), BF16)
    for ref in (vh_ref, vl_ref):
        ref[: LOW - EDGE] = zero
        ref[high + EDGE :] = tail
    vh_ref[LOW - EDGE : LOW], vl_ref[LOW - EDGE : LOW] = halves(left_ref[...])
    vh_ref[high : high + EDGE], vl_ref[high : high + EDGE] = halves(right_ref[...])
    chunk = 256

    def split_own(i, carry):
        at = pl.multiple_of(i * chunk, chunk)
        h, l = halves(own_ref[pl.ds(at, chunk), :])
        vh_ref[pl.ds(LOW + at, chunk), :] = h
        vl_ref[pl.ds(LOW + at, chunk), :] = l
        return carry

    lax.fori_loop(0, own // chunk, split_own, 0)

    def apply(xh_ref, xl_ref):
        y_ref[...] = jnp.zeros_like(y_ref)

        def window(g, carry):
            at = pl.multiple_of(HALO + g * STEP, 64)
            xh = xh_ref[pl.ds(at, WIN), :]
            xl = xl_ref[pl.ds(at, WIN), :]
            y_ref[pl.ds(at, WIN), :] += dot3(bh_ref[g], bl_ref[g], xh, xl)
            return carry

        lax.fori_loop(0, windows, window, 0)

        def extra(h_ref, l_ref, lo, rows, out, at):
            y_ref[out : out + rows] += dot3(
                h_ref[lo : lo + rows], l_ref[lo : lo + rows],
                xh_ref[at : at + WIN], xl_ref[at : at + WIN],
            )

        extra(lh_ref, ll_ref, 0, 128, HALO, 0)
        extra(lh_ref, ll_ref, 128, 192, HALO + 64, HALO + 64)
        extra(rh_ref, rl_ref, 0, 256, own + HALO, own + HALO)
        extra(rh_ref, rl_ref, 256, 64, own + HALO + STEP, own + HALO + STEP)

    def keep(oh_ref, ol_ref):
        oh_ref[:HALO] = jnp.zeros((HALO, cols), BF16)
        ol_ref[:HALO] = jnp.zeros((HALO, cols), BF16)
        oh_ref[high + HALO :] = jnp.zeros((frame - high - HALO, cols), BF16)
        ol_ref[high + HALO :] = jnp.zeros((frame - high - HALO, cols), BF16)
        lower = jnp.where(valid_ref[0] > 0, y_ref[HALO:LOW], 0.0)
        upper = jnp.where(valid_ref[1] > 0, y_ref[high : high + HALO], 0.0)
        oh_ref[HALO:LOW], ol_ref[HALO:LOW] = halves(lower)
        oh_ref[high : high + HALO], ol_ref[high : high + HALO] = halves(upper)

        def split(i, carry):
            at = pl.multiple_of(LOW + i * chunk, chunk)
            h, l = halves(y_ref[pl.ds(at, chunk), :])
            oh_ref[pl.ds(at, chunk), :] = h
            ol_ref[pl.ds(at, chunk), :] = l
            return carry

        lax.fori_loop(0, own // chunk, split, 0)

    tn = ((0,), (0,))

    def put(n, value):
        here = valid_ref[2] == n // ITERS

        @pl.when(here)
        def _():
            for c in range(cols // 128):
                mine_ref[n % ITERS, c] = value[:, c * 128 : (c + 1) * 128]

        @pl.when(jnp.logical_not(here))
        def _():
            for c in range(cols // 128):
                theirs_ref[n % ITERS, c] = value[:, c * 128 : (c + 1) * 128]

    def square(n, xh_ref, xl_ref):
        xh = xh_ref[LOW:high]
        cross = dot(xh, xl_ref[LOW:high], tn)
        put(n, dot(xh, xh, tn) + (cross + cross.T))

    def product(n, xh_ref, xl_ref, zh_ref, zl_ref):
        put(n, dot3(xh_ref[LOW:high], xl_ref[LOW:high], zh_ref[LOW:high], zl_ref[LOW:high], tn))

    square(0, vh_ref, vl_ref)
    apply(vh_ref, vl_ref)
    k1_ref[...] = y_ref[LOW:high]
    keep(wh_ref, wl_ref)
    product(1, vh_ref, vl_ref, wh_ref, wl_ref)
    square(2, wh_ref, wl_ref)
    apply(wh_ref, wl_ref)
    k2_ref[...] = y_ref[LOW:high]
    keep(vh_ref, vl_ref)
    product(3, wh_ref, wl_ref, vh_ref, vl_ref)
    square(4, vh_ref, vl_ref)
    apply(vh_ref, vl_ref)
    keep(wh_ref, wl_ref)
    product(5, vh_ref, vl_ref, wh_ref, wl_ref)


def powers(vector, left, right, valid, bands):
    band, lband, rband = bands
    own, cols = vector.shape
    frame = own + 2 * LOW + 64
    full = jax.ShapeDtypeStruct((own, cols), F32)
    half = jax.ShapeDtypeStruct((ITERS, cols // 128, cols, 128), F32)
    wide = pltpu.VMEM((frame, cols), BF16)
    edge = pltpu.VMEM(lband.shape, BF16)
    return pl.pallas_call(
        powers_kernel,
        out_shape=(full, full, half, half),
        in_specs=[pl.BlockSpec(memory_space=pltpu.SMEM)] + in_vmem(6),
        out_specs=tuple(in_vmem(4)),
        compiler_params=pltpu.CompilerParams(vmem_limit_bytes=44 << 20),
        scratch_shapes=[pltpu.VMEM(band.shape, BF16)] * 2 + [edge] * 4 + [wide] * 4
        + [pltpu.VMEM((frame, cols), F32)],
        name="powers",
    )(valid, vector, left, right, band, lband, rband)


def diagonals(matrix):
    size = matrix.shape[0]
    on = jnp.where(iota((size, size), 0) == iota((size, size), 1), matrix, 0.0)
    return jnp.sum(on, axis=0, keepdims=True), jnp.sum(on, axis=1, keepdims=True)


def split_dot(a, b):
    return dot3(*halves(a), *halves(b))


def inverse_spd(matrix, mul):
    size = matrix.shape[0]
    unit = (iota((size, size), 0) == iota((size, size), 1)).astype(F32)
    along, down = diagonals(matrix)
    scale = lax.rsqrt(along) * lax.rsqrt(down)
    scaled = matrix * scale
    norm = jnp.max(jnp.sum(jnp.abs(scaled), axis=1, keepdims=True))
    factor = jnp.where(norm < 1.9, 1.0, 1.9 / norm)
    rest = unit - factor * scaled

    def going(state):
        k, worst, _, _ = state
        return (k < 40) & (worst > 1e-8)

    def step(state):
        k, _, total, power = state
        both = mul(jnp.concatenate([total, power], axis=0), power)
        total = total + both[:size]
        power = both[size:]
        return k + 1, jnp.max(jnp.abs(power)), total, power

    rounds, worst, total, _ = lax.while_loop(
        going, step, (0, jnp.max(jnp.abs(rest)), unit * factor, rest)
    )
    return total * scale, worst, rounds


def ratio(left, whole):
    return jnp.min(diagonals(left)[0] / diagonals(whole)[0])


def galerkin_kernel(core_ref, mine_ref, theirs_ref, out_ref, good_ref, mom_ref):
    parts = mine_ref.shape[1]

    def unpack(source_ref, start):
        for n in range(ITERS):
            mom_ref[start + n] = jnp.concatenate([source_ref[n, c] for c in range(parts)], axis=1)

    @pl.when(core_ref[0] == 0)
    def _():
        unpack(mine_ref, 0)
        unpack(theirs_ref, ITERS)

    @pl.when(core_ref[0] != 0)
    def _():
        unpack(theirs_ref, 0)
        unpack(mine_ref, ITERS)

    m = [mom_ref[n] for n in range(2 * ITERS)]
    m = [0.5 * (x + x.T) for x in m]
    h = [m[n + 1] + SHIFT * m[n] for n in range(2 * ITERS - 1)]
    size = m[0].shape[0]

    def right_of(inverse, *targets):
        wide = split_dot(inverse, jnp.concatenate(targets, axis=1))
        return [wide[:, n * size : (n + 1) * size] for n in range(len(targets))]

    s0, w0, k0 = inverse_spd(h[0], split_dot)
    z01, z02, z0m = right_of(s0, h[1], h[2], m[0])
    lower = split_dot(
        jnp.concatenate([h[1], h[2]], axis=0), jnp.concatenate([z01, z02, z0m], axis=1)
    )
    first = h[2] - lower[:size, :size]
    cross = h[3] - lower[:size, size : 2 * size]
    m1 = m[1] - lower[:size, 2 * size :]
    last = h[4] - lower[size:, size : 2 * size]
    m2 = m[2] - lower[size:, 2 * size :]
    first = 0.5 * (first + first.T)
    s1, w1, k1 = inverse_spd(first, split_dot)
    z12, z1m = right_of(s1, cross, m1)
    lower = split_dot(cross.T, jnp.concatenate([z12, z1m], axis=1))
    rest = last - lower[:, :size]
    rest = 0.5 * (rest + rest.T)
    m2 = m2 - lower[:, size:]
    s2, w2, k2 = inverse_spd(rest, split_dot)
    y2 = split_dot(s2, m2)
    y1 = z1m - split_dot(z12, y2)
    y0 = z0m - split_dot(jnp.concatenate([z01, z02], axis=1), jnp.concatenate([y1, y2], axis=0))
    out_ref[:size] = y0
    out_ref[size : 2 * size] = y1
    out_ref[2 * size :] = y2
    share = jnp.minimum(ratio(first, h[2]), ratio(rest, h[4]))
    rounds = jnp.maximum(k0, jnp.maximum(k1, k2))
    worst = jnp.maximum(w0, jnp.maximum(w1, w2))
    good_ref[0] = jnp.where((share > GUARD) & (worst <= 1e-8) & (rounds <= ROUNDS), 1, 0)


def galerkin(core, mine, theirs):
    size = mine.shape[2]
    smem = pl.BlockSpec(memory_space=pltpu.SMEM)
    return pl.pallas_call(
        galerkin_kernel,
        out_shape=(jax.ShapeDtypeStruct((ITERS * size, size), F32), jax.ShapeDtypeStruct((1,), jnp.int32)),
        in_specs=[smem] + in_vmem(2),
        out_specs=(pl.BlockSpec(memory_space=pltpu.VMEM), smem),
        scratch_shapes=[pltpu.VMEM((2 * ITERS, size, size), F32)],
        compiler_params=pltpu.CompilerParams(vmem_limit_bytes=32 << 20),
        name="galerkin",
    )(core, mine, theirs)


def solve_kernel(matrix_ref, target_ref, out_ref):
    matrix = matrix_ref[...]
    matrix = 0.5 * (matrix + matrix.T)
    inverse, _, _ = inverse_spd(matrix, full_dot)
    guess = full_dot(inverse, target_ref[...])
    out_ref[...] = guess + full_dot(inverse, target_ref[...] - full_dot(matrix, guess))


def solve(matrix, target):
    return pl.pallas_call(
        solve_kernel,
        out_shape=jax.ShapeDtypeStruct(target.shape, F32),
        in_specs=in_vmem(2),
        out_specs=in_vmem(1)[0],
        name="solve",
    )(matrix, target)


def total_of(mine, theirs):
    shape = mine.shape
    chips = lax.axis_size(CHIPS)
    other = [(0, 1), (1, 0)]
    pair = mine + lax.ppermute(theirs, "core", other)
    pair = pair.reshape(chips, -1, 128)
    own = lax.all_to_all(pair, CHIPS, 0, 0, tiled=True).sum(axis=0)
    gathered = lax.all_to_all(jnp.broadcast_to(own[None], pair.shape), CHIPS, 0, 0, tiled=True)
    gathered = gathered.reshape(shape)
    return gathered, lax.ppermute(gathered, "core", other)


def both_ways(to_right, to_left):
    count = lax.axis_size(AXES)
    up = [(i, i + 1) for i in range(count - 1)]
    return lax.ppermute(to_right, AXES, up), lax.ppermute(to_left, AXES, [(b, a) for a, b in up])


def halo_of(vector):
    return both_ways(vector[-EDGE:], vector[:EDGE])


def plain_cg(right_side, valid, bands):
    def times(a, b):
        return jnp.dot(a, b, preferred_element_type=F32, precision=lax.Precision.HIGHEST)

    def gram_of(parts):
        return jnp.concatenate([parts[0], parts[1]], axis=1)

    def step(k, state):
        answer, residual, direction, gram = state
        on_direction = k % 2 == 0
        vector = jnp.where(on_direction, direction, residual)
        image, _, mine, theirs = powers(vector, *halo_of(vector), valid, bands)
        low, high = total_of(mine, theirs)
        low = jnp.where(valid[2] == 0, low, high)
        square = gram_of(low[0])
        gram = jnp.where(k == 0, square, gram)
        dir_gram = gram_of(low[1]) + SHIFT * square
        factor = solve(
            jnp.where(on_direction, dir_gram, gram), jnp.where(on_direction, gram, square)
        )
        along = times(direction, factor)
        applied = times(image + SHIFT * vector, factor)
        answer = jnp.where(on_direction, answer + along, answer)
        direction = jnp.where(on_direction, direction, residual + along)
        residual = jnp.where(on_direction, residual - applied, residual)
        return answer, residual, direction, jnp.where(on_direction, gram, square)

    state = (jnp.zeros_like(right_side), right_side, right_side, jnp.zeros((right_side.shape[1],) * 2, F32))
    return lax.fori_loop(0, 2 * ITERS - 1, step, state)[0]


def loads_kernel(nodes_ref, load_ref, high_ref, low_ref):
    groups, pairs = nodes_ref.shape
    slots = 8
    support = pairs // slots
    blocks = high_ref.shape[1] // 128
    own_lane = iota((slots, pairs), 1) // support == iota((slots, pairs), 0)
    row = iota((128, pairs), 0)

    def half_group(g):
        nodes = nodes_ref[pl.ds(g, 1), :]
        hot = jnp.where(row == nodes % 128, 1.0, 0.0).astype(BF16)
        block = jnp.broadcast_to(nodes // 128, (slots, pairs))
        terms = []
        for k in range(3):
            spread = jnp.where(own_lane, load_ref[k, pl.ds(g, 1), :], 0.0)
            high = spread.astype(BF16).astype(F32)
            terms.append((high, spread - high))
        rows = []
        for c in range(blocks):
            hit = block == c
            for high, low in terms:
                rows.append(
                    jnp.concatenate([jnp.where(hit, high, 0.0), jnp.where(hit, low, 0.0)], axis=1)
                )
        left = jnp.concatenate(rows, axis=0).astype(BF16)
        return dot(left, jnp.concatenate([hot, hot], axis=1), ((1,), (1,)))

    def group(g, carry):
        first = half_group(2 * g)
        second = half_group(2 * g + 1)
        total = groups * slots
        for c in range(blocks):
            for k in range(3):
                at = (c * 3 + k) * slots
                value = jnp.concatenate([first[at : at + slots], second[at : at + slots]], axis=0)
                high, low = halves(value)
                to = pl.multiple_of(k * total + g * 2 * slots, 16)
                high_ref[pl.ds(to, 2 * slots), c * 128 : (c + 1) * 128] = high
                low_ref[pl.ds(to, 2 * slots), c * 128 : (c + 1) * 128] = low
        return carry

    lax.fori_loop(0, groups // 2, group, 0)


def load_matrix(slot_nodes, slot_load, rows):
    support, slots = slot_nodes.shape
    groups = slots * support // 128
    nodes = slot_nodes.T.reshape(groups, 128)
    loads = slot_load.reshape(support, slots, 3).transpose(2, 1, 0).reshape(3, groups, 128)
    out = jax.ShapeDtypeStruct((3 * slots, rows), BF16)
    return pl.pallas_call(
        loads_kernel,
        out_shape=(out, out),
        in_specs=in_vmem(2),
        out_specs=tuple(in_vmem(2)),
        compiler_params=pltpu.CompilerParams(vmem_limit_bytes=20 << 20),
        name="loads",
    )(nodes, loads)


def rows_of(wh, wl, xh, xl, out_ref):
    full = dot3(wh, wl, xh, xl)
    cols = full.shape[1]
    slots = full.shape[0] // 3
    for k in range(3):
        out_ref[:, k * cols : (k + 1) * cols] += full[k * slots : (k + 1) * slots]


def combine_kernel(k0_ref, k1_ref, k2_ref, c_ref, wh_ref, wl_ref, x_ref, out_ref, ch_ref, cl_ref):
    size = c_ref.shape[1]

    @pl.when(pl.program_id(0) == 0)
    def _():
        ch_ref[...], cl_ref[...] = halves(c_ref[...])
        out_ref[...] = jnp.zeros_like(out_ref)

    total = jnp.zeros(x_ref.shape, F32)
    for n, ref in enumerate((k0_ref, k1_ref, k2_ref)):
        ah, al = halves(ref[...])
        at = n * size
        total = total + dot3(ah, al, ch_ref[at : at + size], cl_ref[at : at + size])
    x_ref[...] = total
    rows_of(wh_ref[...], wl_ref[...], *halves(total), out_ref)


def leading_kernel(x_ref, wh_ref, wl_ref, out_ref):
    @pl.when(pl.program_id(0) == 0)
    def _():
        out_ref[...] = jnp.zeros_like(out_ref)

    rows_of(wh_ref[...], wl_ref[...], *halves(x_ref[...]), out_ref)


CHUNK = 512


def combine(k0, k1, k2, coef, weights):
    rows, cols = k0.shape
    loads = weights[0].shape[0]
    block = pl.BlockSpec((CHUNK, cols), lambda i: (i, 0))
    weight = pl.BlockSpec((loads, CHUNK), lambda i: (0, i))
    out = (loads // 3, 3 * cols)
    return pl.pallas_call(
        combine_kernel,
        grid=(rows // CHUNK,),
        out_shape=(jax.ShapeDtypeStruct((rows, cols), F32), jax.ShapeDtypeStruct(out, F32)),
        in_specs=[block] * 3 + [pl.BlockSpec(coef.shape, lambda i: (0, 0)), weight, weight],
        out_specs=(block, pl.BlockSpec(out, lambda i: (0, 0))),
        scratch_shapes=[pltpu.VMEM(coef.shape, BF16)] * 2,
        compiler_params=pltpu.CompilerParams(vmem_limit_bytes=32 << 20),
        name="combine",
    )(k0, k1, k2, coef, *weights)


def leading(x, weights):
    rows, cols = x.shape
    loads = weights[0].shape[0]
    weight = pl.BlockSpec((loads, CHUNK), lambda i: (0, i))
    out = (loads // 3, 3 * cols)
    return pl.pallas_call(
        leading_kernel,
        grid=(rows // CHUNK,),
        out_shape=jax.ShapeDtypeStruct(out, F32),
        in_specs=[pl.BlockSpec((CHUNK, cols), lambda i: (i, 0)), weight, weight],
        out_specs=pl.BlockSpec(out, lambda i: (0, 0)),
        name="leading",
    )(x, *weights)


def exact_path(right_side, valid, bands, weights):
    answer = plain_cg(right_side, valid, bands)
    return answer, leading(answer, weights)


def one_device(right_side, tile_stiff, tile_nodes, node_shift, slot_nodes, slot_load, dipole_slot):
    count = lax.axis_size(AXES)
    index = lax.axis_index(AXES)
    core = lax.axis_index("core")
    valid = jnp.stack([index > 0, index < count - 1, core]).astype(jnp.int32)
    left, right = halo_of(right_side)
    band = assemble(tile_stiff, tile_nodes, node_shift)
    to_right = jnp.concatenate([band[-2, 128:], band[-1, :192]], axis=0)
    to_left = jnp.concatenate([band[0], band[1, :64]], axis=0)
    bands = (band, *both_ways(to_right, to_left))
    weights = load_matrix(slot_nodes, slot_load, right_side.shape[0])
    k1, k2, mine, theirs = powers(right_side, left, right, valid, bands)
    coef, good = galerkin(core[None], *total_of(mine, theirs))
    answer, rows = lax.cond(
        good[0] > 0,
        lambda: combine(right_side, k1, k2, coef, weights),
        lambda: exact_path(right_side, valid, bands, weights),
    )
    slots, wide = rows.shape
    received = lax.all_to_all(rows.reshape(count, slots // count, wide), AXES, 0, 0, tiled=True)
    picked = received.reshape(slots, wide)[dipole_slot]
    leadfield = picked.reshape(-1, 3, wide // 3).transpose(1, 0, 2)
    return answer, leadfield


def solution(mesh):
    rows, depth = mesh.devices.shape
    outer = 4 if rows % 4 == 0 else 1
    flat = Mesh(mesh.devices.reshape(outer, rows // outer, depth // 2, 2), AXES)
    return jax.shard_map(
        one_device,
        mesh=flat,
        in_specs=(
            P(AXES, None),
            P(AXES, None, None),
            P(AXES, None),
            P(AXES),
            P(None, AXES),
            P(None, AXES),
            P(AXES),
        ),
        out_specs=(P(AXES, None), P(None, AXES, None)),
        check_vma=False,
    )
```

```python
import jax
import jax.numpy as jnp
from jax import lax
from jax.experimental import pallas as pl
from jax.experimental.pallas import tpu as pltpu
from jax.sharding import Mesh
from jax.sharding import PartitionSpec as P


F32 = jnp.float32
BF16 = jnp.bfloat16
AXES = ("row", "column", "depth", "core")
CHIPS = ("row", "column", "depth")
ITERS = 3
HALO = 128
REACH = 64
WIN = 256
STEP = WIN - REACH
SHIFT = 4.5
ROUNDS = 8
CLOSE = 1e-7
GUARD = 0.01
SMALL = 128
SPAN = 80
BATCH = 8
TOGETHER = 2
EDGE = 192


def dot(a, b, dims=((1,), (0,))):
    return lax.dot_general(a, b, (dims, ((), ())), preferred_element_type=F32)


def halves(x):
    high = x.astype(BF16)
    return high, (x - high.astype(F32)).astype(BF16)


def dot3(ah, al, bh, bl, dims=((1,), (0,))):
    return dot(ah, bh, dims) + (dot(ah, bl, dims) + dot(al, bh, dims))


def full_dot(a, b):
    return lax.dot_general(
        a, b, (((1,), (0,)), ((), ())), preferred_element_type=F32, precision=lax.Precision.HIGHEST
    )


def iota(shape, dim):
    return lax.broadcasted_iota(jnp.int32, shape, dim)


def in_vmem(count):
    return [pl.BlockSpec(memory_space=pltpu.VMEM)] * count


def assemble_kernel(
    group_ref, first_ref, stiff_ref, place_ref, offset_ref, diag_ref, out_ref,
    rows_ref, small_ref, block_ref, lane_ref,
):
    slots, _, tiles = stiff_ref.shape
    windows = out_ref.shape[0]
    lanes = BATCH * slots
    one = lambda mask: jnp.where(mask, 1.0, 0.0).astype(BF16)
    block_ref[...] = one(iota((lanes, lanes), 0) // slots == iota((lanes, lanes), 1) // slots)
    for t in range(BATCH):
        lane_ref[t * SPAN : (t + 1) * SPAN] = one(iota((SPAN, lanes), 1) // slots == t)

    def clear(g, carry):
        small_ref[g] = jnp.zeros((SMALL, SMALL), F32)
        return carry

    lax.fori_loop(0, small_ref.shape[0], clear, 0)
    for i in range(slots):
        plane = stiff_ref[i]
        stacked = jnp.concatenate([plane] * (128 // slots), axis=0)
        rows_ref[pl.ds(i, tiles, stride=slots), :] = stacked.T

    row_in_window = iota((SMALL, lanes), 0)
    row_in_span = iota((SPAN, lanes), 0)

    def product_of(b):
        base = pl.multiple_of(b * lanes, lanes)
        parts = halves(rows_ref[pl.ds(base, lanes), :])
        block = block_ref[...]
        wide = [jnp.concatenate([part] * (lanes // 128), axis=1) * block for part in parts]
        hot = one(row_in_window == place_ref[pl.ds(b, 1), :])
        both = dot(jnp.concatenate(wide, axis=0), hot, ((1,), (1,)))
        uh, ul = halves(both[:lanes] + both[lanes:])
        match = one(row_in_span == offset_ref[pl.ds(b, 1), :])
        pick = jnp.concatenate([match] * BATCH, axis=0) * lane_ref[...]
        full = dot(pick, jnp.concatenate([uh, ul], axis=1))
        return full[:, :SMALL] + full[:, SMALL:]

    def batch(i, carry):
        full = [product_of(TOGETHER * i + n) for n in range(TOGETHER)]
        for n in range(TOGETHER):
            for t in range(BATCH):
                tile = (TOGETHER * i + n) * BATCH + t
                r = pl.multiple_of(first_ref[tile], 16)
                small_ref[group_ref[tile], pl.ds(r, SPAN), :] += full[n][t * SPAN : (t + 1) * SPAN]
        return carry

    lax.fori_loop(0, tiles // (BATCH * TOGETHER), batch, 0)

    eye = iota((WIN, WIN), 0) == iota((WIN, WIN), 1)
    gap = jnp.zeros((SMALL, REACH), F32)

    def gather(g, carry):
        out_ref[g] = jnp.where(eye, diag_ref[pl.ds(g, 1), :], 0.0)
        out_ref[g, :SMALL, :SMALL] += small_ref[3 * g]
        middle = jnp.concatenate([gap, small_ref[3 * g + 1], gap], axis=1)
        out_ref[g, REACH : REACH + SMALL, :] += middle
        out_ref[g, SMALL:, SMALL:] += small_ref[3 * g + 2]
        return carry

    lax.fori_loop(0, windows, gather, 0)


def assemble(tile_stiff, tile_nodes, node_shift):
    tiles, slots = tile_nodes.shape
    ext = node_shift.shape[0] + 2 * HALO
    windows = ext // STEP
    smalls = ext // REACH
    lowest = jnp.min(tile_nodes, axis=1)
    group = jnp.minimum(lowest // REACH, smalls - 1)
    first = jnp.minimum((lowest - group * REACH) // 16 * 16, REACH - 16)
    place = jnp.where(tile_nodes == ext, -1, tile_nodes - group[:, None] * REACH)
    offset = jnp.where(tile_nodes == ext, -1, place - first[:, None])
    diag = jnp.pad(node_shift - SHIFT, (HALO, HALO)).reshape(windows, STEP)
    diag = jnp.pad(diag, ((0, 0), (0, WIN - STEP)))
    lanes = BATCH * slots
    smem = pl.BlockSpec(memory_space=pltpu.SMEM)
    return pl.pallas_call(
        assemble_kernel,
        out_shape=jax.ShapeDtypeStruct((windows, WIN, WIN), F32),
        in_specs=[smem, smem] + in_vmem(4),
        out_specs=pl.BlockSpec(memory_space=pltpu.VMEM),
        scratch_shapes=[
            pltpu.VMEM((tiles * slots, 128), F32),
            pltpu.VMEM((smalls, SMALL, SMALL), F32),
            pltpu.VMEM((lanes, lanes), BF16),
            pltpu.VMEM((BATCH * SPAN, lanes), BF16),
        ],
        compiler_params=pltpu.CompilerParams(vmem_limit_bytes=28 << 20),
        name="assemble",
    )(
        group,
        first,
        jnp.transpose(tile_stiff, (1, 2, 0)),
        place.reshape(-1, lanes),
        offset.reshape(-1, lanes),
        diag,
    )


LOW = 2 * HALO


def powers_kernel(
    valid_ref, own_ref, left_ref, right_ref, band_ref, lband_ref, rband_ref,
    k1_ref, k2_ref, mine_ref, theirs_ref,
    bh_ref, bl_ref, lh_ref, ll_ref, rh_ref, rl_ref,
    vh_ref, vl_ref, wh_ref, wl_ref, y_ref,
):
    own, cols = own_ref.shape
    windows = band_ref.shape[0]
    frame = vh_ref.shape[0]
    high = LOW + own

    def split_band(g, carry):
        bh_ref[g], bl_ref[g] = halves(band_ref[g])
        return carry

    lax.fori_loop(0, windows, split_band, 0)
    lh_ref[...], ll_ref[...] = halves(lband_ref[...])
    rh_ref[...], rl_ref[...] = halves(rband_ref[...])

    zero = jnp.zeros((LOW - EDGE, cols), BF16)
    tail = jnp.zeros((frame - high - EDGE, cols), BF16)
    for ref in (vh_ref, vl_ref):
        ref[: LOW - EDGE] = zero
        ref[high + EDGE :] = tail
    vh_ref[LOW - EDGE : LOW], vl_ref[LOW - EDGE : LOW] = halves(left_ref[...])
    vh_ref[high : high + EDGE], vl_ref[high : high + EDGE] = halves(right_ref[...])
    chunk = 256

    def split_own(i, carry):
        at = pl.multiple_of(i * chunk, chunk)
        h, l = halves(own_ref[pl.ds(at, chunk), :])
        vh_ref[pl.ds(LOW + at, chunk), :] = h
        vl_ref[pl.ds(LOW + at, chunk), :] = l
        return carry

    lax.fori_loop(0, own // chunk, split_own, 0)

    def apply(xh_ref, xl_ref):
        y_ref[...] = jnp.zeros_like(y_ref)

        def window(i, carry):
            values = []
            for n in range(3):
                at = pl.multiple_of(HALO + (3 * i + n) * STEP, 64)
                xh = xh_ref[pl.ds(at, WIN), :]
                xl = xl_ref[pl.ds(at, WIN), :]
                values.append((at, dot3(bh_ref[3 * i + n], bl_ref[3 * i + n], xh, xl)))
            for at, value in values:
                y_ref[pl.ds(at, WIN), :] += value
            return carry

        lax.fori_loop(0, windows // 3, window, 0)

        def extra(h_ref, l_ref, lo, rows, out, at):
            y_ref[out : out + rows] += dot3(
                h_ref[lo : lo + rows], l_ref[lo : lo + rows],
                xh_ref[at : at + WIN], xl_ref[at : at + WIN],
            )

        extra(lh_ref, ll_ref, 0, 128, HALO, 0)
        extra(lh_ref, ll_ref, 128, 192, HALO + 64, HALO + 64)
        extra(rh_ref, rl_ref, 0, 256, own + HALO, own + HALO)
        extra(rh_ref, rl_ref, 256, 64, own + HALO + STEP, own + HALO + STEP)

    def keep(oh_ref, ol_ref):
        oh_ref[:HALO] = jnp.zeros((HALO, cols), BF16)
        ol_ref[:HALO] = jnp.zeros((HALO, cols), BF16)
        oh_ref[high + HALO :] = jnp.zeros((frame - high - HALO, cols), BF16)
        ol_ref[high + HALO :] = jnp.zeros((frame - high - HALO, cols), BF16)
        lower = jnp.where(valid_ref[0] > 0, y_ref[HALO:LOW], 0.0)
        upper = jnp.where(valid_ref[1] > 0, y_ref[high : high + HALO], 0.0)
        oh_ref[HALO:LOW], ol_ref[HALO:LOW] = halves(lower)
        oh_ref[high : high + HALO], ol_ref[high : high + HALO] = halves(upper)

        def split(i, carry):
            at = pl.multiple_of(LOW + i * chunk, chunk)
            h, l = halves(y_ref[pl.ds(at, chunk), :])
            oh_ref[pl.ds(at, chunk), :] = h
            ol_ref[pl.ds(at, chunk), :] = l
            return carry

        lax.fori_loop(0, own // chunk, split, 0)

    tn = ((0,), (0,))

    def put(n, value):
        here = valid_ref[2] == n // ITERS

        @pl.when(here)
        def _():
            for c in range(cols // 128):
                mine_ref[n % ITERS, c] = value[:, c * 128 : (c + 1) * 128]

        @pl.when(jnp.logical_not(here))
        def _():
            for c in range(cols // 128):
                theirs_ref[n % ITERS, c] = value[:, c * 128 : (c + 1) * 128]

    def moments(n, xh_ref, xl_ref, zh_ref, zl_ref):
        xh, zh = xh_ref[LOW:high], zh_ref[LOW:high]
        by_high = dot(xh, jnp.concatenate([xh, xl_ref[LOW:high], zh, zl_ref[LOW:high]], axis=1), tn)
        by_low = dot(xl_ref[LOW:high], zh, tn)
        cross = by_high[:, cols : 2 * cols]
        put(n, by_high[:, :cols] + (cross + cross.T))
        put(n + 1, by_high[:, 2 * cols : 3 * cols] + (by_high[:, 3 * cols :] + by_low))

    apply(vh_ref, vl_ref)
    k1_ref[...] = y_ref[LOW:high]
    keep(wh_ref, wl_ref)
    moments(0, vh_ref, vl_ref, wh_ref, wl_ref)
    apply(wh_ref, wl_ref)
    k2_ref[...] = y_ref[LOW:high]
    keep(vh_ref, vl_ref)
    moments(2, wh_ref, wl_ref, vh_ref, vl_ref)
    apply(vh_ref, vl_ref)
    keep(wh_ref, wl_ref)
    moments(4, vh_ref, vl_ref, wh_ref, wl_ref)


def powers(vector, left, right, valid, bands):
    band, lband, rband = bands
    own, cols = vector.shape
    frame = own + 2 * LOW + 64
    full = jax.ShapeDtypeStruct((own, cols), F32)
    half = jax.ShapeDtypeStruct((ITERS, cols // 128, cols, 128), F32)
    wide = pltpu.VMEM((frame, cols), BF16)
    edge = pltpu.VMEM(lband.shape, BF16)
    return pl.pallas_call(
        powers_kernel,
        out_shape=(full, full, half, half),
        in_specs=[pl.BlockSpec(memory_space=pltpu.SMEM)] + in_vmem(6),
        out_specs=tuple(in_vmem(4)),
        compiler_params=pltpu.CompilerParams(vmem_limit_bytes=32 << 20),
        scratch_shapes=[pltpu.VMEM(band.shape, BF16)] * 2 + [edge] * 4 + [wide] * 4
        + [pltpu.VMEM((frame, cols), F32)],
        name="powers",
    )(valid, vector, left, right, band, lband, rband)


def diagonals(matrix):
    size = matrix.shape[0]
    on = jnp.where(iota((size, size), 0) == iota((size, size), 1), matrix, 0.0)
    return jnp.sum(on, axis=0, keepdims=True), jnp.sum(on, axis=1, keepdims=True)


def split_dot(a, b):
    return dot3(*halves(a), *halves(b))


def inverse_spd(matrix, mul, limit):
    size = matrix.shape[0]
    unit = (iota((size, size), 0) == iota((size, size), 1)).astype(F32)
    along, down = diagonals(matrix)
    scale = lax.rsqrt(along) * lax.rsqrt(down)
    scaled = matrix * scale
    norm = jnp.max(jnp.sum(jnp.abs(scaled), axis=1, keepdims=True))
    factor = jnp.where(norm < 1.9, 1.0, 1.9 / norm)
    rest = unit - factor * scaled

    def going(state):
        k, worst, _, _ = state
        return (k < 40) & (worst > limit)

    def step(state):
        k, _, total, power = state
        both = mul(jnp.concatenate([total, power], axis=0), power)
        total = total + both[:size]
        power = both[size:]
        return k + 1, jnp.max(jnp.abs(power)), total, power

    total = factor * (unit + rest)
    power = mul(rest, rest)
    rounds, worst, total, _ = lax.while_loop(
        going, step, (1, jnp.max(jnp.abs(power)), total, power)
    )
    return total * scale, worst, rounds


def ratio(left, whole):
    return jnp.min(diagonals(left)[0] / diagonals(whole)[0])


def galerkin_kernel(core_ref, mine_ref, theirs_ref, out_ref, good_ref, mom_ref):
    parts = mine_ref.shape[1]

    def unpack(source_ref, start):
        for n in range(ITERS):
            mom_ref[start + n] = jnp.concatenate([source_ref[n, c] for c in range(parts)], axis=1)

    @pl.when(core_ref[0] == 0)
    def _():
        unpack(mine_ref, 0)
        unpack(theirs_ref, ITERS)

    @pl.when(core_ref[0] != 0)
    def _():
        unpack(theirs_ref, 0)
        unpack(mine_ref, ITERS)

    m = [mom_ref[n] for n in range(2 * ITERS)]
    m = [x if n % 2 == 0 else 0.5 * (x + x.T) for n, x in enumerate(m)]
    h = [m[n + 1] + SHIFT * m[n] for n in range(2 * ITERS - 1)]
    size = m[0].shape[0]

    def right_of(inverse, *targets):
        wide = split_dot(inverse, jnp.concatenate(targets, axis=1))
        return [wide[:, n * size : (n + 1) * size] for n in range(len(targets))]

    s0, w0, k0 = inverse_spd(h[0], split_dot, CLOSE)
    z01, z02, z0m = right_of(s0, h[1], h[2], m[0])
    lower = split_dot(
        jnp.concatenate([h[1], h[2]], axis=0), jnp.concatenate([z01, z02, z0m], axis=1)
    )
    first = h[2] - lower[:size, :size]
    cross = h[3] - lower[:size, size : 2 * size]
    m1 = m[1] - lower[:size, 2 * size :]
    last = h[4] - lower[size:, size : 2 * size]
    m2 = m[2] - lower[size:, 2 * size :]
    first = 0.5 * (first + first.T)
    s1, w1, k1 = inverse_spd(first, split_dot, CLOSE)
    z12, z1m = right_of(s1, cross, m1)
    lower = split_dot(cross.T, jnp.concatenate([z12, z1m], axis=1))
    rest = last - lower[:, :size]
    rest = 0.5 * (rest + rest.T)
    m2 = m2 - lower[:, size:]
    s2, w2, k2 = inverse_spd(rest, split_dot, CLOSE)
    y2 = split_dot(s2, m2)
    y1 = z1m - split_dot(z12, y2)
    y0 = z0m - split_dot(jnp.concatenate([z01, z02], axis=1), jnp.concatenate([y1, y2], axis=0))
    out_ref[:size] = y0
    out_ref[size : 2 * size] = y1
    out_ref[2 * size :] = y2
    share = jnp.minimum(ratio(first, h[2]), ratio(rest, h[4]))
    rounds = jnp.maximum(k0, jnp.maximum(k1, k2))
    worst = jnp.maximum(w0, jnp.maximum(w1, w2))
    good_ref[0] = jnp.where((share > GUARD) & (worst <= CLOSE) & (rounds <= ROUNDS), 1, 0)


def galerkin(core, mine, theirs):
    size = mine.shape[2]
    smem = pl.BlockSpec(memory_space=pltpu.SMEM)
    return pl.pallas_call(
        galerkin_kernel,
        out_shape=(jax.ShapeDtypeStruct((ITERS * size, size), F32), jax.ShapeDtypeStruct((1,), jnp.int32)),
        in_specs=[smem] + in_vmem(2),
        out_specs=(pl.BlockSpec(memory_space=pltpu.VMEM), smem),
        scratch_shapes=[pltpu.VMEM((2 * ITERS, size, size), F32)],
        compiler_params=pltpu.CompilerParams(vmem_limit_bytes=32 << 20),
        name="galerkin",
    )(core, mine, theirs)


def solve_kernel(matrix_ref, target_ref, out_ref):
    matrix = matrix_ref[...]
    matrix = 0.5 * (matrix + matrix.T)
    inverse, _, _ = inverse_spd(matrix, full_dot, 1e-9)
    guess = full_dot(inverse, target_ref[...])
    out_ref[...] = guess + full_dot(inverse, target_ref[...] - full_dot(matrix, guess))


def solve(matrix, target):
    return pl.pallas_call(
        solve_kernel,
        out_shape=jax.ShapeDtypeStruct(target.shape, F32),
        in_specs=in_vmem(2),
        out_specs=in_vmem(1)[0],
        name="solve",
    )(matrix, target)


def total_of(mine, theirs):
    shape = mine.shape
    chips = lax.axis_size(CHIPS)
    other = [(0, 1), (1, 0)]
    pair = mine + lax.ppermute(theirs, "core", other)
    pair = pair.reshape(chips, -1, 128)
    arrived = lax.all_to_all(pair, CHIPS, 0, 0, tiled=True)
    own = jnp.broadcast_to(arrived.sum(axis=0)[None], pair.shape)
    gathered = lax.all_to_all(own, CHIPS, 0, 0, tiled=True)
    gathered = gathered.reshape(shape)
    return gathered, lax.ppermute(gathered, "core", other)


def both_ways(to_right, to_left):
    count = lax.axis_size(AXES)
    up = [(i, i + 1) for i in range(count - 1)]
    return lax.ppermute(to_right, AXES, up), lax.ppermute(to_left, AXES, [(b, a) for a, b in up])


def halo_of(vector):
    return both_ways(vector[-EDGE:], vector[:EDGE])


def plain_cg(right_side, valid, bands):
    def times(a, b):
        return jnp.dot(a, b, preferred_element_type=F32, precision=lax.Precision.HIGHEST)

    def gram_of(parts):
        return jnp.concatenate([parts[0], parts[1]], axis=1)

    def step(k, state):
        answer, residual, direction, gram = state
        on_direction = k % 2 == 0
        vector = jnp.where(on_direction, direction, residual)
        image, _, mine, theirs = powers(vector, *halo_of(vector), valid, bands)
        low, high = total_of(mine, theirs)
        low = jnp.where(valid[2] == 0, low, high)
        square = gram_of(low[0])
        gram = jnp.where(k == 0, square, gram)
        dir_gram = gram_of(low[1]) + SHIFT * square
        factor = solve(
            jnp.where(on_direction, dir_gram, gram), jnp.where(on_direction, gram, square)
        )
        along = times(direction, factor)
        applied = times(image + SHIFT * vector, factor)
        answer = jnp.where(on_direction, answer + along, answer)
        direction = jnp.where(on_direction, direction, residual + along)
        residual = jnp.where(on_direction, residual - applied, residual)
        return answer, residual, direction, jnp.where(on_direction, gram, square)

    state = (jnp.zeros_like(right_side), right_side, right_side, jnp.zeros((right_side.shape[1],) * 2, F32))
    return lax.fori_loop(0, 2 * ITERS - 1, step, state)[0]


def loads_kernel(nodes_ref, load_ref, high_ref, low_ref):
    groups, pairs = nodes_ref.shape
    slots = 8
    support = pairs // slots
    blocks = high_ref.shape[1] // 128
    own_lane = iota((slots, pairs), 1) // support == iota((slots, pairs), 0)
    row = iota((128, pairs), 0)

    def half_group(g):
        nodes = nodes_ref[pl.ds(g, 1), :]
        hot = jnp.where(row == nodes % 128, 1.0, 0.0).astype(BF16)
        block = jnp.broadcast_to(nodes // 128, (slots, pairs))
        terms = []
        for k in range(3):
            spread = jnp.where(own_lane, load_ref[k, pl.ds(g, 1), :], 0.0)
            high = spread.astype(BF16).astype(F32)
            terms.append((high, spread - high))
        rows = []
        for c in range(blocks):
            hit = block == c
            for high, low in terms:
                rows.append(
                    jnp.concatenate([jnp.where(hit, high, 0.0), jnp.where(hit, low, 0.0)], axis=1)
                )
        left = jnp.concatenate(rows, axis=0).astype(BF16)
        return dot(left, jnp.concatenate([hot, hot], axis=1), ((1,), (1,)))

    def group(g, carry):
        first = half_group(2 * g)
        second = half_group(2 * g + 1)
        total = groups * slots
        for c in range(blocks):
            for k in range(3):
                at = (c * 3 + k) * slots
                value = jnp.concatenate([first[at : at + slots], second[at : at + slots]], axis=0)
                high, low = halves(value)
                to = pl.multiple_of(k * total + g * 2 * slots, 16)
                high_ref[pl.ds(to, 2 * slots), c * 128 : (c + 1) * 128] = high
                low_ref[pl.ds(to, 2 * slots), c * 128 : (c + 1) * 128] = low
        return carry

    lax.fori_loop(0, groups // 2, group, 0)


def load_matrix(slot_nodes, slot_load, rows):
    support, slots = slot_nodes.shape
    groups = slots * support // 128
    nodes = slot_nodes.T.reshape(groups, 128)
    loads = slot_load.reshape(support, slots, 3).transpose(2, 1, 0).reshape(3, groups, 128)
    out = jax.ShapeDtypeStruct((3 * slots, rows), BF16)
    return pl.pallas_call(
        loads_kernel,
        out_shape=(out, out),
        in_specs=in_vmem(2),
        out_specs=tuple(in_vmem(2)),
        compiler_params=pltpu.CompilerParams(vmem_limit_bytes=20 << 20),
        name="loads",
    )(nodes, loads)


CHUNK = 512


def basis_kernel(*refs):
    *vector_refs, wh_ref, wl_ref, out_ref = refs

    @pl.when(pl.program_id(0) == 0)
    def _():
        out_ref[...] = jnp.zeros_like(out_ref)

    slots = out_ref.shape[0]
    cols = vector_refs[0].shape[1]
    count = len(vector_refs)
    for n, ref in enumerate(vector_refs):
        full = dot3(wh_ref[...], wl_ref[...], *halves(ref[...]))
        for k in range(3):
            at = (k * count + n) * cols
            out_ref[:, at : at + cols] += full[k * slots : (k + 1) * slots]


def basis(vectors, weights):
    rows, cols = vectors[0].shape
    loads = weights[0].shape[0]
    weight = pl.BlockSpec((loads, CHUNK), lambda i: (0, i))
    out = (loads // 3, 3 * len(vectors) * cols)
    return pl.pallas_call(
        basis_kernel,
        grid=(rows // CHUNK,),
        out_shape=jax.ShapeDtypeStruct(out, F32),
        in_specs=[pl.BlockSpec((CHUNK, cols), lambda i: (i, 0))] * len(vectors) + [weight, weight],
        out_specs=pl.BlockSpec(out, lambda i: (0, 0)),
        compiler_params=pltpu.CompilerParams(vmem_limit_bytes=28 << 20),
        name="basis",
    )(*vectors, *weights)


def to_owner(rows, dipole_slot):
    slots, wide = rows.shape
    count = lax.axis_size(AXES)
    received = lax.all_to_all(rows.reshape(count, slots // count, wide), AXES, 0, 0, tiled=True)
    return received.reshape(slots, wide)[dipole_slot]


def combine_kernel(k0_ref, k1_ref, k2_ref, c_ref, picked_ref, x_ref, out_ref, ch_ref, cl_ref):
    size = c_ref.shape[1]

    @pl.when(pl.program_id(0) == 0)
    def _():
        ch_ref[...], cl_ref[...] = halves(c_ref[...])
        wide = c_ref.shape[0]
        for k in range(3):
            out_ref[k] = dot3(*halves(picked_ref[:, k * wide : (k + 1) * wide]), ch_ref[...], cl_ref[...])

    total = jnp.zeros(x_ref.shape, F32)
    for n, ref in enumerate((k0_ref, k1_ref, k2_ref)):
        ah, al = halves(ref[...])
        at = n * size
        total = total + dot3(ah, al, ch_ref[at : at + size], cl_ref[at : at + size])
    x_ref[...] = total


def combine(k0, k1, k2, coef, picked):
    rows, cols = k0.shape
    block = pl.BlockSpec((CHUNK, cols), lambda i: (i, 0))
    whole = lambda shape: pl.BlockSpec(shape, lambda i: (0,) * len(shape))
    out = (3, picked.shape[0], cols)
    return pl.pallas_call(
        combine_kernel,
        grid=(rows // CHUNK,),
        out_shape=(jax.ShapeDtypeStruct((rows, cols), F32), jax.ShapeDtypeStruct(out, F32)),
        in_specs=[block] * 3 + [whole(coef.shape), whole(picked.shape)],
        out_specs=(block, whole(out)),
        scratch_shapes=[pltpu.VMEM(coef.shape, BF16)] * 2,
        compiler_params=pltpu.CompilerParams(vmem_limit_bytes=28 << 20),
        name="combine",
    )(k0, k1, k2, coef, picked)


def exact_path(right_side, valid, bands, weights, dipole_slot):
    answer = plain_cg(right_side, valid, bands)
    picked = to_owner(basis([answer], weights), dipole_slot)
    return answer, picked.reshape(picked.shape[0], 3, -1).transpose(1, 0, 2)


def one_device(right_side, tile_stiff, tile_nodes, node_shift, slot_nodes, slot_load, dipole_slot):
    count = lax.axis_size(AXES)
    index = lax.axis_index(AXES)
    core = lax.axis_index("core")
    valid = jnp.stack([index > 0, index < count - 1, core]).astype(jnp.int32)
    left, right = halo_of(right_side)
    band = assemble(tile_stiff, tile_nodes, node_shift)
    to_right = jnp.concatenate([band[-2, 128:], band[-1, :192]], axis=0)
    to_left = jnp.concatenate([band[0], band[1, :64]], axis=0)
    bands = (band, *both_ways(to_right, to_left))
    weights = load_matrix(slot_nodes, slot_load, right_side.shape[0])
    k1, k2, mine, theirs = powers(right_side, left, right, valid, bands)
    rows = basis([right_side, k1, k2], weights)
    picked = to_owner(rows, dipole_slot)
    coef, good = galerkin(core[None], *total_of(mine, theirs))
    return lax.cond(
        good[0] > 0,
        lambda: combine(right_side, k1, k2, coef, picked),
        lambda: exact_path(right_side, valid, bands, weights, dipole_slot),
    )


def solution(mesh):
    rows, depth = mesh.devices.shape
    outer = 4 if rows % 4 == 0 else 1
    flat = Mesh(mesh.devices.reshape(outer, rows // outer, depth // 2, 2), AXES)
    return jax.shard_map(
        one_device,
        mesh=flat,
        in_specs=(
            P(AXES, None),
            P(AXES, None, None),
            P(AXES, None),
            P(AXES),
            P(None, AXES),
            P(None, AXES),
            P(AXES),
        ),
        out_specs=(P(AXES, None), P(None, AXES, None)),
        check_vma=False,
    )
```

```python
import jax
import jax.numpy as jnp
from jax import lax
from jax.experimental import pallas as pl
from jax.experimental.pallas import tpu as pltpu
from jax.sharding import Mesh
from jax.sharding import PartitionSpec as P


F32 = jnp.float32
BF16 = jnp.bfloat16
AXES = ("row", "column", "depth", "core")
CHIPS = ("row", "column", "depth")
ITERS = 3
HALO = 128
REACH = 64
WIN = 256
STEP = WIN - REACH
SHIFT = 4.5
ROUNDS = 8
CLOSE = 1e-7
GUARD = 0.01
SMALL = 128
SPAN = 80
BATCH = 8
TOGETHER = 2
EDGE = 192


def dot(a, b, dims=((1,), (0,))):
    return lax.dot_general(a, b, (dims, ((), ())), preferred_element_type=F32)


def halves(x):
    high = x.astype(BF16)
    return high, (x - high.astype(F32)).astype(BF16)


def dot3(ah, al, bh, bl, dims=((1,), (0,))):
    return dot(ah, bh, dims) + (dot(ah, bl, dims) + dot(al, bh, dims))


def full_dot(a, b):
    return lax.dot_general(
        a, b, (((1,), (0,)), ((), ())), preferred_element_type=F32, precision=lax.Precision.HIGHEST
    )


def iota(shape, dim):
    return lax.broadcasted_iota(jnp.int32, shape, dim)


def in_vmem(count):
    return [pl.BlockSpec(memory_space=pltpu.VMEM)] * count


def assemble_kernel(
    group_ref, first_ref, stiff_ref, place_ref, offset_ref, diag_ref,
    out_ref, up_ref, down_ref,
    rows_ref, small_ref, block_ref, lane_ref, wait_ref,
):
    slots, _, tiles = stiff_ref.shape
    windows = out_ref.shape[0]
    lanes = BATCH * slots
    one = lambda mask: jnp.where(mask, 1.0, 0.0).astype(BF16)
    block_ref[...] = one(iota((lanes, lanes), 0) % BATCH == iota((lanes, lanes), 1) // slots)
    for t in range(BATCH):
        lane_ref[t * SPAN : (t + 1) * SPAN] = one(iota((SPAN, lanes), 1) % BATCH == t)

    def clear(g, carry):
        small_ref[g] = jnp.zeros((SMALL, SMALL), F32)
        return carry

    lax.fori_loop(0, small_ref.shape[0], clear, 0)

    def turn(i, carry):
        for n in range(4):
            plane = stiff_ref[4 * i + n]
            rows_ref[4 * i + n] = jnp.concatenate([plane] * (128 // slots), axis=0).T
        return carry

    lax.fori_loop(0, slots // 4, turn, 0)

    row_in_window = iota((SMALL, lanes), 0)
    row_in_span = iota((SPAN, lanes), 0)

    def first_side(b):
        base = pl.multiple_of(b * BATCH, BATCH)
        parts = halves(rows_ref[:, pl.ds(base, BATCH), :].reshape(lanes, 128))
        block = block_ref[...]
        wide = [jnp.concatenate([part] * (lanes // 128), axis=1) * block for part in parts]
        hot = one(row_in_window == place_ref[pl.ds(b, 1), :])
        return jnp.concatenate(wide, axis=0), hot

    def second_side(b):
        match = one(row_in_span == offset_ref[pl.ds(b, 1), :])
        return jnp.concatenate([match] * BATCH, axis=0) * lane_ref[...]

    def compute(i):
        batches = [TOGETHER * i + n for n in range(TOGETHER)]
        sides = [first_side(b) for b in batches]
        both = [dot(wide, hot, ((1,), (1,))) for wide, hot in sides]
        picks = [second_side(b) for b in batches]
        rights = [jnp.concatenate(halves(x[:lanes] + x[lanes:]), axis=1) for x in both]
        full = [dot(pick, right) for pick, right in zip(picks, rights)]
        return [x[:, :SMALL] + x[:, SMALL:] for x in full]

    def hold(full):
        for n in range(TOGETHER):
            wait_ref[n] = full[n]

    def add_up(i):
        for n in range(TOGETHER):
            for t in range(BATCH):
                tile = (TOGETHER * i + n) * BATCH + t
                r = pl.multiple_of(first_ref[tile], 16)
                small_ref[group_ref[tile], pl.ds(r, SPAN), :] += wait_ref[n, t * SPAN : (t + 1) * SPAN]

    rounds = tiles // (BATCH * TOGETHER)
    hold(compute(0))

    def batch(i, carry):
        full = compute(i)
        add_up(i - 1)
        hold(full)
        return carry

    lax.fori_loop(1, rounds, batch, 0)
    add_up(rounds - 1)

    eye = iota((WIN, WIN), 0) == iota((WIN, WIN), 1)
    gap = jnp.zeros((SMALL, REACH), F32)

    def gather(g, carry):
        out_ref[g] = jnp.where(eye, diag_ref[pl.ds(g, 1), :], 0.0)
        out_ref[g, :SMALL, :SMALL] += small_ref[3 * g]
        middle = jnp.concatenate([gap, small_ref[3 * g + 1], gap], axis=1)
        out_ref[g, REACH : REACH + SMALL, :] += middle
        out_ref[g, SMALL:, SMALL:] += small_ref[3 * g + 2]
        return carry

    lax.fori_loop(0, windows, gather, 0)
    up_ref[:128] = out_ref[windows - 2, 128:]
    up_ref[128:] = out_ref[windows - 1, :192]
    down_ref[:WIN] = out_ref[0]
    down_ref[WIN:] = out_ref[1, :64]


def assemble(tile_stiff, tile_nodes, node_shift):
    tiles, slots = tile_nodes.shape
    ext = node_shift.shape[0] + 2 * HALO
    windows = ext // STEP
    smalls = ext // REACH
    lowest = jnp.min(tile_nodes, axis=1)
    group = jnp.minimum(lowest // REACH, smalls - 1)
    first = jnp.minimum((lowest - group * REACH) // 16 * 16, REACH - 16)
    place = jnp.where(tile_nodes == ext, -1, tile_nodes - group[:, None] * REACH)
    offset = jnp.where(tile_nodes == ext, -1, place - first[:, None])
    diag = jnp.pad(node_shift - SHIFT, (HALO, HALO)).reshape(windows, STEP)
    diag = jnp.pad(diag, ((0, 0), (0, WIN - STEP)))
    lanes = BATCH * slots
    smem = pl.BlockSpec(memory_space=pltpu.SMEM)
    edge = jax.ShapeDtypeStruct((320, WIN), F32)
    return pl.pallas_call(
        assemble_kernel,
        out_shape=(jax.ShapeDtypeStruct((windows, WIN, WIN), F32), edge, edge),
        in_specs=[smem, smem] + in_vmem(4),
        out_specs=tuple(in_vmem(3)),
        scratch_shapes=[
            pltpu.VMEM((slots, tiles, 128), F32),
            pltpu.VMEM((smalls, SMALL, SMALL), F32),
            pltpu.VMEM((lanes, lanes), BF16),
            pltpu.VMEM((BATCH * SPAN, lanes), BF16),
            pltpu.VMEM((TOGETHER, BATCH * SPAN, SMALL), F32),
        ],
        compiler_params=pltpu.CompilerParams(vmem_limit_bytes=28 << 20),
        name="assemble",
    )(
        group,
        first,
        jnp.transpose(tile_stiff, (1, 2, 0)),
        place.reshape(-1, lanes),
        offset.reshape(-1, BATCH, slots).transpose(0, 2, 1).reshape(-1, lanes),
        diag,
    )


LOW = 2 * HALO


def powers_kernel(
    valid_ref, own_ref, left_ref, right_ref, band_ref, lband_ref, rband_ref,
    image_ref, mine_ref, theirs_ref,
    bh_ref, bl_ref, lh_ref, ll_ref, rh_ref, rl_ref, vh_ref, vl_ref, y_ref,
):
    own, cols = own_ref.shape
    windows = band_ref.shape[0]
    frame = y_ref.shape[0]
    high = LOW + own
    chunk = 256

    def split_band(g, carry):
        bh_ref[g], bl_ref[g] = halves(band_ref[g])
        return carry

    lax.fori_loop(0, windows, split_band, 0)
    lh_ref[...], ll_ref[...] = halves(lband_ref[...])
    rh_ref[...], rl_ref[...] = halves(rband_ref[...])
    for ref in (vh_ref, vl_ref):
        for n, width in enumerate((EDGE, HALO)):
            ref[n, : LOW - width] = jnp.zeros((LOW - width, cols), BF16)
            ref[n, high + width :] = jnp.zeros((frame - high - width, cols), BF16)

    def put(n, at, value):
        vh_ref[n, at, :], vl_ref[n, at, :] = halves(value)

    put(0, pl.ds(LOW - EDGE, EDGE), left_ref[...])
    put(0, pl.ds(high, EDGE), right_ref[...])

    def split_own(i, carry):
        at = pl.multiple_of(i * chunk, chunk)
        put(0, pl.ds(LOW + at, chunk), own_ref[pl.ds(at, chunk), :])
        return carry

    lax.fori_loop(0, own // chunk, split_own, 0)

    def clear(i, carry):
        y_ref[pl.ds(pl.multiple_of(i * 64, 64), 64), :] = jnp.zeros((64, cols), F32)
        return carry

    tn = ((0,), (0,))

    def keep_moment(j, value):
        here = valid_ref[2] == j // ITERS
        for ref, chosen in ((mine_ref, here), (theirs_ref, jnp.logical_not(here))):
            @pl.when(chosen)
            def _(ref=ref):
                for c in range(cols // 128):
                    ref[j % ITERS, c] = value[:, c * 128 : (c + 1) * 128]

    def power(n, carry):
        now = n % 2
        then = 1 - now
        lax.fori_loop(0, frame // 64, clear, 0)

        def window(i, carry):
            values = []
            for m in range(3):
                at = pl.multiple_of(HALO + (3 * i + m) * STEP, 64)
                xh = vh_ref[now, pl.ds(at, WIN), :]
                xl = vl_ref[now, pl.ds(at, WIN), :]
                values.append((at, dot3(bh_ref[3 * i + m], bl_ref[3 * i + m], xh, xl)))
            for at, value in values:
                y_ref[pl.ds(at, WIN), :] += value
            return carry

        lax.fori_loop(0, windows // 3, window, 0)

        values = []
        for h_ref, l_ref, lo, rows, out, at in (
            (lh_ref, ll_ref, 0, 128, HALO, 0),
            (lh_ref, ll_ref, 128, 192, HALO + 64, HALO + 64),
            (rh_ref, rl_ref, 0, 256, own + HALO, own + HALO),
            (rh_ref, rl_ref, 256, 64, own + HALO + STEP, own + HALO + STEP),
        ):
            value = dot3(
                h_ref[lo : lo + rows], l_ref[lo : lo + rows],
                vh_ref[now, at : at + WIN], vl_ref[now, at : at + WIN],
            )
            values.append((out, rows, value))
        for out, rows, value in values:
            y_ref[out : out + rows] += value

        put(then, pl.ds(HALO, HALO), jnp.where(valid_ref[0] > 0, y_ref[HALO:LOW], 0.0))
        put(then, pl.ds(high, HALO), jnp.where(valid_ref[1] > 0, y_ref[high : high + HALO], 0.0))

        def split(i, carry):
            at = pl.multiple_of(i * chunk, chunk)
            value = y_ref[pl.ds(LOW + at, chunk), :]
            put(then, pl.ds(LOW + at, chunk), value)

            @pl.when(n + 1 < ITERS)
            def _():
                image_ref[jnp.minimum(n, ITERS - 2), pl.ds(at, chunk), :] = value

            return carry

        lax.fori_loop(0, own // chunk, split, 0)

        xh, xl = vh_ref[now, LOW:high], vl_ref[now, LOW:high]
        zh, zl = vh_ref[then, LOW:high], vl_ref[then, LOW:high]
        by_high = dot(xh, jnp.concatenate([xh, xl, zh, zl], axis=1), tn)
        by_low = dot(xl, zh, tn)
        cross = by_high[:, cols : 2 * cols]
        keep_moment(2 * n, by_high[:, :cols] + (cross + cross.T))
        keep_moment(2 * n + 1, by_high[:, 2 * cols : 3 * cols] + (by_high[:, 3 * cols :] + by_low))

        @pl.when(n == 0)
        def _():
            for ref in (vh_ref, vl_ref):
                ref[0, : HALO] = jnp.zeros((HALO, cols), BF16)
                ref[0, high + HALO :] = jnp.zeros((frame - high - HALO, cols), BF16)

        return carry

    lax.fori_loop(0, ITERS, power, 0)


def powers(vector, left, right, valid, bands):
    band, lband, rband = bands
    own, cols = vector.shape
    frame = own + 2 * LOW + 64
    half = jax.ShapeDtypeStruct((ITERS, cols // 128, cols, 128), F32)
    wide = pltpu.VMEM((2, frame, cols), BF16)
    edge = pltpu.VMEM(lband.shape, BF16)
    return pl.pallas_call(
        powers_kernel,
        out_shape=(jax.ShapeDtypeStruct((ITERS - 1, own, cols), F32), half, half),
        in_specs=[pl.BlockSpec(memory_space=pltpu.SMEM)] + in_vmem(6),
        out_specs=tuple(in_vmem(3)),
        compiler_params=pltpu.CompilerParams(vmem_limit_bytes=32 << 20),
        scratch_shapes=[pltpu.VMEM(band.shape, BF16)] * 2 + [edge] * 4 + [wide] * 2
        + [pltpu.VMEM((frame, cols), F32)],
        name="powers",
    )(valid, vector, left, right, band, lband, rband)


def diagonals(matrix):
    size = matrix.shape[0]
    on = jnp.where(iota((size, size), 0) == iota((size, size), 1), matrix, 0.0)
    return jnp.sum(on, axis=0, keepdims=True), jnp.sum(on, axis=1, keepdims=True)


def split_dot(a, b):
    return dot3(*halves(a), *halves(b))


def inverse_spd(matrix, mul, limit):
    size = matrix.shape[0]
    unit = (iota((size, size), 0) == iota((size, size), 1)).astype(F32)
    along, down = diagonals(matrix)
    scale = lax.rsqrt(along) * lax.rsqrt(down)
    scaled = matrix * scale
    norm = jnp.max(jnp.sum(jnp.abs(scaled), axis=1, keepdims=True))
    factor = jnp.where(norm < 1.9, 1.0, 1.9 / norm)
    rest = unit - factor * scaled

    def going(state):
        k, worst, _, _ = state
        return (k < 40) & (worst > limit)

    def step(state):
        k, _, total, power = state
        both = mul(jnp.concatenate([total, power], axis=0), power)
        total = total + both[:size]
        power = both[size:]
        return k + 1, jnp.max(jnp.abs(power)), total, power

    total = factor * (unit + rest)
    power = mul(rest, rest)
    rounds, worst, total, _ = lax.while_loop(
        going, step, (1, jnp.max(jnp.abs(power)), total, power)
    )
    return total * scale, worst, rounds


def ratio(left, whole):
    return jnp.min(diagonals(left)[0] / diagonals(whole)[0])


def galerkin_kernel(core_ref, mine_ref, theirs_ref, out_ref, good_ref, mom_ref):
    parts = mine_ref.shape[1]

    def unpack(source_ref, start):
        for n in range(ITERS):
            mom_ref[start + n] = jnp.concatenate([source_ref[n, c] for c in range(parts)], axis=1)

    @pl.when(core_ref[0] == 0)
    def _():
        unpack(mine_ref, 0)
        unpack(theirs_ref, ITERS)

    @pl.when(core_ref[0] != 0)
    def _():
        unpack(theirs_ref, 0)
        unpack(mine_ref, ITERS)

    m = [mom_ref[n] for n in range(2 * ITERS)]
    m = [x if n % 2 == 0 else 0.5 * (x + x.T) for n, x in enumerate(m)]
    h = [m[n + 1] + SHIFT * m[n] for n in range(2 * ITERS - 1)]
    size = m[0].shape[0]

    def right_of(inverse, *targets):
        wide = split_dot(inverse, jnp.concatenate(targets, axis=1))
        return [wide[:, n * size : (n + 1) * size] for n in range(len(targets))]

    s0, w0, k0 = inverse_spd(h[0], split_dot, CLOSE)
    z01, z02, z0m = right_of(s0, h[1], h[2], m[0])
    lower = split_dot(
        jnp.concatenate([h[1], h[2]], axis=0), jnp.concatenate([z01, z02, z0m], axis=1)
    )
    first = h[2] - lower[:size, :size]
    cross = h[3] - lower[:size, size : 2 * size]
    m1 = m[1] - lower[:size, 2 * size :]
    last = h[4] - lower[size:, size : 2 * size]
    m2 = m[2] - lower[size:, 2 * size :]
    first = 0.5 * (first + first.T)
    s1, w1, k1 = inverse_spd(first, split_dot, CLOSE)
    z12, z1m = right_of(s1, cross, m1)
    lower = split_dot(cross.T, jnp.concatenate([z12, z1m], axis=1))
    rest = last - lower[:, :size]
    rest = 0.5 * (rest + rest.T)
    m2 = m2 - lower[:, size:]
    s2, w2, k2 = inverse_spd(rest, split_dot, CLOSE)
    y2 = split_dot(s2, m2)
    y1 = z1m - split_dot(z12, y2)
    y0 = z0m - split_dot(jnp.concatenate([z01, z02], axis=1), jnp.concatenate([y1, y2], axis=0))
    out_ref[:size] = y0
    out_ref[size : 2 * size] = y1
    out_ref[2 * size :] = y2
    share = jnp.minimum(ratio(first, h[2]), ratio(rest, h[4]))
    rounds = jnp.maximum(k0, jnp.maximum(k1, k2))
    worst = jnp.maximum(w0, jnp.maximum(w1, w2))
    good_ref[0] = jnp.where((share > GUARD) & (worst <= CLOSE) & (rounds <= ROUNDS), 1, 0)


def galerkin(core, mine, theirs):
    size = mine.shape[2]
    smem = pl.BlockSpec(memory_space=pltpu.SMEM)
    return pl.pallas_call(
        galerkin_kernel,
        out_shape=(jax.ShapeDtypeStruct((ITERS * size, size), F32), jax.ShapeDtypeStruct((1,), jnp.int32)),
        in_specs=[smem] + in_vmem(2),
        out_specs=(pl.BlockSpec(memory_space=pltpu.VMEM), smem),
        scratch_shapes=[pltpu.VMEM((2 * ITERS, size, size), F32)],
        compiler_params=pltpu.CompilerParams(vmem_limit_bytes=32 << 20),
        name="galerkin",
    )(core, mine, theirs)


def solve_kernel(matrix_ref, target_ref, out_ref):
    matrix = matrix_ref[...]
    matrix = 0.5 * (matrix + matrix.T)
    inverse, _, _ = inverse_spd(matrix, full_dot, 1e-9)
    guess = full_dot(inverse, target_ref[...])
    out_ref[...] = guess + full_dot(inverse, target_ref[...] - full_dot(matrix, guess))


def solve(matrix, target):
    return pl.pallas_call(
        solve_kernel,
        out_shape=jax.ShapeDtypeStruct(target.shape, F32),
        in_specs=in_vmem(2),
        out_specs=in_vmem(1)[0],
        name="solve",
    )(matrix, target)


def total_of(mine, theirs):
    shape = mine.shape
    chips = lax.axis_size(CHIPS)
    other = [(0, 1), (1, 0)]
    pair = mine + lax.ppermute(theirs, "core", other)
    pair = pair.reshape(chips, -1, 128)
    arrived = lax.all_to_all(pair, CHIPS, 0, 0, tiled=True)
    own = jnp.broadcast_to(arrived.sum(axis=0)[None], pair.shape)
    gathered = lax.all_to_all(own, CHIPS, 0, 0, tiled=True)
    gathered = gathered.reshape(shape)
    return gathered, lax.ppermute(gathered, "core", other)


def both_ways(to_right, to_left):
    count = lax.axis_size(AXES)
    up = [(i, i + 1) for i in range(count - 1)]
    return lax.ppermute(to_right, AXES, up), lax.ppermute(to_left, AXES, [(b, a) for a, b in up])


def halo_of(vector):
    return both_ways(vector[-EDGE:], vector[:EDGE])


def plain_cg(right_side, valid, bands):
    def times(a, b):
        return jnp.dot(a, b, preferred_element_type=F32, precision=lax.Precision.HIGHEST)

    def gram_of(parts):
        return jnp.concatenate([parts[0], parts[1]], axis=1)

    def step(k, state):
        answer, residual, direction, gram = state
        on_direction = k % 2 == 0
        vector = jnp.where(on_direction, direction, residual)
        image, mine, theirs = powers(vector, *halo_of(vector), valid, bands)
        low, high = total_of(mine, theirs)
        low = jnp.where(valid[2] == 0, low, high)
        square = gram_of(low[0])
        gram = jnp.where(k == 0, square, gram)
        dir_gram = gram_of(low[1]) + SHIFT * square
        factor = solve(
            jnp.where(on_direction, dir_gram, gram), jnp.where(on_direction, gram, square)
        )
        along = times(direction, factor)
        applied = times(image[0] + SHIFT * vector, factor)
        answer = jnp.where(on_direction, answer + along, answer)
        direction = jnp.where(on_direction, direction, residual + along)
        residual = jnp.where(on_direction, residual - applied, residual)
        return answer, residual, direction, jnp.where(on_direction, gram, square)

    state = (jnp.zeros_like(right_side), right_side, right_side, jnp.zeros((right_side.shape[1],) * 2, F32))
    return lax.fori_loop(0, 2 * ITERS - 1, step, state)[0]


def loads_kernel(nodes_ref, load_ref, high_ref, low_ref):
    groups, pairs = nodes_ref.shape
    slots = 8
    support = pairs // slots
    blocks = high_ref.shape[1] // 128
    own_lane = iota((slots, pairs), 1) // support == iota((slots, pairs), 0)
    row = iota((128, pairs), 0)

    def half_group(g):
        nodes = nodes_ref[pl.ds(g, 1), :]
        hot = jnp.where(row == nodes % 128, 1.0, 0.0).astype(BF16)
        block = jnp.broadcast_to(nodes // 128, (slots, pairs))
        terms = []
        for k in range(3):
            spread = jnp.where(own_lane, load_ref[k, pl.ds(g, 1), :], 0.0)
            high = spread.astype(BF16).astype(F32)
            terms.append((high, spread - high))
        rows = []
        for c in range(blocks):
            hit = block == c
            for high, low in terms:
                rows.append(
                    jnp.concatenate([jnp.where(hit, high, 0.0), jnp.where(hit, low, 0.0)], axis=1)
                )
        left = jnp.concatenate(rows, axis=0).astype(BF16)
        return dot(left, jnp.concatenate([hot, hot], axis=1), ((1,), (1,)))

    def group(g, carry):
        first = half_group(2 * g)
        second = half_group(2 * g + 1)
        total = groups * slots
        for c in range(blocks):
            for k in range(3):
                at = (c * 3 + k) * slots
                value = jnp.concatenate([first[at : at + slots], second[at : at + slots]], axis=0)
                high, low = halves(value)
                to = pl.multiple_of(k * total + g * 2 * slots, 16)
                high_ref[pl.ds(to, 2 * slots), c * 128 : (c + 1) * 128] = high
                low_ref[pl.ds(to, 2 * slots), c * 128 : (c + 1) * 128] = low
        return carry

    lax.fori_loop(0, groups // 2, group, 0)


def load_matrix(slot_nodes, slot_load, rows):
    support, slots = slot_nodes.shape
    groups = slots * support // 128
    nodes = slot_nodes.T.reshape(groups, 128)
    loads = slot_load.reshape(support, slots, 3).transpose(2, 1, 0).reshape(3, groups, 128)
    out = jax.ShapeDtypeStruct((3 * slots, rows), BF16)
    return pl.pallas_call(
        loads_kernel,
        out_shape=(out, out),
        in_specs=in_vmem(2),
        out_specs=tuple(in_vmem(2)),
        compiler_params=pltpu.CompilerParams(vmem_limit_bytes=20 << 20),
        name="loads",
    )(nodes, loads)


CHUNK = 512


def basis_kernel(*refs):
    *vector_refs, wh_ref, wl_ref, out_ref = refs

    @pl.when(pl.program_id(0) == 0)
    def _():
        out_ref[...] = jnp.zeros_like(out_ref)

    slots = out_ref.shape[0]
    cols = vector_refs[0].shape[1]
    count = len(vector_refs)
    for n, ref in enumerate(vector_refs):
        full = dot3(wh_ref[...], wl_ref[...], *halves(ref[...]))
        for k in range(3):
            at = (k * count + n) * cols
            out_ref[:, at : at + cols] += full[k * slots : (k + 1) * slots]


def basis(vectors, weights):
    rows, cols = vectors[0][0].shape[-2:]
    loads = weights[0].shape[0]
    weight = pl.BlockSpec((loads, CHUNK), lambda i: (0, i))
    out = (loads // 3, 3 * len(vectors) * cols)
    return pl.pallas_call(
        basis_kernel,
        grid=(rows // CHUNK,),
        out_shape=jax.ShapeDtypeStruct(out, F32),
        in_specs=[spec for _, spec in vectors] + [weight, weight],
        out_specs=pl.BlockSpec(out, lambda i: (0, 0)),
        compiler_params=pltpu.CompilerParams(vmem_limit_bytes=28 << 20),
        name="basis",
    )(*[vector for vector, _ in vectors], *weights)


def in_chunks(vector, n=None):
    cols = vector.shape[-1]
    if n is None:
        return vector, pl.BlockSpec((CHUNK, cols), lambda i: (i, 0))
    return vector, pl.BlockSpec((None, CHUNK, cols), lambda i: (n, i, 0))


def to_owner(rows):
    slots, wide = rows.shape
    count = lax.axis_size(AXES)
    return lax.all_to_all(rows.reshape(count, slots // count, wide), AXES, 0, 0, tiled=True)


def combine_kernel(k0_ref, k1_ref, k2_ref, c_ref, x_ref, ch_ref, cl_ref):
    size = c_ref.shape[1]

    @pl.when(pl.program_id(0) == 0)
    def _():
        ch_ref[...], cl_ref[...] = halves(c_ref[...])

    total = jnp.zeros(x_ref.shape, F32)
    for n, ref in enumerate((k0_ref, k1_ref, k2_ref)):
        ah, al = halves(ref[...])
        at = n * size
        total = total + dot3(ah, al, ch_ref[at : at + size], cl_ref[at : at + size])
    x_ref[...] = total


def combine(vectors, coef):
    rows, cols = vectors[0][0].shape[-2:]
    return pl.pallas_call(
        combine_kernel,
        grid=(rows // CHUNK,),
        out_shape=jax.ShapeDtypeStruct((rows, cols), F32),
        in_specs=[spec for _, spec in vectors] + [pl.BlockSpec(coef.shape, lambda i: (0, 0))],
        out_specs=pl.BlockSpec((CHUNK, cols), lambda i: (i, 0)),
        scratch_shapes=[pltpu.VMEM(coef.shape, BF16)] * 2,
        compiler_params=pltpu.CompilerParams(vmem_limit_bytes=20 << 20),
        name="combine",
    )(*[vector for vector, _ in vectors], coef)


def lead_kernel(slot_ref, received_ref, c_ref, out_ref, pick_ref):
    _, places, wide = received_ref.shape
    dipoles = out_ref.shape[1]
    together = 8

    def pick(i, carry):
        for n in range(together):
            slot = slot_ref[i * together + n]
            pick_ref[pl.ds(i * together + n, 1), :] = received_ref[slot // places, pl.ds(slot % places, 1), :]
        return carry

    lax.fori_loop(0, dipoles // together, pick, 0)
    ch, cl = halves(c_ref[...])
    part = wide // 3
    for k in range(3):
        out_ref[k] = dot3(*halves(pick_ref[:, k * part : (k + 1) * part]), ch, cl)


def lead(received, dipole_slot, coef):
    out = (3, dipole_slot.shape[0], coef.shape[1])
    return pl.pallas_call(
        lead_kernel,
        out_shape=jax.ShapeDtypeStruct(out, F32),
        in_specs=[pl.BlockSpec(memory_space=pltpu.SMEM)] + in_vmem(2),
        out_specs=in_vmem(1)[0],
        scratch_shapes=[pltpu.VMEM((dipole_slot.shape[0], received.shape[2]), F32)],
        compiler_params=pltpu.CompilerParams(vmem_limit_bytes=20 << 20),
        name="lead",
    )(dipole_slot, received, coef)


def lead_exactly(answer, weights, dipole_slot):
    received = to_owner(basis([in_chunks(answer)], weights))
    picked = received.reshape(-1, received.shape[2])[dipole_slot]
    return picked.reshape(picked.shape[0], 3, -1).transpose(1, 0, 2)


def one_device(right_side, tile_stiff, tile_nodes, node_shift, slot_nodes, slot_load, dipole_slot):
    count = lax.axis_size(AXES)
    index = lax.axis_index(AXES)
    core = lax.axis_index("core")
    valid = jnp.stack([index > 0, index < count - 1, core]).astype(jnp.int32)
    left, right = halo_of(right_side)
    band, to_right, to_left = assemble(tile_stiff, tile_nodes, node_shift)
    bands = (band, *both_ways(to_right, to_left))
    weights = load_matrix(slot_nodes, slot_load, right_side.shape[0])
    images, mine, theirs = powers(right_side, left, right, valid, bands)
    vectors = [in_chunks(right_side), in_chunks(images, 0), in_chunks(images, 1)]
    rows = basis(vectors, weights)
    received = to_owner(rows)
    mine, theirs = total_of(mine, theirs)
    coef, good = galerkin(core[None], mine, theirs)
    answer = combine(vectors, coef)
    leadfield = lead(received, dipole_slot, coef)

    def exactly(_):
        exact = plain_cg(right_side, valid, bands)
        return jnp.ones((), jnp.int32), exact, lead_exactly(exact, weights, dipole_slot)

    state = lax.while_loop(lambda state: state[0] == 0, exactly, (good[0], answer, leadfield))
    return state[1:]


def solution(mesh):
    rows, depth = mesh.devices.shape
    outer = 4 if rows % 4 == 0 else 1
    flat = Mesh(mesh.devices.reshape(outer, rows // outer, depth // 2, 2), AXES)
    return jax.shard_map(
        one_device,
        mesh=flat,
        in_specs=(
            P(AXES, None),
            P(AXES, None, None),
            P(AXES, None),
            P(AXES),
            P(None, AXES),
            P(None, AXES),
            P(AXES),
        ),
        out_specs=(P(AXES, None), P(None, AXES, None)),
        check_vma=False,
    )
```

```python
import jax
import jax.numpy as jnp
from jax import lax
from jax.experimental import pallas as pl
from jax.experimental.pallas import tpu as pltpu
from jax.sharding import Mesh
from jax.sharding import PartitionSpec as P


F32 = jnp.float32
BF16 = jnp.bfloat16
AXES = ("row", "column", "depth", "core")
CHIPS = ("row", "column", "depth")
ITERS = 3
HALO = 128
REACH = 64
WIN = 256
STEP = WIN - REACH
SHIFT = 4.5
ROUNDS = 8
CLOSE = 1e-6
GUARD = 0.01
SMALL = 128
SPAN = 80
BATCH = 8
TOGETHER = 2
EDGE = 192


def dot(a, b, dims=((1,), (0,))):
    return lax.dot_general(a, b, (dims, ((), ())), preferred_element_type=F32)


def halves(x):
    high = x.astype(BF16)
    return high, (x - high.astype(F32)).astype(BF16)


def dot3(ah, al, bh, bl, dims=((1,), (0,))):
    return dot(ah, bh, dims) + (dot(ah, bl, dims) + dot(al, bh, dims))


def full_dot(a, b):
    return lax.dot_general(
        a, b, (((1,), (0,)), ((), ())), preferred_element_type=F32, precision=lax.Precision.HIGHEST
    )


def iota(shape, dim):
    return lax.broadcasted_iota(jnp.int32, shape, dim)


def in_vmem(count):
    return [pl.BlockSpec(memory_space=pltpu.VMEM)] * count


def assemble_kernel(
    core_ref, group_ref, first_ref, stiff_ref, place_ref, offset_ref, diag_ref,
    out_ref, inner_ref, outer_ref,
    rows_ref, small_ref, block_ref, lane_ref, wait_ref,
):
    slots, _, tiles = stiff_ref.shape
    windows = out_ref.shape[0]
    lanes = BATCH * slots
    one = lambda mask: jnp.where(mask, 1.0, 0.0).astype(BF16)
    block_ref[...] = one(iota((lanes, lanes), 0) % BATCH == iota((lanes, lanes), 1) // slots)
    for t in range(BATCH):
        lane_ref[t * SPAN : (t + 1) * SPAN] = one(iota((SPAN, lanes), 1) % BATCH == t)

    def clear(g, carry):
        small_ref[g] = jnp.zeros((SMALL, SMALL), F32)
        return carry

    lax.fori_loop(0, small_ref.shape[0], clear, 0)

    def turn(i, carry):
        for n in range(4):
            plane = stiff_ref[4 * i + n]
            rows_ref[4 * i + n] = jnp.concatenate([plane] * (128 // slots), axis=0).T
        return carry

    lax.fori_loop(0, slots // 4, turn, 0)

    row_in_window = iota((SMALL, lanes), 0)
    row_in_span = iota((SPAN, lanes), 0)

    def first_side(b):
        base = pl.multiple_of(b * BATCH, BATCH)
        parts = halves(rows_ref[:, pl.ds(base, BATCH), :].reshape(lanes, 128))
        block = block_ref[...]
        wide = [jnp.concatenate([part] * (lanes // 128), axis=1) * block for part in parts]
        hot = one(row_in_window == place_ref[pl.ds(b, 1), :])
        return jnp.concatenate(wide, axis=0), hot

    def second_side(b):
        match = one(row_in_span == offset_ref[pl.ds(b, 1), :])
        return jnp.concatenate([match] * BATCH, axis=0) * lane_ref[...]

    def compute(i):
        batches = [TOGETHER * i + n for n in range(TOGETHER)]
        sides = [first_side(b) for b in batches]
        both = [dot(wide, hot, ((1,), (1,))) for wide, hot in sides]
        picks = [second_side(b) for b in batches]
        rights = [jnp.concatenate(halves(x[:lanes] + x[lanes:]), axis=1) for x in both]
        full = [dot(pick, right) for pick, right in zip(picks, rights)]
        return [x[:, :SMALL] + x[:, SMALL:] for x in full]

    def hold(full):
        for n in range(TOGETHER):
            wait_ref[n] = full[n]

    def add_up(i):
        for n in range(TOGETHER):
            for t in range(BATCH):
                tile = (TOGETHER * i + n) * BATCH + t
                r = pl.multiple_of(first_ref[tile], 16)
                small_ref[group_ref[tile], pl.ds(r, SPAN), :] += wait_ref[n, t * SPAN : (t + 1) * SPAN]

    rounds = tiles // (BATCH * TOGETHER)
    hold(compute(0))

    def batch(i, carry):
        full = compute(i)
        add_up(i - 1)
        hold(full)
        return carry

    lax.fori_loop(1, rounds, batch, 0)
    add_up(rounds - 1)

    eye = iota((WIN, WIN), 0) == iota((WIN, WIN), 1)
    gap = jnp.zeros((SMALL, REACH), F32)

    def gather(g, carry):
        out_ref[g] = jnp.where(eye, diag_ref[pl.ds(g, 1), :], 0.0)
        out_ref[g, :SMALL, :SMALL] += small_ref[3 * g]
        middle = jnp.concatenate([gap, small_ref[3 * g + 1], gap], axis=1)
        out_ref[g, REACH : REACH + SMALL, :] += middle
        out_ref[g, SMALL:, SMALL:] += small_ref[3 * g + 2]
        return carry

    lax.fori_loop(0, windows, gather, 0)

    def edges(up_ref, down_ref):
        up_ref[:128] = out_ref[windows - 2, 128:]
        up_ref[128:] = out_ref[windows - 1, :192]
        down_ref[:WIN] = out_ref[0]
        down_ref[WIN:] = out_ref[1, :64]

    pl.when(core_ref[0] == 0)(lambda: edges(inner_ref, outer_ref))
    pl.when(core_ref[0] != 0)(lambda: edges(outer_ref, inner_ref))


def assemble(core, tile_stiff, tile_nodes, node_shift):
    tiles, slots = tile_nodes.shape
    ext = node_shift.shape[0] + 2 * HALO
    windows = ext // STEP
    smalls = ext // REACH
    lowest = jnp.min(tile_nodes, axis=1)
    group = jnp.minimum(lowest // REACH, smalls - 1)
    first = jnp.minimum((lowest - group * REACH) // 16 * 16, REACH - 16)
    place = jnp.where(tile_nodes == ext, -1, tile_nodes - group[:, None] * REACH)
    offset = jnp.where(tile_nodes == ext, -1, place - first[:, None])
    diag = jnp.pad(node_shift - SHIFT, (HALO, HALO)).reshape(windows, STEP)
    diag = jnp.pad(diag, ((0, 0), (0, WIN - STEP)))
    lanes = BATCH * slots
    smem = pl.BlockSpec(memory_space=pltpu.SMEM)
    edge = jax.ShapeDtypeStruct((320, WIN), F32)
    return pl.pallas_call(
        assemble_kernel,
        out_shape=(jax.ShapeDtypeStruct((windows, WIN, WIN), F32), edge, edge),
        in_specs=[smem] * 3 + in_vmem(4),
        out_specs=tuple(in_vmem(3)),
        scratch_shapes=[
            pltpu.VMEM((slots, tiles, 128), F32),
            pltpu.VMEM((smalls, SMALL, SMALL), F32),
            pltpu.VMEM((lanes, lanes), BF16),
            pltpu.VMEM((BATCH * SPAN, lanes), BF16),
            pltpu.VMEM((TOGETHER, BATCH * SPAN, SMALL), F32),
        ],
        compiler_params=pltpu.CompilerParams(vmem_limit_bytes=28 << 20),
        name="assemble",
    )(
        core,
        group,
        first,
        jnp.transpose(tile_stiff, (1, 2, 0)),
        place.reshape(-1, lanes),
        offset.reshape(-1, BATCH, slots).transpose(0, 2, 1).reshape(-1, lanes),
        diag,
    )


LOW = 2 * HALO


def powers_kernel(
    valid_ref, own_ref, inner_ref, outer_ref, band_ref, iband_ref, oband_ref,
    image_ref, mine_ref, theirs_ref,
    bh_ref, bl_ref, lh_ref, ll_ref, rh_ref, rl_ref, vh_ref, vl_ref, y_ref, sem,
):
    own, cols = own_ref.shape
    windows = band_ref.shape[0]
    frame = y_ref.shape[0]
    high = LOW + own
    chunk = 256

    def split_band(g, carry):
        bh_ref[g], bl_ref[g] = halves(band_ref[g])
        return carry

    lax.fori_loop(0, windows, split_band, 0)
    for ref in (vh_ref, vl_ref):
        for n, width in enumerate((EDGE, HALO)):
            ref[n, : LOW - width] = jnp.zeros((LOW - width, cols), BF16)
            ref[n, high + width :] = jnp.zeros((frame - high - width, cols), BF16)

    def put(n, at, value):
        vh_ref[n, at, :], vl_ref[n, at, :] = halves(value)

    def sides(left_ref, right_ref, lband_ref, rband_ref):
        put(0, pl.ds(LOW - EDGE, EDGE), left_ref[...])
        put(0, pl.ds(high, EDGE), right_ref[...])
        lh_ref[...], ll_ref[...] = halves(lband_ref[...])
        rh_ref[...], rl_ref[...] = halves(rband_ref[...])

    pl.when(valid_ref[2] == 0)(lambda: sides(outer_ref, inner_ref, oband_ref, iband_ref))
    pl.when(valid_ref[2] != 0)(lambda: sides(inner_ref, outer_ref, iband_ref, oband_ref))

    def split_own(i, carry):
        at = pl.multiple_of(i * chunk, chunk)
        put(0, pl.ds(LOW + at, chunk), own_ref[pl.ds(at, chunk), :])
        return carry

    lax.fori_loop(0, own // chunk, split_own, 0)

    def clear(i, carry):
        y_ref[pl.ds(pl.multiple_of(i * 64, 64), 64), :] = jnp.zeros((64, cols), F32)
        return carry

    tn = ((0,), (0,))

    def keep_moment(j, value):
        here = valid_ref[2] == j // ITERS
        for ref, chosen in ((mine_ref, here), (theirs_ref, jnp.logical_not(here))):
            @pl.when(chosen)
            def _(ref=ref):
                for c in range(cols // 128):
                    ref[j % ITERS, c] = value[:, c * 128 : (c + 1) * 128]

    def power(n, carry):
        now = n % 2
        then = 1 - now
        lax.fori_loop(0, frame // 64, clear, 0)

        def window(i, carry):
            values = []
            for m in range(3):
                at = pl.multiple_of(HALO + (3 * i + m) * STEP, 64)
                xh = vh_ref[now, pl.ds(at, WIN), :]
                xl = vl_ref[now, pl.ds(at, WIN), :]
                values.append((at, dot3(bh_ref[3 * i + m], bl_ref[3 * i + m], xh, xl)))
            for at, value in values:
                y_ref[pl.ds(at, WIN), :] += value
            return carry

        lax.fori_loop(0, windows // 3, window, 0)

        values = []
        for h_ref, l_ref, lo, rows, out, at in (
            (lh_ref, ll_ref, 0, 128, HALO, 0),
            (lh_ref, ll_ref, 128, 192, HALO + 64, HALO + 64),
            (rh_ref, rl_ref, 0, 256, own + HALO, own + HALO),
            (rh_ref, rl_ref, 256, 64, own + HALO + STEP, own + HALO + STEP),
        ):
            value = dot3(
                h_ref[lo : lo + rows], l_ref[lo : lo + rows],
                vh_ref[now, at : at + WIN], vl_ref[now, at : at + WIN],
            )
            values.append((out, rows, value))
        for out, rows, value in values:
            y_ref[out : out + rows] += value

        put(then, pl.ds(HALO, HALO), jnp.where(valid_ref[0] > 0, y_ref[HALO:LOW], 0.0))
        put(then, pl.ds(high, HALO), jnp.where(valid_ref[1] > 0, y_ref[high : high + HALO], 0.0))

        def split(i, carry):
            at = pl.multiple_of(i * chunk, chunk)
            value = y_ref[pl.ds(LOW + at, chunk), :]
            put(then, pl.ds(LOW + at, chunk), value)
            return carry

        copy = pltpu.make_async_copy(
            y_ref.at[pl.ds(LOW, own)], image_ref.at[jnp.minimum(n, ITERS - 2)], sem
        )
        pl.when(n + 1 < ITERS)(copy.start)
        lax.fori_loop(0, own // chunk, split, 0)

        xh, xl = vh_ref[now, LOW:high], vl_ref[now, LOW:high]
        zh, zl = vh_ref[then, LOW:high], vl_ref[then, LOW:high]
        by_high = dot(xh, jnp.concatenate([xh, xl, zh, zl], axis=1), tn)
        by_low = dot(xl, zh, tn)
        cross = by_high[:, cols : 2 * cols]
        keep_moment(2 * n, by_high[:, :cols] + (cross + cross.T))
        keep_moment(2 * n + 1, by_high[:, 2 * cols : 3 * cols] + (by_high[:, 3 * cols :] + by_low))

        pl.when(n + 1 < ITERS)(copy.wait)

        @pl.when(n == 0)
        def _():
            for ref in (vh_ref, vl_ref):
                ref[0, : HALO] = jnp.zeros((HALO, cols), BF16)
                ref[0, high + HALO :] = jnp.zeros((frame - high - HALO, cols), BF16)

        return carry

    lax.fori_loop(0, ITERS, power, 0)


def powers(vector, inner, outer, valid, bands):
    band, inner_band, outer_band = bands
    own, cols = vector.shape
    frame = own + 2 * LOW + 64
    half = jax.ShapeDtypeStruct((ITERS, cols // 128, cols, 128), F32)
    wide = pltpu.VMEM((2, frame, cols), BF16)
    edge = pltpu.VMEM(inner_band.shape, BF16)
    return pl.pallas_call(
        powers_kernel,
        out_shape=(pltpu.HBM((ITERS - 1, own, cols), F32), half, half),
        in_specs=[pl.BlockSpec(memory_space=pltpu.SMEM)] + in_vmem(6),
        out_specs=(pl.BlockSpec(memory_space=pltpu.HBM), *in_vmem(2)),
        compiler_params=pltpu.CompilerParams(vmem_limit_bytes=32 << 20),
        scratch_shapes=[pltpu.VMEM(band.shape, BF16)] * 2 + [edge] * 4 + [wide] * 2
        + [pltpu.VMEM((frame, cols), F32), pltpu.SemaphoreType.DMA],
        name="powers",
    )(valid, vector, inner, outer, band, inner_band, outer_band)


def diagonals(matrix):
    size = matrix.shape[0]
    on = jnp.where(iota((size, size), 0) == iota((size, size), 1), matrix, 0.0)
    return jnp.sum(on, axis=0, keepdims=True), jnp.sum(on, axis=1, keepdims=True)


def split_dot(a, b):
    return dot3(*halves(a), *halves(b))


def inverse_spd(matrix, mul, limit):
    size = matrix.shape[0]
    unit = (iota((size, size), 0) == iota((size, size), 1)).astype(F32)
    along, down = diagonals(matrix)
    scale = lax.rsqrt(along) * lax.rsqrt(down)
    scaled = matrix * scale
    norm = jnp.max(jnp.sum(jnp.abs(scaled), axis=1, keepdims=True))
    factor = jnp.where(norm < 1.9, 1.0, 1.9 / norm)
    rest = unit - factor * scaled

    def going(state):
        k, worst, _, _ = state
        return (k < 40) & (size * worst * worst > limit)

    def step(state):
        k, _, total, power = state
        both = mul(jnp.concatenate([total, power], axis=0), power)
        total = total + both[:size]
        power = both[size:]
        return k + 1, jnp.max(jnp.abs(power)), total, power

    total = factor * (unit + rest)
    power = mul(rest, rest)
    rounds, worst, total, power = lax.while_loop(
        going, step, (1, jnp.max(jnp.abs(power)), total, power)
    )
    worst = size * worst * worst
    total = total + mul(total, power)
    return total * scale, worst, rounds


def ratio(left, whole):
    return jnp.min(diagonals(left)[0] / diagonals(whole)[0])


def galerkin_kernel(core_ref, mine_ref, theirs_ref, basis_ref, out_ref, rows_ref, good_ref, mom_ref):
    parts = mine_ref.shape[1]

    def unpack(source_ref, start):
        for n in range(ITERS):
            mom_ref[start + n] = jnp.concatenate([source_ref[n, c] for c in range(parts)], axis=1)

    @pl.when(core_ref[0] == 0)
    def _():
        unpack(mine_ref, 0)
        unpack(theirs_ref, ITERS)

    @pl.when(core_ref[0] != 0)
    def _():
        unpack(theirs_ref, 0)
        unpack(mine_ref, ITERS)

    m = [mom_ref[n] for n in range(2 * ITERS)]
    m = [x if n % 2 == 0 else 0.5 * (x + x.T) for n, x in enumerate(m)]
    h = [m[n + 1] + SHIFT * m[n] for n in range(2 * ITERS - 1)]
    size = m[0].shape[0]

    def right_of(inverse, *targets):
        wide = split_dot(inverse, jnp.concatenate(targets, axis=1))
        return [wide[:, n * size : (n + 1) * size] for n in range(len(targets))]

    s0, w0, k0 = inverse_spd(h[0], split_dot, CLOSE)
    z01, z02, z0m = right_of(s0, h[1], h[2], m[0])
    upper = split_dot(h[1], jnp.concatenate([z01, z02, z0m], axis=1))
    lower = split_dot(h[2], jnp.concatenate([z02, z0m], axis=1))
    first = h[2] - upper[:, :size]
    cross = h[3] - upper[:, size : 2 * size]
    m1 = m[1] - upper[:, 2 * size :]
    last = h[4] - lower[:, :size]
    m2 = m[2] - lower[:, size:]
    first = 0.5 * (first + first.T)
    s1, w1, k1 = inverse_spd(first, split_dot, CLOSE)
    z12, z1m = right_of(s1, cross, m1)
    lower = split_dot(cross.T, jnp.concatenate([z12, z1m], axis=1))
    rest = last - lower[:, :size]
    rest = 0.5 * (rest + rest.T)
    m2 = m2 - lower[:, size:]
    s2, w2, k2 = inverse_spd(rest, split_dot, CLOSE)
    y2 = split_dot(s2, m2)
    y1 = z1m - split_dot(z12, y2)
    y0 = z0m - split_dot(jnp.concatenate([z01, z02], axis=1), jnp.concatenate([y1, y2], axis=0))
    out_ref[:size] = y0
    out_ref[size : 2 * size] = y1
    out_ref[2 * size :] = y2
    wide = out_ref.shape[0]
    yh, yl = halves(out_ref[...])
    for k in range(3):
        part = dot3(*halves(basis_ref[:, k * wide : (k + 1) * wide]), yh, yl)
        rows_ref[:, k * size : (k + 1) * size] = part
    share = jnp.minimum(ratio(first, h[2]), ratio(rest, h[4]))
    rounds = jnp.maximum(k0, jnp.maximum(k1, k2))
    worst = jnp.maximum(w0, jnp.maximum(w1, w2))
    good_ref[0] = jnp.where((share > GUARD) & (worst <= CLOSE) & (rounds <= ROUNDS), 1, 0)


def galerkin(core, mine, theirs, basis_rows):
    size = mine.shape[2]
    slots, wide = basis_rows.shape
    smem = pl.BlockSpec(memory_space=pltpu.SMEM)
    return pl.pallas_call(
        galerkin_kernel,
        out_shape=(
            jax.ShapeDtypeStruct((ITERS * size, size), F32),
            jax.ShapeDtypeStruct((slots, wide // ITERS), F32),
            jax.ShapeDtypeStruct((1,), jnp.int32),
        ),
        in_specs=[smem] + in_vmem(3),
        out_specs=(*in_vmem(2), smem),
        scratch_shapes=[pltpu.VMEM((2 * ITERS, size, size), F32)],
        compiler_params=pltpu.CompilerParams(vmem_limit_bytes=32 << 20),
        name="galerkin",
    )(core, mine, theirs, basis_rows)


def solve_kernel(matrix_ref, target_ref, out_ref):
    matrix = matrix_ref[...]
    matrix = 0.5 * (matrix + matrix.T)
    inverse, _, _ = inverse_spd(matrix, full_dot, 1e-9)
    guess = full_dot(inverse, target_ref[...])
    out_ref[...] = guess + full_dot(inverse, target_ref[...] - full_dot(matrix, guess))


def solve(matrix, target):
    return pl.pallas_call(
        solve_kernel,
        out_shape=jax.ShapeDtypeStruct(target.shape, F32),
        in_specs=in_vmem(2),
        out_specs=in_vmem(1)[0],
        name="solve",
    )(matrix, target)


def total_of(mine, theirs):
    shape = mine.shape
    chips = lax.axis_size(CHIPS)
    other = [(0, 1), (1, 0)]
    pair = mine + lax.ppermute(theirs, "core", other)
    pair = pair.reshape(chips, -1, 128)
    arrived = lax.all_to_all(pair, CHIPS, 0, 0, tiled=True)
    own = jnp.broadcast_to(arrived.sum(axis=0)[None], pair.shape)
    gathered = lax.all_to_all(own, CHIPS, 0, 0, tiled=True)
    gathered = gathered.reshape(shape)
    return gathered, lax.ppermute(gathered, "core", other)


def swap_sides(inner, outer):
    count = lax.axis_size(AXES)
    across = [(i, i + 1) for i in range(1, count - 1, 2)]
    return (
        lax.ppermute(inner, "core", [(0, 1), (1, 0)]),
        lax.ppermute(outer, AXES, across + [(b, a) for a, b in across]),
    )


def halo_of(vector):
    first = lax.axis_index("core") == 0
    head, tail = vector[:EDGE], vector[-EDGE:]
    return swap_sides(jnp.where(first, tail, head), jnp.where(first, head, tail))


def plain_cg(right_side, valid, bands):
    def times(a, b):
        return jnp.dot(a, b, preferred_element_type=F32, precision=lax.Precision.HIGHEST)

    def gram_of(parts):
        return jnp.concatenate([parts[0], parts[1]], axis=1)

    def step(k, state):
        answer, residual, direction, gram = state
        on_direction = k % 2 == 0
        vector = jnp.where(on_direction, direction, residual)
        image, mine, theirs = powers(vector, *halo_of(vector), valid, bands)
        low, high = total_of(mine, theirs)
        low = jnp.where(valid[2] == 0, low, high)
        square = gram_of(low[0])
        gram = jnp.where(k == 0, square, gram)
        dir_gram = gram_of(low[1]) + SHIFT * square
        factor = solve(
            jnp.where(on_direction, dir_gram, gram), jnp.where(on_direction, gram, square)
        )
        along = times(direction, factor)
        applied = times(image[0] + SHIFT * vector, factor)
        answer = jnp.where(on_direction, answer + along, answer)
        direction = jnp.where(on_direction, direction, residual + along)
        residual = jnp.where(on_direction, residual - applied, residual)
        return answer, residual, direction, jnp.where(on_direction, gram, square)

    state = (jnp.zeros_like(right_side), right_side, right_side, jnp.zeros((right_side.shape[1],) * 2, F32))
    return lax.fori_loop(0, 2 * ITERS - 1, step, state)[0]


def loads_kernel(nodes_ref, load_ref, high_ref, low_ref):
    groups, pairs = nodes_ref.shape
    slots = 8
    support = pairs // slots
    blocks = high_ref.shape[1] // 128
    own_lane = iota((slots, pairs), 1) // support == iota((slots, pairs), 0)
    row = iota((128, pairs), 0)

    def half_group(g):
        nodes = nodes_ref[pl.ds(g, 1), :]
        hot = jnp.where(row == nodes % 128, 1.0, 0.0).astype(BF16)
        block = jnp.broadcast_to(nodes // 128, (slots, pairs))
        terms = []
        for k in range(3):
            spread = jnp.where(own_lane, load_ref[k, pl.ds(g, 1), :], 0.0)
            high = spread.astype(BF16).astype(F32)
            terms.append((high, spread - high))
        rows = []
        for c in range(blocks):
            hit = block == c
            for high, low in terms:
                rows.append(
                    jnp.concatenate([jnp.where(hit, high, 0.0), jnp.where(hit, low, 0.0)], axis=1)
                )
        left = jnp.concatenate(rows, axis=0).astype(BF16)
        return dot(left, jnp.concatenate([hot, hot], axis=1), ((1,), (1,)))

    def group(g, carry):
        first = half_group(2 * g)
        second = half_group(2 * g + 1)
        total = groups * slots
        for c in range(blocks):
            for k in range(3):
                at = (c * 3 + k) * slots
                value = jnp.concatenate([first[at : at + slots], second[at : at + slots]], axis=0)
                high, low = halves(value)
                to = pl.multiple_of(k * total + g * 2 * slots, 16)
                high_ref[pl.ds(to, 2 * slots), c * 128 : (c + 1) * 128] = high
                low_ref[pl.ds(to, 2 * slots), c * 128 : (c + 1) * 128] = low
        return carry

    lax.fori_loop(0, groups // 2, group, 0)


def load_matrix(slot_nodes, slot_load, rows):
    support, slots = slot_nodes.shape
    groups = slots * support // 128
    nodes = slot_nodes.T.reshape(groups, 128)
    loads = slot_load.reshape(support, slots, 3).transpose(2, 1, 0).reshape(3, groups, 128)
    out = jax.ShapeDtypeStruct((3 * slots, rows), BF16)
    return pl.pallas_call(
        loads_kernel,
        out_shape=(out, out),
        in_specs=in_vmem(2),
        out_specs=tuple(in_vmem(2)),
        compiler_params=pltpu.CompilerParams(vmem_limit_bytes=20 << 20),
        name="loads",
    )(nodes, loads)


CHUNK = 512


def basis_kernel(*refs):
    *vector_refs, wh_ref, wl_ref, out_ref = refs

    @pl.when(pl.program_id(0) == 0)
    def _():
        out_ref[...] = jnp.zeros_like(out_ref)

    slots = out_ref.shape[0]
    cols = vector_refs[0].shape[1]
    count = len(vector_refs)
    for n, ref in enumerate(vector_refs):
        full = dot3(wh_ref[...], wl_ref[...], *halves(ref[...]))
        for k in range(3):
            at = (k * count + n) * cols
            out_ref[:, at : at + cols] += full[k * slots : (k + 1) * slots]


def basis(vectors, weights):
    rows, cols = vectors[0][0].shape[-2:]
    loads = weights[0].shape[0]
    weight = pl.BlockSpec((loads, CHUNK), lambda i: (0, i))
    out = (loads // 3, 3 * len(vectors) * cols)
    return pl.pallas_call(
        basis_kernel,
        grid=(rows // CHUNK,),
        out_shape=jax.ShapeDtypeStruct(out, F32),
        in_specs=[spec for _, spec in vectors] + [weight, weight],
        out_specs=pl.BlockSpec(out, lambda i: (0, 0)),
        compiler_params=pltpu.CompilerParams(vmem_limit_bytes=28 << 20),
        name="basis",
    )(*[vector for vector, _ in vectors], *weights)


def in_chunks(vector, n=None):
    cols = vector.shape[-1]
    if n is None:
        return vector, pl.BlockSpec((CHUNK, cols), lambda i: (i, 0))
    placed = pltpu.with_memory_space_constraint(vector, pltpu.HBM)
    return placed, pl.BlockSpec((None, CHUNK, cols), lambda i: (n, i, 0))


def to_owner(rows):
    slots, wide = rows.shape
    count = lax.axis_size(AXES)
    return lax.all_to_all(rows.reshape(count, slots // count, wide), AXES, 0, 0, tiled=True)


def combine_kernel(k0_ref, k1_ref, k2_ref, c_ref, x_ref, ch_ref, cl_ref):
    size = c_ref.shape[1]

    @pl.when(pl.program_id(0) == 0)
    def _():
        ch_ref[...], cl_ref[...] = halves(c_ref[...])

    total = jnp.zeros(x_ref.shape, F32)
    for n, ref in enumerate((k0_ref, k1_ref, k2_ref)):
        ah, al = halves(ref[...])
        at = n * size
        total = total + dot3(ah, al, ch_ref[at : at + size], cl_ref[at : at + size])
    x_ref[...] = total


def combine(vectors, coef):
    rows, cols = vectors[0][0].shape[-2:]
    return pl.pallas_call(
        combine_kernel,
        grid=(rows // CHUNK,),
        out_shape=jax.ShapeDtypeStruct((rows, cols), F32),
        in_specs=[spec for _, spec in vectors] + [pl.BlockSpec(coef.shape, lambda i: (0, 0))],
        out_specs=pl.BlockSpec((CHUNK, cols), lambda i: (i, 0)),
        scratch_shapes=[pltpu.VMEM(coef.shape, BF16)] * 2,
        compiler_params=pltpu.CompilerParams(vmem_limit_bytes=20 << 20),
        name="combine",
    )(*[vector for vector, _ in vectors], coef)


def lead_kernel(slot_ref, received_ref, out_ref):
    _, places, wide = received_ref.shape
    _, dipoles, cols = out_ref.shape
    together = 8

    def pick(i, carry):
        for n in range(together):
            slot = slot_ref[i * together + n]
            row = received_ref[slot // places, pl.ds(slot % places, 1), :]
            for k in range(wide // cols):
                out_ref[k, pl.ds(i * together + n, 1), :] = row[:, k * cols : (k + 1) * cols]
        return carry

    lax.fori_loop(0, dipoles // together, pick, 0)


def lead(received, dipole_slot):
    out = (3, dipole_slot.shape[0], received.shape[2] // 3)
    return pl.pallas_call(
        lead_kernel,
        out_shape=jax.ShapeDtypeStruct(out, F32),
        in_specs=[pl.BlockSpec(memory_space=pltpu.SMEM)] + in_vmem(1),
        out_specs=in_vmem(1)[0],
        compiler_params=pltpu.CompilerParams(vmem_limit_bytes=20 << 20),
        name="lead",
    )(dipole_slot, received)


def one_device(right_side, tile_stiff, tile_nodes, node_shift, slot_nodes, slot_load, dipole_slot):
    count = lax.axis_size(AXES)
    index = lax.axis_index(AXES)
    core = lax.axis_index("core")
    valid = jnp.stack([index > 0, index < count - 1, core]).astype(jnp.int32)
    inner, outer = halo_of(right_side)
    band, inner_band, outer_band = assemble(core[None], tile_stiff, tile_nodes, node_shift)
    bands = (band, *swap_sides(inner_band, outer_band))
    weights = load_matrix(slot_nodes, slot_load, right_side.shape[0])
    images, mine, theirs = powers(right_side, inner, outer, valid, bands)
    vectors = [in_chunks(right_side), in_chunks(images, 0), in_chunks(images, 1)]
    basis_rows = basis(vectors, weights)
    mine, theirs = total_of(mine, theirs)
    coef, rows, good = galerkin(core[None], mine, theirs, basis_rows)
    received = to_owner(rows)
    answer = combine(vectors, coef)
    leadfield = lead(received, dipole_slot)

    def exactly(_):
        exact = plain_cg(right_side, valid, bands)
        received = to_owner(basis([in_chunks(exact)], weights))
        return jnp.ones((), jnp.int32), exact, lead(received, dipole_slot)

    state = lax.while_loop(lambda state: state[0] == 0, exactly, (good[0], answer, leadfield))
    return state[1:]


def solution(mesh):
    rows, depth = mesh.devices.shape
    outer = 4 if rows % 4 == 0 else 1
    flat = Mesh(mesh.devices.reshape(outer, rows // outer, depth // 2, 2), AXES)
    return jax.shard_map(
        one_device,
        mesh=flat,
        in_specs=(
            P(AXES, None),
            P(AXES, None, None),
            P(AXES, None),
            P(AXES),
            P(None, AXES),
            P(None, AXES),
            P(AXES),
        ),
        out_specs=(P(AXES, None), P(None, AXES, None)),
        check_vma=False,
    )
```

```python
import jax
import jax.numpy as jnp
from jax import lax
from jax.experimental import pallas as pl
from jax.experimental.pallas import tpu as pltpu
from jax.sharding import Mesh
from jax.sharding import PartitionSpec as P


F32 = jnp.float32
BF16 = jnp.bfloat16
AXES = ("row", "column", "depth", "core")
CHIPS = ("row", "column", "depth")
ITERS = 3
HALO = 128
REACH = 64
WIN = 256
STEP = WIN - REACH
SHIFT = 4.5
ROUNDS = 8
CLOSE = 1e-6
GUARD = 0.01
SMALL = 128
SPAN = 80
BATCH = 8
TOGETHER = 2
EDGE = 192


def dot(a, b, dims=((1,), (0,))):
    return lax.dot_general(a, b, (dims, ((), ())), preferred_element_type=F32)


def halves(x):
    high = x.astype(BF16)
    return high, (x - high.astype(F32)).astype(BF16)


def dot3(ah, al, bh, bl, dims=((1,), (0,))):
    return dot(ah, bh, dims) + (dot(ah, bl, dims) + dot(al, bh, dims))


def full_dot(a, b):
    return lax.dot_general(
        a, b, (((1,), (0,)), ((), ())), preferred_element_type=F32, precision=lax.Precision.HIGHEST
    )


def iota(shape, dim):
    return lax.broadcasted_iota(jnp.int32, shape, dim)


def in_vmem(count):
    return [pl.BlockSpec(memory_space=pltpu.VMEM)] * count


def assemble_kernel(
    core_ref, group_ref, first_ref, stiff_ref, place_ref, offset_ref, diag_ref,
    out_ref, inner_ref, outer_ref,
    rows_ref, small_ref, block_ref, lane_ref, wait_ref,
):
    slots, _, tiles = stiff_ref.shape
    windows = out_ref.shape[0]
    lanes = BATCH * slots
    one = lambda mask: jnp.where(mask, 1.0, 0.0).astype(BF16)
    block_ref[...] = one(iota((lanes, lanes), 0) % BATCH == iota((lanes, lanes), 1) // slots)
    for t in range(BATCH):
        lane_ref[t * SPAN : (t + 1) * SPAN] = one(iota((SPAN, lanes), 1) % BATCH == t)

    def clear(g, carry):
        small_ref[g] = jnp.zeros((SMALL, SMALL), F32)
        return carry

    lax.fori_loop(0, small_ref.shape[0], clear, 0)

    def turn(i, carry):
        for n in range(4):
            plane = stiff_ref[4 * i + n]
            rows_ref[4 * i + n] = jnp.concatenate([plane] * (128 // slots), axis=0).T
        return carry

    lax.fori_loop(0, slots // 4, turn, 0)

    row_in_window = iota((SMALL, lanes), 0)
    row_in_span = iota((SPAN, lanes), 0)

    def first_side(b):
        base = pl.multiple_of(b * BATCH, BATCH)
        parts = halves(rows_ref[:, pl.ds(base, BATCH), :].reshape(lanes, 128))
        block = block_ref[...]
        wide = [jnp.concatenate([part] * (lanes // 128), axis=1) * block for part in parts]
        hot = one(row_in_window == place_ref[pl.ds(b, 1), :])
        return jnp.concatenate(wide, axis=0), hot

    def second_side(b):
        match = one(row_in_span == offset_ref[pl.ds(b, 1), :])
        return jnp.concatenate([match] * BATCH, axis=0) * lane_ref[...]

    def compute(i):
        batches = [TOGETHER * i + n for n in range(TOGETHER)]
        sides = [first_side(b) for b in batches]
        both = [dot(wide, hot, ((1,), (1,))) for wide, hot in sides]
        picks = [second_side(b) for b in batches]
        rights = [jnp.concatenate(halves(x[:lanes] + x[lanes:]), axis=1) for x in both]
        full = [dot(pick, right) for pick, right in zip(picks, rights)]
        return [x[:, :SMALL] + x[:, SMALL:] for x in full]

    def hold(full):
        for n in range(TOGETHER):
            wait_ref[n] = full[n]

    def add_up(i):
        for n in range(TOGETHER):
            for t in range(BATCH):
                tile = (TOGETHER * i + n) * BATCH + t
                r = pl.multiple_of(first_ref[tile], 16)
                small_ref[group_ref[tile], pl.ds(r, SPAN), :] += wait_ref[n, t * SPAN : (t + 1) * SPAN]

    rounds = tiles // (BATCH * TOGETHER)
    hold(compute(0))

    def batch(i, carry):
        full = compute(i)
        add_up(i - 1)
        hold(full)
        return carry

    lax.fori_loop(1, rounds, batch, 0)
    add_up(rounds - 1)

    eye = iota((WIN, WIN), 0) == iota((WIN, WIN), 1)
    gap = jnp.zeros((SMALL, REACH), F32)

    def gather(g, carry):
        out_ref[g] = jnp.where(eye, diag_ref[pl.ds(g, 1), :], 0.0)
        out_ref[g, :SMALL, :SMALL] += small_ref[3 * g]
        middle = jnp.concatenate([gap, small_ref[3 * g + 1], gap], axis=1)
        out_ref[g, REACH : REACH + SMALL, :] += middle
        out_ref[g, SMALL:, SMALL:] += small_ref[3 * g + 2]
        return carry

    lax.fori_loop(0, windows, gather, 0)

    def edges(up_ref, down_ref):
        up_ref[:128] = out_ref[windows - 2, 128:]
        up_ref[128:] = out_ref[windows - 1, :192]
        down_ref[:WIN] = out_ref[0]
        down_ref[WIN:] = out_ref[1, :64]

    pl.when(core_ref[0] == 0)(lambda: edges(inner_ref, outer_ref))
    pl.when(core_ref[0] != 0)(lambda: edges(outer_ref, inner_ref))


def assemble(core, tile_stiff, tile_nodes, node_shift):
    tiles, slots = tile_nodes.shape
    ext = node_shift.shape[0] + 2 * HALO
    windows = ext // STEP
    smalls = ext // REACH
    lowest = jnp.min(tile_nodes, axis=1)
    group = jnp.minimum(lowest // REACH, smalls - 1)
    first = jnp.minimum((lowest - group * REACH) // 16 * 16, REACH - 16)
    place = jnp.where(tile_nodes == ext, -1, tile_nodes - group[:, None] * REACH)
    offset = jnp.where(tile_nodes == ext, -1, place - first[:, None])
    diag = jnp.pad(node_shift - SHIFT, (HALO, HALO)).reshape(windows, STEP)
    diag = jnp.pad(diag, ((0, 0), (0, WIN - STEP)))
    lanes = BATCH * slots
    smem = pl.BlockSpec(memory_space=pltpu.SMEM)
    edge = jax.ShapeDtypeStruct((320, WIN), F32)
    return pl.pallas_call(
        assemble_kernel,
        out_shape=(jax.ShapeDtypeStruct((windows, WIN, WIN), F32), edge, edge),
        in_specs=[smem] * 3 + in_vmem(4),
        out_specs=tuple(in_vmem(3)),
        scratch_shapes=[
            pltpu.VMEM((slots, tiles, 128), F32),
            pltpu.VMEM((smalls, SMALL, SMALL), F32),
            pltpu.VMEM((lanes, lanes), BF16),
            pltpu.VMEM((BATCH * SPAN, lanes), BF16),
            pltpu.VMEM((TOGETHER, BATCH * SPAN, SMALL), F32),
        ],
        compiler_params=pltpu.CompilerParams(vmem_limit_bytes=28 << 20),
        name="assemble",
    )(
        core,
        group,
        first,
        jnp.transpose(tile_stiff, (1, 2, 0)),
        place.reshape(-1, lanes),
        offset.reshape(-1, BATCH, slots).transpose(0, 2, 1).reshape(-1, lanes),
        diag,
    )


LOW = 2 * HALO
PACK = 320


def powers_kernel(
    valid_ref, own_ref, inner_ref, outer_ref, band_ref, iband_ref, oband_ref,
    image_ref, mine_ref, theirs_ref,
    bh_ref, bl_ref, lh_ref, ll_ref, rh_ref, rl_ref, vh_ref, vl_ref, y_ref, sem,
):
    own, cols = own_ref.shape
    windows = band_ref.shape[0]
    frame = y_ref.shape[0]
    high = LOW + own
    chunk = 256

    def split_band(g, carry):
        bh_ref[g], bl_ref[g] = halves(band_ref[g])
        return carry

    lax.fori_loop(0, windows, split_band, 0)
    for ref in (vh_ref, vl_ref):
        for n, width in enumerate((EDGE, HALO)):
            ref[n, : LOW - width] = jnp.zeros((LOW - width, cols), BF16)
            ref[n, high + width :] = jnp.zeros((frame - high - width, cols), BF16)

    def put(n, at, value):
        vh_ref[n, at, :], vl_ref[n, at, :] = halves(value)

    def sides(left_ref, right_ref, lband_ref, rband_ref):
        put(0, pl.ds(LOW - EDGE, EDGE), left_ref[...])
        put(0, pl.ds(high, EDGE), right_ref[...])
        lh_ref[...], ll_ref[...] = halves(lband_ref[...])
        rh_ref[...], rl_ref[...] = halves(rband_ref[...])

    pl.when(valid_ref[2] == 0)(lambda: sides(outer_ref, inner_ref, oband_ref, iband_ref))
    pl.when(valid_ref[2] != 0)(lambda: sides(inner_ref, outer_ref, iband_ref, oband_ref))

    def split_own(i, carry):
        at = pl.multiple_of(i * chunk, chunk)
        put(0, pl.ds(LOW + at, chunk), own_ref[pl.ds(at, chunk), :])
        return carry

    lax.fori_loop(0, own // chunk, split_own, 0)

    def clear(i, carry):
        y_ref[pl.ds(pl.multiple_of(i * 64, 64), 64), :] = jnp.zeros((64, cols), F32)
        return carry

    tn = ((0,), (0,))

    def keep_moment(j, value):
        here = valid_ref[2] == j // ITERS
        low, up = value[:, :128], value[:, 128:]
        mixed = jnp.where(
            iota((64, 128), 1) < 64, pltpu.roll(low[64:128], 64, 1), up[192:]
        )
        for ref, chosen in ((mine_ref, here), (theirs_ref, jnp.logical_not(here))):
            @pl.when(chosen)
            def _(ref=ref):
                at = pl.multiple_of(j % ITERS * PACK, 64)
                ref[pl.ds(at, 64), :] = low[:64]
                ref[pl.ds(at + 64, 192), :] = up[:192]
                ref[pl.ds(at + 256, 64), :] = mixed

    for ref in (mine_ref, theirs_ref):
        ref[ITERS * PACK :] = jnp.zeros((ref.shape[0] - ITERS * PACK, 128), F32)

    def power(n, carry):
        now = n % 2
        then = 1 - now
        lax.fori_loop(0, frame // 64, clear, 0)

        def window(i, carry):
            values = []
            for m in range(3):
                at = pl.multiple_of(HALO + (3 * i + m) * STEP, 64)
                xh = vh_ref[now, pl.ds(at, WIN), :]
                xl = vl_ref[now, pl.ds(at, WIN), :]
                values.append((at, dot3(bh_ref[3 * i + m], bl_ref[3 * i + m], xh, xl)))
            for at, value in values:
                y_ref[pl.ds(at, WIN), :] += value
            return carry

        lax.fori_loop(0, windows // 3, window, 0)

        values = []
        for h_ref, l_ref, lo, rows, out, at in (
            (lh_ref, ll_ref, 0, 128, HALO, 0),
            (lh_ref, ll_ref, 128, 192, HALO + 64, HALO + 64),
            (rh_ref, rl_ref, 0, 256, own + HALO, own + HALO),
            (rh_ref, rl_ref, 256, 64, own + HALO + STEP, own + HALO + STEP),
        ):
            value = dot3(
                h_ref[lo : lo + rows], l_ref[lo : lo + rows],
                vh_ref[now, at : at + WIN], vl_ref[now, at : at + WIN],
            )
            values.append((out, rows, value))
        for out, rows, value in values:
            y_ref[out : out + rows] += value

        put(then, pl.ds(HALO, HALO), jnp.where(valid_ref[0] > 0, y_ref[HALO:LOW], 0.0))
        put(then, pl.ds(high, HALO), jnp.where(valid_ref[1] > 0, y_ref[high : high + HALO], 0.0))

        def split(i, carry):
            at = pl.multiple_of(i * chunk, chunk)
            value = y_ref[pl.ds(LOW + at, chunk), :]
            put(then, pl.ds(LOW + at, chunk), value)
            return carry

        copy = pltpu.make_async_copy(
            y_ref.at[pl.ds(LOW, own)], image_ref.at[jnp.minimum(n, ITERS - 2)], sem
        )
        pl.when(n + 1 < ITERS)(copy.start)
        lax.fori_loop(0, own // chunk, split, 0)

        xh, xl = vh_ref[now, LOW:high], vl_ref[now, LOW:high]
        zh, zl = vh_ref[then, LOW:high], vl_ref[then, LOW:high]
        by_high = dot(xh, jnp.concatenate([xh, xl, zh, zl], axis=1), tn)
        by_low = dot(xl, zh, tn)
        cross = by_high[:, cols : 2 * cols]
        keep_moment(2 * n, by_high[:, :cols] + (cross + cross.T))
        keep_moment(2 * n + 1, by_high[:, 2 * cols : 3 * cols] + (by_high[:, 3 * cols :] + by_low))

        pl.when(n + 1 < ITERS)(copy.wait)

        @pl.when(n == 0)
        def _():
            for ref in (vh_ref, vl_ref):
                ref[0, : HALO] = jnp.zeros((HALO, cols), BF16)
                ref[0, high + HALO :] = jnp.zeros((frame - high - HALO, cols), BF16)

        return carry

    lax.fori_loop(0, ITERS, power, 0)


def powers(vector, inner, outer, valid, bands):
    band, inner_band, outer_band = bands
    own, cols = vector.shape
    frame = own + 2 * LOW + 64
    half = jax.ShapeDtypeStruct((1024, 128), F32)
    wide = pltpu.VMEM((2, frame, cols), BF16)
    edge = pltpu.VMEM(inner_band.shape, BF16)
    return pl.pallas_call(
        powers_kernel,
        out_shape=(pltpu.HBM((ITERS - 1, own, cols), F32), half, half),
        in_specs=[pl.BlockSpec(memory_space=pltpu.SMEM)] + in_vmem(6),
        out_specs=(pl.BlockSpec(memory_space=pltpu.HBM), *in_vmem(2)),
        compiler_params=pltpu.CompilerParams(vmem_limit_bytes=32 << 20),
        scratch_shapes=[pltpu.VMEM(band.shape, BF16)] * 2 + [edge] * 4 + [wide] * 2
        + [pltpu.VMEM((frame, cols), F32), pltpu.SemaphoreType.DMA],
        name="powers",
    )(valid, vector, inner, outer, band, inner_band, outer_band)


def diagonals(matrix):
    size = matrix.shape[0]
    on = jnp.where(iota((size, size), 0) == iota((size, size), 1), matrix, 0.0)
    return jnp.sum(on, axis=0, keepdims=True), jnp.sum(on, axis=1, keepdims=True)


def split_dot(a, b):
    return dot3(*halves(a), *halves(b))


def inverse_spd(matrix, mul, limit):
    size = matrix.shape[0]
    unit = (iota((size, size), 0) == iota((size, size), 1)).astype(F32)
    along, down = diagonals(matrix)
    scale = lax.rsqrt(along) * lax.rsqrt(down)
    scaled = matrix * scale
    norm = jnp.max(jnp.sum(jnp.abs(scaled), axis=1, keepdims=True))
    factor = jnp.where(norm < 1.9, 1.0, 1.9 / norm)
    rest = unit - factor * scaled

    def going(state):
        k, worst, _, _ = state
        return (k < 40) & (size * worst * worst > limit)

    def step(state):
        k, _, total, power = state
        both = mul(jnp.concatenate([total, power], axis=0), power)
        total = total + both[:size]
        power = both[size:]
        return k + 1, jnp.max(jnp.abs(power)), total, power

    total = factor * (unit + rest)
    power = mul(rest, rest)
    rounds, worst, total, power = lax.while_loop(
        going, step, (1, jnp.max(jnp.abs(power)), total, power)
    )
    worst = size * worst * worst
    total = total + mul(total, power)
    return total * scale, worst, rounds


def ratio(left, whole):
    return jnp.min(diagonals(left)[0] / diagonals(whole)[0])


def galerkin_kernel(core_ref, mine_ref, theirs_ref, basis_ref, out_ref, rows_ref, good_ref, mom_ref):
    size = out_ref.shape[1]
    gap = jnp.zeros((64, 128), F32)
    right = iota((64, 128), 1) < 64
    upper = iota((size, size), 0) // 64 <= iota((size, size), 1) // 64

    def unpack(source_ref, start):
        for n in range(ITERS):
            at = n * PACK
            mixed = source_ref[at + 256 : at + 320]
            low = [source_ref[at : at + 64], jnp.where(right, 0.0, pltpu.roll(mixed, 64, 1)), gap, gap]
            up = [source_ref[at + 64 : at + 256], jnp.where(right, 0.0, mixed)]
            half = jnp.concatenate(
                [jnp.concatenate(low, axis=0), jnp.concatenate(up, axis=0)], axis=1
            )
            mom_ref[start + n] = jnp.where(upper, half, half.T)

    @pl.when(core_ref[0] == 0)
    def _():
        unpack(mine_ref, 0)
        unpack(theirs_ref, ITERS)

    @pl.when(core_ref[0] != 0)
    def _():
        unpack(theirs_ref, 0)
        unpack(mine_ref, ITERS)

    m = [mom_ref[n] for n in range(2 * ITERS)]
    h = [m[n + 1] + SHIFT * m[n] for n in range(2 * ITERS - 1)]

    def right_of(inverse, *targets):
        wide = split_dot(inverse, jnp.concatenate(targets, axis=1))
        return [wide[:, n * size : (n + 1) * size] for n in range(len(targets))]

    s0, w0, k0 = inverse_spd(h[0], split_dot, CLOSE)
    z01, z02, z0m = right_of(s0, h[1], h[2], m[0])
    upper = split_dot(h[1], jnp.concatenate([z01, z02, z0m], axis=1))
    lower = split_dot(h[2], jnp.concatenate([z02, z0m], axis=1))
    first = h[2] - upper[:, :size]
    cross = h[3] - upper[:, size : 2 * size]
    m1 = m[1] - upper[:, 2 * size :]
    last = h[4] - lower[:, :size]
    m2 = m[2] - lower[:, size:]
    first = 0.5 * (first + first.T)
    s1, w1, k1 = inverse_spd(first, split_dot, CLOSE)
    z12, z1m = right_of(s1, cross, m1)
    lower = split_dot(cross.T, jnp.concatenate([z12, z1m], axis=1))
    rest = last - lower[:, :size]
    rest = 0.5 * (rest + rest.T)
    m2 = m2 - lower[:, size:]
    s2, w2, k2 = inverse_spd(rest, split_dot, CLOSE)
    y2 = split_dot(s2, m2)
    y1 = z1m - split_dot(z12, y2)
    y0 = z0m - split_dot(jnp.concatenate([z01, z02], axis=1), jnp.concatenate([y1, y2], axis=0))
    out_ref[:size] = y0
    out_ref[size : 2 * size] = y1
    out_ref[2 * size :] = y2
    wide = out_ref.shape[0]
    yh, yl = halves(out_ref[...])
    for k in range(3):
        part = dot3(*halves(basis_ref[:, k * wide : (k + 1) * wide]), yh, yl)
        rows_ref[:, :, k * size : (k + 1) * size] = part.reshape(rows_ref.shape[0], -1, size)
    share = jnp.minimum(ratio(first, h[2]), ratio(rest, h[4]))
    rounds = jnp.maximum(k0, jnp.maximum(k1, k2))
    worst = jnp.maximum(w0, jnp.maximum(w1, w2))
    good_ref[0] = jnp.where((share > GUARD) & (worst <= CLOSE) & (rounds <= ROUNDS), 1, 0)


def galerkin(core, mine, theirs, basis_rows, peers):
    slots, wide = basis_rows.shape
    size = wide // (3 * ITERS)
    smem = pl.BlockSpec(memory_space=pltpu.SMEM)
    return pl.pallas_call(
        galerkin_kernel,
        out_shape=(
            jax.ShapeDtypeStruct((ITERS * size, size), F32),
            jax.ShapeDtypeStruct((peers, slots // peers, wide // ITERS), F32),
            jax.ShapeDtypeStruct((1,), jnp.int32),
        ),
        in_specs=[smem] + in_vmem(3),
        out_specs=(*in_vmem(2), smem),
        scratch_shapes=[pltpu.VMEM((2 * ITERS, size, size), F32)],
        compiler_params=pltpu.CompilerParams(vmem_limit_bytes=32 << 20),
        name="galerkin",
    )(core, mine, theirs, basis_rows)


def solve_kernel(matrix_ref, target_ref, out_ref):
    matrix = matrix_ref[...]
    matrix = 0.5 * (matrix + matrix.T)
    inverse, _, _ = inverse_spd(matrix, full_dot, 1e-9)
    guess = full_dot(inverse, target_ref[...])
    out_ref[...] = guess + full_dot(inverse, target_ref[...] - full_dot(matrix, guess))


def solve(matrix, target):
    return pl.pallas_call(
        solve_kernel,
        out_shape=jax.ShapeDtypeStruct(target.shape, F32),
        in_specs=in_vmem(2),
        out_specs=in_vmem(1)[0],
        name="solve",
    )(matrix, target)


def total_of(mine, theirs):
    shape = mine.shape
    chips = lax.axis_size(CHIPS)
    other = [(0, 1), (1, 0)]
    pair = mine + lax.ppermute(theirs, "core", other)
    pair = pair.reshape(chips, -1, 128)
    arrived = lax.all_to_all(pair, CHIPS, 0, 0, tiled=True)
    own = jnp.broadcast_to(arrived.sum(axis=0)[None], pair.shape)
    gathered = lax.all_to_all(own, CHIPS, 0, 0, tiled=True)
    gathered = gathered.reshape(shape)
    return gathered, lax.ppermute(gathered, "core", other)


def swap_sides(inner, outer):
    count = lax.axis_size(AXES)
    across = [(i, i + 1) for i in range(1, count - 1, 2)]
    return (
        lax.ppermute(inner, "core", [(0, 1), (1, 0)]),
        lax.ppermute(outer, AXES, across + [(b, a) for a, b in across]),
    )


def halo_of(vector):
    first = lax.axis_index("core") == 0
    head, tail = vector[:EDGE], vector[-EDGE:]
    return swap_sides(jnp.where(first, tail, head), jnp.where(first, head, tail))


def plain_cg(right_side, valid, bands):
    def times(a, b):
        return jnp.dot(a, b, preferred_element_type=F32, precision=lax.Precision.HIGHEST)

    def gram_of(lines, n):
        part = lines[n * PACK : (n + 1) * PACK]
        mixed = part[256:]
        gap = jnp.zeros((64, 64), F32)
        low = jnp.concatenate([gap, mixed[:, :64]], axis=1)
        up = jnp.concatenate([gap, mixed[:, 64:]], axis=1)
        empty = jnp.zeros((128, 128), F32)
        half = jnp.concatenate(
            [jnp.concatenate([part[:64], low, empty]), jnp.concatenate([part[64:256], up])], axis=1
        )
        block = jnp.arange(half.shape[0]) // 64
        return jnp.where(block[:, None] <= block[None, :], half, half.T)

    def step(k, state):
        answer, residual, direction, gram = state
        on_direction = k % 2 == 0
        vector = jnp.where(on_direction, direction, residual)
        image, mine, theirs = powers(vector, *halo_of(vector), valid, bands)
        low, high = total_of(mine, theirs)
        low = jnp.where(valid[2] == 0, low, high)
        square = gram_of(low, 0)
        gram = jnp.where(k == 0, square, gram)
        dir_gram = gram_of(low, 1) + SHIFT * square
        factor = solve(
            jnp.where(on_direction, dir_gram, gram), jnp.where(on_direction, gram, square)
        )
        along = times(direction, factor)
        applied = times(image[0] + SHIFT * vector, factor)
        answer = jnp.where(on_direction, answer + along, answer)
        direction = jnp.where(on_direction, direction, residual + along)
        residual = jnp.where(on_direction, residual - applied, residual)
        return answer, residual, direction, jnp.where(on_direction, gram, square)

    state = (jnp.zeros_like(right_side), right_side, right_side, jnp.zeros((right_side.shape[1],) * 2, F32))
    return lax.fori_loop(0, 2 * ITERS - 1, step, state)[0]


def loads_kernel(nodes_ref, load_ref, high_ref, low_ref, line_ref):
    support, slots = nodes_ref.shape
    unit = 8
    groups = slots // unit
    pairs = unit * support
    blocks = high_ref.shape[1] // 128
    wide = 3 * slots
    one = lambda mask: jnp.where(mask, 1.0, 0.0).astype(BF16)

    source = iota((wide, wide), 0)
    target = iota((wide, wide), 1)
    apart = one(source == target % slots * 3 + target // slots)
    parts = dot(jnp.concatenate(halves(load_ref[...]), axis=0), apart)

    owner = iota((groups, slots), 1) // unit == iota((groups, slots), 0)
    place = iota((slots, pairs), 0) % unit == iota((slots, pairs), 1) % unit
    turn = iota((slots, pairs), 1) // unit
    nodes = nodes_ref[...]
    fields = [parts[h * support : (h + 1) * support, k * slots : (k + 1) * slots] for k in range(3) for h in range(2)]
    fields += [(nodes // 128).astype(F32), (nodes % 128).astype(F32)]
    total = jnp.zeros((len(fields) * groups, pairs), F32)
    for s in range(support):
        spread = [jnp.where(owner, field[s : s + 1, :], 0.0) for field in fields]
        total = total + dot(jnp.concatenate(spread, axis=0).astype(BF16), one(place & (turn == s)))
    line_ref[...] = total

    own_lane = iota((unit, pairs), 1) % unit == iota((unit, pairs), 0)
    row = iota((128, pairs), 0)

    def line(n, g):
        return line_ref[pl.ds(n * groups + g, 1), :]

    def half_group(g):
        hot = one(row == line(7, g).astype(jnp.int32))
        block = jnp.broadcast_to(line(6, g).astype(jnp.int32), (unit, pairs))
        terms = [[jnp.where(own_lane, line(2 * k + h, g), 0.0) for h in range(2)] for k in range(3)]
        rows = []
        for c in range(blocks):
            hit = block == c
            for high, low in terms:
                rows.append(
                    jnp.concatenate([jnp.where(hit, high, 0.0), jnp.where(hit, low, 0.0)], axis=1)
                )
        left = jnp.concatenate(rows, axis=0).astype(BF16)
        return dot(left, jnp.concatenate([hot, hot], axis=1), ((1,), (1,)))

    def group(g, carry):
        first = half_group(2 * g)
        second = half_group(2 * g + 1)
        for c in range(blocks):
            for k in range(3):
                at = (c * 3 + k) * unit
                value = jnp.concatenate([first[at : at + unit], second[at : at + unit]], axis=0)
                high, low = halves(value)
                to = pl.multiple_of(k * slots + g * 2 * unit, 16)
                high_ref[pl.ds(to, 2 * unit), c * 128 : (c + 1) * 128] = high
                low_ref[pl.ds(to, 2 * unit), c * 128 : (c + 1) * 128] = low
        return carry

    lax.fori_loop(0, groups // 2, group, 0)


def load_matrix(slot_nodes, slot_load, rows):
    support, slots = slot_nodes.shape
    out = jax.ShapeDtypeStruct((3 * slots, rows), BF16)
    return pl.pallas_call(
        loads_kernel,
        out_shape=(out, out),
        in_specs=in_vmem(2),
        out_specs=tuple(in_vmem(2)),
        scratch_shapes=[pltpu.VMEM((slots, 8 * support), F32)],
        compiler_params=pltpu.CompilerParams(vmem_limit_bytes=24 << 20),
        name="loads",
    )(slot_nodes, slot_load)


CHUNK = 512


def basis_kernel(*refs):
    *vector_refs, wh_ref, wl_ref, out_ref = refs

    @pl.when(pl.program_id(0) == 0)
    def _():
        out_ref[...] = jnp.zeros_like(out_ref)

    slots = out_ref.shape[0]
    cols = vector_refs[0].shape[1]
    count = len(vector_refs)
    for n, ref in enumerate(vector_refs):
        full = dot3(wh_ref[...], wl_ref[...], *halves(ref[...]))
        for k in range(3):
            at = (k * count + n) * cols
            out_ref[:, at : at + cols] += full[k * slots : (k + 1) * slots]


def basis(vectors, weights):
    rows, cols = vectors[0][0].shape[-2:]
    loads = weights[0].shape[0]
    weight = pl.BlockSpec((loads, CHUNK), lambda i: (0, i))
    out = (loads // 3, 3 * len(vectors) * cols)
    return pl.pallas_call(
        basis_kernel,
        grid=(rows // CHUNK,),
        out_shape=jax.ShapeDtypeStruct(out, F32),
        in_specs=[spec for _, spec in vectors] + [weight, weight],
        out_specs=pl.BlockSpec(out, lambda i: (0, 0)),
        compiler_params=pltpu.CompilerParams(vmem_limit_bytes=28 << 20),
        name="basis",
    )(*[vector for vector, _ in vectors], *weights)


def in_chunks(vector, n=None):
    cols = vector.shape[-1]
    if n is None:
        return vector, pl.BlockSpec((CHUNK, cols), lambda i: (i, 0))
    placed = pltpu.with_memory_space_constraint(vector, pltpu.HBM)
    return placed, pl.BlockSpec((None, CHUNK, cols), lambda i: (n, i, 0))


def to_owner(rows):
    return lax.all_to_all(rows, AXES, 0, 0, tiled=True)


def combine_kernel(k0_ref, k1_ref, k2_ref, c_ref, x_ref, ch_ref, cl_ref):
    size = c_ref.shape[1]

    @pl.when(pl.program_id(0) == 0)
    def _():
        ch_ref[...], cl_ref[...] = halves(c_ref[...])

    total = jnp.zeros(x_ref.shape, F32)
    for n, ref in enumerate((k0_ref, k1_ref, k2_ref)):
        ah, al = halves(ref[...])
        at = n * size
        total = total + dot3(ah, al, ch_ref[at : at + size], cl_ref[at : at + size])
    x_ref[...] = total


def combine(vectors, coef):
    rows, cols = vectors[0][0].shape[-2:]
    return pl.pallas_call(
        combine_kernel,
        grid=(rows // CHUNK,),
        out_shape=jax.ShapeDtypeStruct((rows, cols), F32),
        in_specs=[spec for _, spec in vectors] + [pl.BlockSpec(coef.shape, lambda i: (0, 0))],
        out_specs=pl.BlockSpec((CHUNK, cols), lambda i: (i, 0)),
        scratch_shapes=[pltpu.VMEM(coef.shape, BF16)] * 2,
        compiler_params=pltpu.CompilerParams(vmem_limit_bytes=20 << 20),
        name="combine",
    )(*[vector for vector, _ in vectors], coef)


def lead_kernel(slot_ref, received_ref, out_ref):
    _, places, wide = received_ref.shape
    _, dipoles, cols = out_ref.shape
    together = 8

    def pick(i, carry):
        for n in range(together):
            slot = slot_ref[i * together + n]
            row = received_ref[slot // places, pl.ds(slot % places, 1), :]
            for k in range(wide // cols):
                out_ref[k, pl.ds(i * together + n, 1), :] = row[:, k * cols : (k + 1) * cols]
        return carry

    lax.fori_loop(0, dipoles // together, pick, 0)


def lead(received, dipole_slot):
    out = (3, dipole_slot.shape[0], received.shape[2] // 3)
    return pl.pallas_call(
        lead_kernel,
        out_shape=jax.ShapeDtypeStruct(out, F32),
        in_specs=[pl.BlockSpec(memory_space=pltpu.SMEM)] + in_vmem(1),
        out_specs=in_vmem(1)[0],
        compiler_params=pltpu.CompilerParams(vmem_limit_bytes=20 << 20),
        name="lead",
    )(dipole_slot, received)


def one_device(right_side, tile_stiff, tile_nodes, node_shift, slot_nodes, slot_load, dipole_slot):
    count = lax.axis_size(AXES)
    index = lax.axis_index(AXES)
    core = lax.axis_index("core")
    valid = jnp.stack([index > 0, index < count - 1, core]).astype(jnp.int32)
    inner, outer = halo_of(right_side)
    band, inner_band, outer_band = assemble(core[None], tile_stiff, tile_nodes, node_shift)
    bands = (band, *swap_sides(inner_band, outer_band))
    weights = load_matrix(slot_nodes, slot_load, right_side.shape[0])
    images, mine, theirs = powers(right_side, inner, outer, valid, bands)
    vectors = [in_chunks(right_side), in_chunks(images, 0), in_chunks(images, 1)]
    basis_rows = basis(vectors, weights)
    mine, theirs = total_of(mine, theirs)
    coef, rows, good = galerkin(core[None], mine, theirs, basis_rows, count)
    received = to_owner(rows)
    answer = combine(vectors, coef)
    leadfield = lead(received, dipole_slot)

    def exactly(_):
        exact = plain_cg(right_side, valid, bands)
        own_rows = basis([in_chunks(exact)], weights)
        received = to_owner(own_rows.reshape(count, -1, own_rows.shape[1]))
        return jnp.ones((), jnp.int32), exact, lead(received, dipole_slot)

    state = lax.while_loop(lambda state: state[0] == 0, exactly, (good[0], answer, leadfield))
    return state[1:]


def solution(mesh):
    rows, depth = mesh.devices.shape
    outer = 4 if rows % 4 == 0 else 1
    flat = Mesh(mesh.devices.reshape(outer, rows // outer, depth // 2, 2), AXES)
    return jax.shard_map(
        one_device,
        mesh=flat,
        in_specs=(
            P(AXES, None),
            P(AXES, None, None),
            P(AXES, None),
            P(AXES),
            P(None, AXES),
            P(None, AXES),
            P(AXES),
        ),
        out_specs=(P(AXES, None), P(None, AXES, None)),
        check_vma=False,
    )
```

```python
import jax
import jax.numpy as jnp
from jax import lax
from jax.experimental import pallas as pl
from jax.experimental.pallas import tpu as pltpu
from jax.sharding import Mesh
from jax.sharding import PartitionSpec as P


F32 = jnp.float32
BF16 = jnp.bfloat16
AXES = ("row", "column", "depth", "core")
CHIPS = ("row", "column", "depth")
ITERS = 3
HALO = 128
REACH = 64
WIN = 256
STEP = WIN - REACH
SHIFT = 4.5
ROUNDS = 8
CLOSE = 1e-6
GUARD = 0.01
SMALL = 128
SPAN = 80
BATCH = 8
TOGETHER = 4
EDGE = 192


def dot(a, b, dims=((1,), (0,))):
    return lax.dot_general(a, b, (dims, ((), ())), preferred_element_type=F32)


def halves(x):
    high = x.astype(BF16)
    return high, (x - high.astype(F32)).astype(BF16)


def dot3(ah, al, bh, bl, dims=((1,), (0,))):
    return dot(ah, bh, dims) + (dot(ah, bl, dims) + dot(al, bh, dims))


def full_dot(a, b):
    return lax.dot_general(
        a, b, (((1,), (0,)), ((), ())), preferred_element_type=F32, precision=lax.Precision.HIGHEST
    )


def iota(shape, dim):
    return lax.broadcasted_iota(jnp.int32, shape, dim)


def in_vmem(count):
    return [pl.BlockSpec(memory_space=pltpu.VMEM)] * count


def assemble_kernel(
    core_ref, group_ref, first_ref, stiff_ref, place_ref, offset_ref, diag_ref,
    out_ref, inner_ref, outer_ref,
    rows_ref, small_ref, block_ref, lane_ref, wait_ref,
):
    slots, _, tiles = stiff_ref.shape
    windows = out_ref.shape[0]
    lanes = BATCH * slots
    one = lambda mask: jnp.where(mask, 1.0, 0.0).astype(BF16)
    block_ref[...] = one(iota((lanes, lanes), 0) % BATCH == iota((lanes, lanes), 1) // slots)
    for t in range(BATCH):
        lane_ref[t * SPAN : (t + 1) * SPAN] = one(iota((SPAN, lanes), 1) % BATCH == t)

    def clear(g, carry):
        small_ref[g] = jnp.zeros((SMALL, SMALL), F32)
        return carry

    lax.fori_loop(0, small_ref.shape[0], clear, 0)

    def turn(i, carry):
        for n in range(4):
            plane = stiff_ref[4 * i + n]
            rows_ref[4 * i + n] = jnp.concatenate([plane] * (128 // slots), axis=0).T
        return carry

    lax.fori_loop(0, slots // 4, turn, 0)

    row_in_window = iota((SMALL, lanes), 0)
    row_in_span = iota((SPAN, lanes), 0)

    def first_side(b):
        base = pl.multiple_of(b * BATCH, BATCH)
        parts = halves(rows_ref[:, pl.ds(base, BATCH), :].reshape(lanes, 128))
        block = block_ref[...]
        wide = [jnp.concatenate([part] * (lanes // 128), axis=1) * block for part in parts]
        hot = one(row_in_window == place_ref[pl.ds(b, 1), :])
        return jnp.concatenate(wide, axis=0), hot

    def second_side(b):
        match = one(row_in_span == offset_ref[pl.ds(b, 1), :])
        return jnp.concatenate([match] * BATCH, axis=0) * lane_ref[...]

    def compute(i):
        batches = [TOGETHER * i + n for n in range(TOGETHER)]
        sides = [first_side(b) for b in batches]
        both = [dot(wide, hot, ((1,), (1,))) for wide, hot in sides]
        picks = [second_side(b) for b in batches]
        rights = [jnp.concatenate(halves(x[:lanes] + x[lanes:]), axis=1) for x in both]
        full = [dot(pick, right) for pick, right in zip(picks, rights)]
        return [x[:, :SMALL] + x[:, SMALL:] for x in full]

    def hold(full):
        for n in range(TOGETHER):
            wait_ref[n] = full[n]

    def add_up(i):
        for n in range(TOGETHER):
            for t in range(BATCH):
                tile = (TOGETHER * i + n) * BATCH + t
                r = pl.multiple_of(first_ref[tile], 16)
                small_ref[group_ref[tile], pl.ds(r, SPAN), :] += wait_ref[n, t * SPAN : (t + 1) * SPAN]

    rounds = tiles // (BATCH * TOGETHER)
    hold(compute(0))

    def batch(i, carry):
        full = compute(i)
        add_up(i - 1)
        hold(full)
        return carry

    lax.fori_loop(1, rounds, batch, 0)
    add_up(rounds - 1)

    eye = iota((WIN, WIN), 0) == iota((WIN, WIN), 1)
    gap = jnp.zeros((SMALL, REACH), F32)

    def gather(g, carry):
        out_ref[g] = jnp.where(eye, diag_ref[pl.ds(g, 1), :], 0.0)
        out_ref[g, :SMALL, :SMALL] += small_ref[3 * g]
        middle = jnp.concatenate([gap, small_ref[3 * g + 1], gap], axis=1)
        out_ref[g, REACH : REACH + SMALL, :] += middle
        out_ref[g, SMALL:, SMALL:] += small_ref[3 * g + 2]
        return carry

    lax.fori_loop(0, windows, gather, 0)

    def edges(up_ref, down_ref):
        up_ref[:128] = out_ref[windows - 2, 128:]
        up_ref[128:] = out_ref[windows - 1, :192]
        down_ref[:WIN] = out_ref[0]
        down_ref[WIN:] = out_ref[1, :64]

    pl.when(core_ref[0] == 0)(lambda: edges(inner_ref, outer_ref))
    pl.when(core_ref[0] != 0)(lambda: edges(outer_ref, inner_ref))


def assemble(core, tile_stiff, tile_nodes, node_shift):
    tiles, slots = tile_nodes.shape
    ext = node_shift.shape[0] + 2 * HALO
    windows = ext // STEP
    smalls = ext // REACH
    lowest = jnp.min(tile_nodes, axis=1)
    group = jnp.minimum(lowest // REACH, smalls - 1)
    first = jnp.minimum((lowest - group * REACH) // 16 * 16, REACH - 16)
    place = jnp.where(tile_nodes == ext, -1, tile_nodes - group[:, None] * REACH)
    offset = jnp.where(tile_nodes == ext, -1, place - first[:, None])
    diag = jnp.pad(node_shift - SHIFT, (HALO, HALO)).reshape(windows, STEP)
    diag = jnp.pad(diag, ((0, 0), (0, WIN - STEP)))
    lanes = BATCH * slots
    smem = pl.BlockSpec(memory_space=pltpu.SMEM)
    edge = jax.ShapeDtypeStruct((320, WIN), F32)
    return pl.pallas_call(
        assemble_kernel,
        out_shape=(jax.ShapeDtypeStruct((windows, WIN, WIN), F32), edge, edge),
        in_specs=[smem] * 3 + in_vmem(4),
        out_specs=tuple(in_vmem(3)),
        scratch_shapes=[
            pltpu.VMEM((slots, tiles, 128), F32),
            pltpu.VMEM((smalls, SMALL, SMALL), F32),
            pltpu.VMEM((lanes, lanes), BF16),
            pltpu.VMEM((BATCH * SPAN, lanes), BF16),
            pltpu.VMEM((TOGETHER, BATCH * SPAN, SMALL), F32),
        ],
        compiler_params=pltpu.CompilerParams(vmem_limit_bytes=28 << 20),
        name="assemble",
    )(
        core,
        group,
        first,
        jnp.transpose(tile_stiff, (1, 2, 0)),
        place.reshape(-1, lanes),
        offset.reshape(-1, BATCH, slots).transpose(0, 2, 1).reshape(-1, lanes),
        diag,
    )


LOW = 2 * HALO
PACK = 320


def powers_kernel(
    valid_ref, own_ref, inner_ref, outer_ref, band_ref, iband_ref, oband_ref,
    image_ref, mine_ref, theirs_ref,
    bh_ref, bl_ref, lh_ref, ll_ref, rh_ref, rl_ref, vh_ref, vl_ref, y_ref, sem,
):
    own, cols = own_ref.shape
    windows = band_ref.shape[0]
    frame = y_ref.shape[0]
    high = LOW + own
    chunk = 256

    def split_band(g, carry):
        bh_ref[g], bl_ref[g] = halves(band_ref[g])
        return carry

    lax.fori_loop(0, windows, split_band, 0)
    for ref in (vh_ref, vl_ref):
        for n, width in enumerate((EDGE, HALO)):
            ref[n, : LOW - width] = jnp.zeros((LOW - width, cols), BF16)
            ref[n, high + width :] = jnp.zeros((frame - high - width, cols), BF16)

    def put(n, at, value):
        vh_ref[n, at, :], vl_ref[n, at, :] = halves(value)

    def sides(left_ref, right_ref, lband_ref, rband_ref):
        put(0, pl.ds(LOW - EDGE, EDGE), left_ref[...])
        put(0, pl.ds(high, EDGE), right_ref[...])
        lh_ref[...], ll_ref[...] = halves(lband_ref[...])
        rh_ref[...], rl_ref[...] = halves(rband_ref[...])

    pl.when(valid_ref[2] == 0)(lambda: sides(outer_ref, inner_ref, oband_ref, iband_ref))
    pl.when(valid_ref[2] != 0)(lambda: sides(inner_ref, outer_ref, iband_ref, oband_ref))

    def split_own(i, carry):
        at = pl.multiple_of(i * chunk, chunk)
        put(0, pl.ds(LOW + at, chunk), own_ref[pl.ds(at, chunk), :])
        return carry

    lax.fori_loop(0, own // chunk, split_own, 0)

    def clear(i, carry):
        y_ref[pl.ds(pl.multiple_of(i * 64, 64), 64), :] = jnp.zeros((64, cols), F32)
        return carry

    tn = ((0,), (0,))

    def keep_moment(j, value):
        here = valid_ref[2] == j // ITERS
        low, up = value[:, :128], value[:, 128:]
        mixed = jnp.where(
            iota((64, 128), 1) < 64, pltpu.roll(low[64:128], 64, 1), up[192:]
        )
        for ref, chosen in ((mine_ref, here), (theirs_ref, jnp.logical_not(here))):
            @pl.when(chosen)
            def _(ref=ref):
                at = pl.multiple_of(j % ITERS * PACK, 64)
                ref[pl.ds(at, 64), :] = low[:64]
                ref[pl.ds(at + 64, 192), :] = up[:192]
                ref[pl.ds(at + 256, 64), :] = mixed

    for ref in (mine_ref, theirs_ref):
        ref[ITERS * PACK :] = jnp.zeros((ref.shape[0] - ITERS * PACK, 128), F32)

    def power(n, carry):
        now = n % 2
        then = 1 - now
        lax.fori_loop(0, frame // 64, clear, 0)

        def window(i, carry):
            values = []
            for m in range(3):
                at = pl.multiple_of(HALO + (3 * i + m) * STEP, 64)
                xh = vh_ref[now, pl.ds(at, WIN), :]
                xl = vl_ref[now, pl.ds(at, WIN), :]
                values.append((at, dot3(bh_ref[3 * i + m], bl_ref[3 * i + m], xh, xl)))
            for at, value in values:
                y_ref[pl.ds(at, WIN), :] += value
            return carry

        lax.fori_loop(0, windows // 3, window, 0)

        values = []
        for h_ref, l_ref, lo, rows, out, at in (
            (lh_ref, ll_ref, 0, 128, HALO, 0),
            (lh_ref, ll_ref, 128, 192, HALO + 64, HALO + 64),
            (rh_ref, rl_ref, 0, 256, own + HALO, own + HALO),
            (rh_ref, rl_ref, 256, 64, own + HALO + STEP, own + HALO + STEP),
        ):
            value = dot3(
                h_ref[lo : lo + rows], l_ref[lo : lo + rows],
                vh_ref[now, at : at + WIN], vl_ref[now, at : at + WIN],
            )
            values.append((out, rows, value))
        for out, rows, value in values:
            y_ref[out : out + rows] += value

        put(then, pl.ds(HALO, HALO), jnp.where(valid_ref[0] > 0, y_ref[HALO:LOW], 0.0))
        put(then, pl.ds(high, HALO), jnp.where(valid_ref[1] > 0, y_ref[high : high + HALO], 0.0))

        def split(i, carry):
            at = pl.multiple_of(i * chunk, chunk)
            value = y_ref[pl.ds(LOW + at, chunk), :]
            put(then, pl.ds(LOW + at, chunk), value)
            return carry

        copy = pltpu.make_async_copy(
            y_ref.at[pl.ds(LOW, own)], image_ref.at[jnp.minimum(n, ITERS - 2)], sem
        )
        pl.when(n + 1 < ITERS)(copy.start)
        lax.fori_loop(0, own // chunk, split, 0)

        xh, xl = vh_ref[now, LOW:high], vl_ref[now, LOW:high]
        zh, zl = vh_ref[then, LOW:high], vl_ref[then, LOW:high]
        by_high = dot(xh, jnp.concatenate([xh, xl, zh, zl], axis=1), tn)
        by_low = dot(xl, zh, tn)
        cross = by_high[:, cols : 2 * cols]
        keep_moment(2 * n, by_high[:, :cols] + (cross + cross.T))
        keep_moment(2 * n + 1, by_high[:, 2 * cols : 3 * cols] + (by_high[:, 3 * cols :] + by_low))

        pl.when(n + 1 < ITERS)(copy.wait)

        @pl.when(n == 0)
        def _():
            for ref in (vh_ref, vl_ref):
                ref[0, : HALO] = jnp.zeros((HALO, cols), BF16)
                ref[0, high + HALO :] = jnp.zeros((frame - high - HALO, cols), BF16)

        return carry

    lax.fori_loop(0, ITERS, power, 0)


def powers(vector, inner, outer, valid, bands):
    band, inner_band, outer_band = bands
    own, cols = vector.shape
    frame = own + 2 * LOW + 64
    half = jax.ShapeDtypeStruct((1024, 128), F32)
    wide = pltpu.VMEM((2, frame, cols), BF16)
    edge = pltpu.VMEM(inner_band.shape, BF16)
    return pl.pallas_call(
        powers_kernel,
        out_shape=(pltpu.HBM((ITERS - 1, own, cols), F32), half, half),
        in_specs=[pl.BlockSpec(memory_space=pltpu.SMEM)] + in_vmem(6),
        out_specs=(pl.BlockSpec(memory_space=pltpu.HBM), *in_vmem(2)),
        compiler_params=pltpu.CompilerParams(vmem_limit_bytes=32 << 20),
        scratch_shapes=[pltpu.VMEM(band.shape, BF16)] * 2 + [edge] * 4 + [wide] * 2
        + [pltpu.VMEM((frame, cols), F32), pltpu.SemaphoreType.DMA],
        name="powers",
    )(valid, vector, inner, outer, band, inner_band, outer_band)


def diagonals(matrix):
    size = matrix.shape[0]
    on = jnp.where(iota((size, size), 0) == iota((size, size), 1), matrix, 0.0)
    return jnp.sum(on, axis=0, keepdims=True), jnp.sum(on, axis=1, keepdims=True)


def split_dot(a, b):
    return dot3(*halves(a), *halves(b))


def inverse_spd(matrix):
    size = matrix.shape[0]
    unit = (iota((size, size), 0) == iota((size, size), 1)).astype(F32)
    along, down = diagonals(matrix)
    scale = lax.rsqrt(along) * lax.rsqrt(down)
    scaled = matrix * scale
    norm = jnp.max(jnp.sum(jnp.abs(scaled), axis=1, keepdims=True))
    factor = jnp.where(norm < 1.9, 1.0, 1.9 / norm)
    rest = unit - factor * scaled

    def going(state):
        k, worst, _, _ = state
        return (k < 40) & (size * worst * worst > 1e-9)

    def step(state):
        k, _, total, power = state
        both = full_dot(jnp.concatenate([total, power], axis=0), power)
        total = total + both[:size]
        power = both[size:]
        return k + 1, jnp.max(jnp.abs(power)), total, power

    total = factor * (unit + rest)
    power = full_dot(rest, rest)
    rounds, worst, total, power = lax.while_loop(
        going, step, (1, jnp.max(jnp.abs(power)), total, power)
    )
    worst = size * worst * worst
    total = total + full_dot(total, power)
    return total * scale, worst, rounds


def solve_fast(matrix, target):
    size = matrix.shape[0]
    direct = target.shape[1] == size
    unit = jnp.where(iota((size, size), 0) == iota((size, size), 1), 1.0, 0.0)
    along, down = diagonals(matrix)
    along, down = lax.rsqrt(along), lax.rsqrt(down)
    scaled = matrix * (along * down)
    norm = jnp.max(jnp.sum(jnp.abs(scaled), axis=1, keepdims=True), axis=0, keepdims=True)
    factor = jnp.where(norm < 1.9, 1.0, 1.9 / norm)
    power = unit - factor * scaled

    def twice(power, total):
        both = split_dot(power, jnp.concatenate([power, total], axis=1))
        return both[:, :size], total + both[:, size:]

    if direct:
        power, total = twice(power, target * (down * factor))
    else:
        total = factor * (unit + power)
        power = split_dot(power, power)
    power, total = twice(power, total)

    def going(state):
        k, worst, _, _ = state
        return (k < 40) & (size * worst * worst > CLOSE)

    def step(state):
        k, _, power, total = state
        power, total = twice(power, total)
        return k + 1, jnp.max(jnp.abs(power)), power, total

    rounds, worst, power, total = lax.while_loop(
        going, step, (2, jnp.max(jnp.abs(power)), power, total)
    )
    total = total + split_dot(power, total)
    if not direct:
        total = split_dot(total * along, target)
    return total * down, size * worst * worst, rounds


def ratio(left, whole):
    return jnp.min(diagonals(left)[0] / diagonals(whole)[0])


def galerkin_kernel(core_ref, mine_ref, theirs_ref, basis_ref, out_ref, rows_ref, good_ref, mom_ref, coef_ref, stage_ref, sems):
    size = out_ref.shape[1]
    gap = jnp.zeros((64, 128), F32)
    right = iota((64, 128), 1) < 64
    upper = iota((size, size), 0) // 64 <= iota((size, size), 1) // 64

    def unpack(source_ref, start):
        for n in range(ITERS):
            at = n * PACK
            mixed = source_ref[at + 256 : at + 320]
            low = [source_ref[at : at + 64], jnp.where(right, 0.0, pltpu.roll(mixed, 64, 1)), gap, gap]
            up = [source_ref[at + 64 : at + 256], jnp.where(right, 0.0, mixed)]
            half = jnp.concatenate(
                [jnp.concatenate(low, axis=0), jnp.concatenate(up, axis=0)], axis=1
            )
            mom_ref[start + n] = jnp.where(upper, half, half.T)

    @pl.when(core_ref[0] == 0)
    def _():
        unpack(mine_ref, 0)
        unpack(theirs_ref, ITERS)

    @pl.when(core_ref[0] != 0)
    def _():
        unpack(theirs_ref, 0)
        unpack(mine_ref, ITERS)

    m = [mom_ref[n] for n in range(2 * ITERS)]
    h = [m[n + 1] + SHIFT * m[n] for n in range(2 * ITERS - 1)]

    def solved(matrix, *targets):
        wide, worst, rounds = solve_fast(matrix, jnp.concatenate(targets, axis=1))
        return [wide[:, n * size : (n + 1) * size] for n in range(len(targets))], worst, rounds

    (z01, z02, z0m), w0, k0 = solved(h[0], h[1], h[2], m[0])
    upper = split_dot(h[1], jnp.concatenate([z01, z02, z0m], axis=1))
    lower = split_dot(h[2], jnp.concatenate([z02, z0m], axis=1))
    first = h[2] - upper[:, :size]
    cross = h[3] - upper[:, size : 2 * size]
    m1 = m[1] - upper[:, 2 * size :]
    last = h[4] - lower[:, :size]
    m2 = m[2] - lower[:, size:]
    first = 0.5 * (first + first.T)
    (z12, z1m), w1, k1 = solved(first, cross, m1)
    lower = split_dot(cross.T, jnp.concatenate([z12, z1m], axis=1))
    rest = last - lower[:, :size]
    rest = 0.5 * (rest + rest.T)
    m2 = m2 - lower[:, size:]
    (y2,), w2, k2 = solved(rest, m2)
    y1 = z1m - split_dot(z12, y2)
    y0 = z0m - split_dot(jnp.concatenate([z01, z02], axis=1), jnp.concatenate([y1, y2], axis=0))
    for n, y in enumerate((y0, y1, y2)):
        coef_ref[n * size : (n + 1) * size] = y
    keep = pltpu.make_async_copy(coef_ref, out_ref, sems.at[0])
    keep.start()
    wide = coef_ref.shape[0]
    yh, yl = halves(coef_ref[...])
    sends = []
    for k in range(3):
        part = dot3(*halves(basis_ref[:, k * wide : (k + 1) * wide]), yh, yl)
        stage_ref[k] = part.reshape(rows_ref.shape[0], -1, size)
        sends.append(
            pltpu.make_async_copy(stage_ref.at[k], rows_ref.at[:, :, pl.ds(k * size, size)], sems.at[k + 1])
        )
        sends[-1].start()
    share = jnp.minimum(ratio(first, h[2]), ratio(rest, h[4]))
    rounds = jnp.maximum(k0, jnp.maximum(k1, k2))
    worst = jnp.maximum(w0, jnp.maximum(w1, w2))
    for copy in [keep, *sends]:
        copy.wait()
    good_ref[0] = jnp.where((share > GUARD) & (worst <= CLOSE) & (rounds <= ROUNDS), 1, 0)


def galerkin(core, mine, theirs, basis_rows, peers):
    slots, wide = basis_rows.shape
    size = wide // (3 * ITERS)
    smem = pl.BlockSpec(memory_space=pltpu.SMEM)
    return pl.pallas_call(
        galerkin_kernel,
        out_shape=(
            pltpu.HBM((ITERS * size, size), F32),
            pltpu.HBM((peers, slots // peers, wide // ITERS), F32),
            jax.ShapeDtypeStruct((1,), jnp.int32),
        ),
        in_specs=[smem] + in_vmem(3),
        out_specs=(*[pl.BlockSpec(memory_space=pltpu.HBM)] * 2, smem),
        scratch_shapes=[
            pltpu.VMEM((2 * ITERS, size, size), F32),
            pltpu.VMEM((ITERS * size, size), F32),
            pltpu.VMEM((3, peers, slots // peers, size), F32),
            pltpu.SemaphoreType.DMA((4,)),
        ],
        compiler_params=pltpu.CompilerParams(vmem_limit_bytes=32 << 20),
        name="galerkin",
    )(core, mine, theirs, basis_rows)


def solve_kernel(matrix_ref, target_ref, out_ref):
    matrix = matrix_ref[...]
    matrix = 0.5 * (matrix + matrix.T)
    inverse, _, _ = inverse_spd(matrix)
    guess = full_dot(inverse, target_ref[...])
    out_ref[...] = guess + full_dot(inverse, target_ref[...] - full_dot(matrix, guess))


def solve(matrix, target):
    return pl.pallas_call(
        solve_kernel,
        out_shape=jax.ShapeDtypeStruct(target.shape, F32),
        in_specs=in_vmem(2),
        out_specs=in_vmem(1)[0],
        name="solve",
    )(matrix, target)


def total_of(mine, theirs):
    shape = mine.shape
    chips = lax.axis_size(CHIPS)
    other = [(0, 1), (1, 0)]
    pair = mine + lax.ppermute(theirs, "core", other)
    pair = pair.reshape(chips, -1, 128)
    arrived = lax.all_to_all(pair, CHIPS, 0, 0, tiled=True)
    own = jnp.broadcast_to(arrived.sum(axis=0)[None], pair.shape)
    gathered = lax.all_to_all(own, CHIPS, 0, 0, tiled=True)
    gathered = gathered.reshape(shape)
    return gathered, lax.ppermute(gathered, "core", other)


def swap_sides(inner, outer):
    count = lax.axis_size(AXES)
    across = [(i, i + 1) for i in range(1, count - 1, 2)]
    return (
        lax.ppermute(inner, "core", [(0, 1), (1, 0)]),
        lax.ppermute(outer, AXES, across + [(b, a) for a, b in across]),
    )


def halo_of(vector):
    first = lax.axis_index("core") == 0
    head, tail = vector[:EDGE], vector[-EDGE:]
    return swap_sides(jnp.where(first, tail, head), jnp.where(first, head, tail))


def plain_cg(right_side, valid, bands):
    def times(a, b):
        return jnp.dot(a, b, preferred_element_type=F32, precision=lax.Precision.HIGHEST)

    def gram_of(lines, n):
        part = lines[n * PACK : (n + 1) * PACK]
        mixed = part[256:]
        gap = jnp.zeros((64, 64), F32)
        low = jnp.concatenate([gap, mixed[:, :64]], axis=1)
        up = jnp.concatenate([gap, mixed[:, 64:]], axis=1)
        empty = jnp.zeros((128, 128), F32)
        half = jnp.concatenate(
            [jnp.concatenate([part[:64], low, empty]), jnp.concatenate([part[64:256], up])], axis=1
        )
        block = jnp.arange(half.shape[0]) // 64
        return jnp.where(block[:, None] <= block[None, :], half, half.T)

    def step(k, state):
        answer, residual, direction, gram = state
        on_direction = k % 2 == 0
        vector = jnp.where(on_direction, direction, residual)
        image, mine, theirs = powers(vector, *halo_of(vector), valid, bands)
        low, high = total_of(mine, theirs)
        low = jnp.where(valid[2] == 0, low, high)
        square = gram_of(low, 0)
        gram = jnp.where(k == 0, square, gram)
        dir_gram = gram_of(low, 1) + SHIFT * square
        factor = solve(
            jnp.where(on_direction, dir_gram, gram), jnp.where(on_direction, gram, square)
        )
        along = times(direction, factor)
        applied = times(image[0] + SHIFT * vector, factor)
        answer = jnp.where(on_direction, answer + along, answer)
        direction = jnp.where(on_direction, direction, residual + along)
        residual = jnp.where(on_direction, residual - applied, residual)
        return answer, residual, direction, jnp.where(on_direction, gram, square)

    state = (jnp.zeros_like(right_side), right_side, right_side, jnp.zeros((right_side.shape[1],) * 2, F32))
    return lax.fori_loop(0, 2 * ITERS - 1, step, state)[0]


def loads_kernel(nodes_ref, load_ref, high_ref, low_ref, line_ref):
    support, slots = nodes_ref.shape
    unit = 8
    groups = slots // unit
    pairs = unit * support
    blocks = high_ref.shape[1] // 128
    wide = 3 * slots
    one = lambda mask: jnp.where(mask, 1.0, 0.0).astype(BF16)

    source = iota((wide, wide), 0)
    target = iota((wide, wide), 1)
    apart = one(source == target % slots * 3 + target // slots)
    parts = dot(jnp.concatenate(halves(load_ref[...]), axis=0), apart)

    owner = iota((groups, slots), 1) // unit == iota((groups, slots), 0)
    place = iota((slots, pairs), 0) % unit == iota((slots, pairs), 1) % unit
    turn = iota((slots, pairs), 1) // unit
    nodes = nodes_ref[...]
    fields = [parts[h * support : (h + 1) * support, k * slots : (k + 1) * slots] for k in range(3) for h in range(2)]
    fields += [(nodes // 128).astype(F32), (nodes % 128).astype(F32)]
    total = jnp.zeros((len(fields) * groups, pairs), F32)
    for s in range(support):
        spread = [jnp.where(owner, field[s : s + 1, :], 0.0) for field in fields]
        total = total + dot(jnp.concatenate(spread, axis=0).astype(BF16), one(place & (turn == s)))
    line_ref[...] = total

    own_lane = iota((unit, pairs), 1) % unit == iota((unit, pairs), 0)
    row = iota((128, pairs), 0)

    def line(n, g):
        return line_ref[pl.ds(n * groups + g, 1), :]

    def half_group(g):
        hot = one(row == line(7, g).astype(jnp.int32))
        block = jnp.broadcast_to(line(6, g).astype(jnp.int32), (unit, pairs))
        terms = [[jnp.where(own_lane, line(2 * k + h, g), 0.0) for h in range(2)] for k in range(3)]
        rows = []
        for c in range(blocks):
            hit = block == c
            for high, low in terms:
                rows.append(
                    jnp.concatenate([jnp.where(hit, high, 0.0), jnp.where(hit, low, 0.0)], axis=1)
                )
        left = jnp.concatenate(rows, axis=0).astype(BF16)
        return dot(left, jnp.concatenate([hot, hot], axis=1), ((1,), (1,)))

    def group(g, carry):
        first = half_group(2 * g)
        second = half_group(2 * g + 1)
        for c in range(blocks):
            for k in range(3):
                at = (c * 3 + k) * unit
                value = jnp.concatenate([first[at : at + unit], second[at : at + unit]], axis=0)
                high, low = halves(value)
                to = pl.multiple_of(k * slots + g * 2 * unit, 16)
                high_ref[pl.ds(to, 2 * unit), c * 128 : (c + 1) * 128] = high
                low_ref[pl.ds(to, 2 * unit), c * 128 : (c + 1) * 128] = low
        return carry

    lax.fori_loop(0, groups // 2, group, 0)


def load_matrix(slot_nodes, slot_load, rows):
    support, slots = slot_nodes.shape
    out = jax.ShapeDtypeStruct((3 * slots, rows), BF16)
    return pl.pallas_call(
        loads_kernel,
        out_shape=(out, out),
        in_specs=in_vmem(2),
        out_specs=tuple(in_vmem(2)),
        scratch_shapes=[pltpu.VMEM((slots, 8 * support), F32)],
        compiler_params=pltpu.CompilerParams(vmem_limit_bytes=24 << 20),
        name="loads",
    )(slot_nodes, slot_load)


CHUNK = 512


def basis_kernel(*refs):
    *vector_refs, wh_ref, wl_ref, out_ref = refs

    @pl.when(pl.program_id(0) == 0)
    def _():
        out_ref[...] = jnp.zeros_like(out_ref)

    slots = out_ref.shape[0]
    cols = vector_refs[0].shape[1]
    count = len(vector_refs)
    for n, ref in enumerate(vector_refs):
        full = dot3(wh_ref[...], wl_ref[...], *halves(ref[...]))
        for k in range(3):
            at = (k * count + n) * cols
            out_ref[:, at : at + cols] += full[k * slots : (k + 1) * slots]


def basis(vectors, weights):
    rows, cols = vectors[0][0].shape[-2:]
    loads = weights[0].shape[0]
    weight = pl.BlockSpec((loads, CHUNK), lambda i: (0, i))
    out = (loads // 3, 3 * len(vectors) * cols)
    return pl.pallas_call(
        basis_kernel,
        grid=(rows // CHUNK,),
        out_shape=jax.ShapeDtypeStruct(out, F32),
        in_specs=[spec for _, spec in vectors] + [weight, weight],
        out_specs=pl.BlockSpec(out, lambda i: (0, 0)),
        compiler_params=pltpu.CompilerParams(vmem_limit_bytes=28 << 20),
        name="basis",
    )(*[vector for vector, _ in vectors], *weights)


def in_chunks(vector, n=None):
    cols = vector.shape[-1]
    if n is None:
        return vector, pl.BlockSpec((CHUNK, cols), lambda i: (i, 0))
    placed = pltpu.with_memory_space_constraint(vector, pltpu.HBM)
    return placed, pl.BlockSpec((None, CHUNK, cols), lambda i: (n, i, 0))


def to_owner(rows):
    return lax.all_to_all(rows, AXES, 0, 0, tiled=True)


def combine_kernel(k0_ref, k1_ref, k2_ref, c_ref, x_ref, ch_ref, cl_ref):
    size = c_ref.shape[1]

    @pl.when(pl.program_id(0) == 0)
    def _():
        ch_ref[...], cl_ref[...] = halves(c_ref[...])

    total = jnp.zeros(x_ref.shape, F32)
    for n, ref in enumerate((k0_ref, k1_ref, k2_ref)):
        ah, al = halves(ref[...])
        at = n * size
        total = total + dot3(ah, al, ch_ref[at : at + size], cl_ref[at : at + size])
    x_ref[...] = total


def combine(vectors, coef):
    rows, cols = vectors[0][0].shape[-2:]
    return pl.pallas_call(
        combine_kernel,
        grid=(rows // CHUNK,),
        out_shape=jax.ShapeDtypeStruct((rows, cols), F32),
        in_specs=[spec for _, spec in vectors] + [pl.BlockSpec(coef.shape, lambda i: (0, 0))],
        out_specs=pl.BlockSpec((CHUNK, cols), lambda i: (i, 0)),
        scratch_shapes=[pltpu.VMEM(coef.shape, BF16)] * 2,
        compiler_params=pltpu.CompilerParams(vmem_limit_bytes=20 << 20),
        name="combine",
    )(*[vector for vector, _ in vectors], pltpu.with_memory_space_constraint(coef, pltpu.HBM))


def lead_kernel(slot_ref, received_ref, out_ref):
    peers, places, wide = received_ref.shape
    _, dipoles, cols = out_ref.shape
    left = received_ref[...].reshape(peers * places, wide)
    hot = jnp.where(iota((peers * places, dipoles), 0) == slot_ref[...], 1.0, 0.0).astype(BF16)
    picked = jnp.zeros((dipoles, wide), F32)
    for _ in range(3):
        part = left.astype(BF16)
        left = left - part.astype(F32)
        picked = picked + dot(hot, part, ((0,), (0,)))
    for k in range(3):
        out_ref[k] = picked[:, k * cols : (k + 1) * cols]


def lead(received, dipole_slot):
    out = (3, dipole_slot.shape[0], received.shape[2] // 3)
    return pl.pallas_call(
        lead_kernel,
        out_shape=jax.ShapeDtypeStruct(out, F32),
        in_specs=in_vmem(2),
        out_specs=in_vmem(1)[0],
        compiler_params=pltpu.CompilerParams(vmem_limit_bytes=20 << 20),
        name="lead",
    )(dipole_slot[None], received)


def one_device(right_side, tile_stiff, tile_nodes, node_shift, slot_nodes, slot_load, dipole_slot):
    count = lax.axis_size(AXES)
    index = lax.axis_index(AXES)
    core = lax.axis_index("core")
    valid = jnp.stack([index > 0, index < count - 1, core]).astype(jnp.int32)
    inner, outer = halo_of(right_side)
    band, inner_band, outer_band = assemble(core[None], tile_stiff, tile_nodes, node_shift)
    bands = (band, *swap_sides(inner_band, outer_band))
    weights = load_matrix(slot_nodes, slot_load, right_side.shape[0])
    images, mine, theirs = powers(right_side, inner, outer, valid, bands)
    vectors = [in_chunks(right_side), in_chunks(images, 0), in_chunks(images, 1)]
    basis_rows = basis(vectors, weights)
    mine, theirs = total_of(mine, theirs)
    coef, rows, good = galerkin(core[None], mine, theirs, basis_rows, count)
    received = to_owner(rows)
    answer = combine(vectors, coef)
    leadfield = lead(received, dipole_slot)

    def exactly(_):
        exact = plain_cg(right_side, valid, bands)
        own_rows = basis([in_chunks(exact)], weights)
        received = to_owner(own_rows.reshape(count, -1, own_rows.shape[1]))
        return jnp.ones((), jnp.int32), exact, lead(received, dipole_slot)

    state = lax.while_loop(lambda state: state[0] == 0, exactly, (good[0], answer, leadfield))
    return state[1:]


def solution(mesh):
    rows, depth = mesh.devices.shape
    outer = 4 if rows % 4 == 0 else 1
    flat = Mesh(mesh.devices.reshape(outer, rows // outer, depth // 2, 2), AXES)
    return jax.shard_map(
        one_device,
        mesh=flat,
        in_specs=(
            P(AXES, None),
            P(AXES, None, None),
            P(AXES, None),
            P(AXES),
            P(None, AXES),
            P(None, AXES),
            P(AXES),
        ),
        out_specs=(P(AXES, None), P(None, AXES, None)),
        check_vma=False,
    )
```

```python
import jax
import jax.numpy as jnp
from jax import lax
from jax.experimental import pallas as pl
from jax.experimental.pallas import tpu as pltpu
from jax.sharding import Mesh
from jax.sharding import PartitionSpec as P


F32 = jnp.float32
BF16 = jnp.bfloat16
AXES = ("row", "column", "depth", "core")
CHIPS = ("row", "column", "depth")
ITERS = 3
HALO = 128
REACH = 64
WIN = 256
STEP = WIN - REACH
SHIFT = 4.5
ROUNDS = 8
CLOSE = 1e-6
GUARD = 0.01
SMALL = 128
SPAN = 80
BATCH = 8
TOGETHER = 4
EDGE = 192


def dot(a, b, dims=((1,), (0,))):
    return lax.dot_general(a, b, (dims, ((), ())), preferred_element_type=F32)


def halves(x):
    high = x.astype(BF16)
    return high, (x - high.astype(F32)).astype(BF16)


def dot3(ah, al, bh, bl, dims=((1,), (0,))):
    return dot(ah, bh, dims) + (dot(ah, bl, dims) + dot(al, bh, dims))


def full_dot(a, b):
    return lax.dot_general(
        a, b, (((1,), (0,)), ((), ())), preferred_element_type=F32, precision=lax.Precision.HIGHEST
    )


def iota(shape, dim):
    return lax.broadcasted_iota(jnp.int32, shape, dim)


def in_vmem(count):
    return [pl.BlockSpec(memory_space=pltpu.VMEM)] * count


def assemble_kernel(
    core_ref, group_ref, first_ref, stiff_ref, place_ref, offset_ref, diag_ref,
    out_ref, inner_ref, outer_ref,
    rows_ref, small_ref, block_ref, lane_ref, wait_ref,
):
    slots, _, tiles = stiff_ref.shape
    windows = out_ref.shape[0]
    lanes = BATCH * slots
    one = lambda mask: jnp.where(mask, 1.0, 0.0).astype(BF16)
    block_ref[...] = one(iota((lanes, lanes), 0) % BATCH == iota((lanes, lanes), 1) // slots)
    for t in range(BATCH):
        lane_ref[t * SPAN : (t + 1) * SPAN] = one(iota((SPAN, lanes), 1) % BATCH == t)

    def clear(g, carry):
        small_ref[g] = jnp.zeros((SMALL, SMALL), F32)
        return carry

    lax.fori_loop(0, small_ref.shape[0], clear, 0)

    def turn(i, carry):
        for n in range(4):
            plane = stiff_ref[4 * i + n]
            rows_ref[4 * i + n] = jnp.concatenate([plane] * (128 // slots), axis=0).T
        return carry

    lax.fori_loop(0, slots // 4, turn, 0)

    row_in_window = iota((SMALL, lanes), 0)
    row_in_span = iota((SPAN, lanes), 0)

    def first_side(b):
        base = pl.multiple_of(b * BATCH, BATCH)
        parts = halves(rows_ref[:, pl.ds(base, BATCH), :].reshape(lanes, 128))
        block = block_ref[...]
        wide = [jnp.concatenate([part] * (lanes // 128), axis=1) * block for part in parts]
        hot = one(row_in_window == place_ref[pl.ds(b, 1), :])
        return jnp.concatenate(wide, axis=0), hot

    def second_side(b):
        match = one(row_in_span == offset_ref[pl.ds(b, 1), :])
        return jnp.concatenate([match] * BATCH, axis=0) * lane_ref[...]

    def compute(i):
        batches = [TOGETHER * i + n for n in range(TOGETHER)]
        sides = [first_side(b) for b in batches]
        both = [dot(wide, hot, ((1,), (1,))) for wide, hot in sides]
        picks = [second_side(b) for b in batches]
        rights = [jnp.concatenate(halves(x[:lanes] + x[lanes:]), axis=1) for x in both]
        full = [dot(pick, right) for pick, right in zip(picks, rights)]
        return [x[:, :SMALL] + x[:, SMALL:] for x in full]

    def hold(full):
        for n in range(TOGETHER):
            wait_ref[n] = full[n]

    def add_up(i):
        for n in range(TOGETHER):
            for t in range(BATCH):
                tile = (TOGETHER * i + n) * BATCH + t
                r = pl.multiple_of(first_ref[tile], 16)
                small_ref[group_ref[tile], pl.ds(r, SPAN), :] += wait_ref[n, t * SPAN : (t + 1) * SPAN]

    rounds = tiles // (BATCH * TOGETHER)
    hold(compute(0))

    def batch(i, carry):
        full = compute(i)
        add_up(i - 1)
        hold(full)
        return carry

    lax.fori_loop(1, rounds, batch, 0)
    add_up(rounds - 1)

    eye = iota((WIN, WIN), 0) == iota((WIN, WIN), 1)
    gap = jnp.zeros((SMALL, REACH), F32)

    def gather(g, carry):
        out_ref[g] = jnp.where(eye, diag_ref[pl.ds(g, 1), :], 0.0)
        out_ref[g, :SMALL, :SMALL] += small_ref[3 * g]
        middle = jnp.concatenate([gap, small_ref[3 * g + 1], gap], axis=1)
        out_ref[g, REACH : REACH + SMALL, :] += middle
        out_ref[g, SMALL:, SMALL:] += small_ref[3 * g + 2]
        return carry

    lax.fori_loop(0, windows, gather, 0)

    def edges(up_ref, down_ref):
        up_ref[:128] = out_ref[windows - 2, 128:]
        up_ref[128:] = out_ref[windows - 1, :192]
        down_ref[:WIN] = out_ref[0]
        down_ref[WIN:] = out_ref[1, :64]

    pl.when(core_ref[0] == 0)(lambda: edges(inner_ref, outer_ref))
    pl.when(core_ref[0] != 0)(lambda: edges(outer_ref, inner_ref))


def assemble(core, tile_stiff, tile_nodes, node_shift):
    tiles, slots = tile_nodes.shape
    ext = node_shift.shape[0] + 2 * HALO
    windows = ext // STEP
    smalls = ext // REACH
    lowest = jnp.min(tile_nodes, axis=1)
    group = jnp.minimum(lowest // REACH, smalls - 1)
    first = jnp.minimum((lowest - group * REACH) // 16 * 16, REACH - 16)
    place = jnp.where(tile_nodes == ext, -1, tile_nodes - group[:, None] * REACH)
    offset = jnp.where(tile_nodes == ext, -1, place - first[:, None])
    diag = jnp.pad(node_shift - SHIFT, (HALO, HALO)).reshape(windows, STEP)
    diag = jnp.pad(diag, ((0, 0), (0, WIN - STEP)))
    lanes = BATCH * slots
    smem = pl.BlockSpec(memory_space=pltpu.SMEM)
    edge = jax.ShapeDtypeStruct((320, WIN), F32)
    return pl.pallas_call(
        assemble_kernel,
        out_shape=(jax.ShapeDtypeStruct((windows, WIN, WIN), F32), edge, edge),
        in_specs=[smem] * 3 + in_vmem(4),
        out_specs=tuple(in_vmem(3)),
        scratch_shapes=[
            pltpu.VMEM((slots, tiles, 128), F32),
            pltpu.VMEM((smalls, SMALL, SMALL), F32),
            pltpu.VMEM((lanes, lanes), BF16),
            pltpu.VMEM((BATCH * SPAN, lanes), BF16),
            pltpu.VMEM((TOGETHER, BATCH * SPAN, SMALL), F32),
        ],
        compiler_params=pltpu.CompilerParams(vmem_limit_bytes=28 << 20),
        name="assemble",
    )(
        core,
        group,
        first,
        jnp.transpose(tile_stiff, (1, 2, 0)),
        place.reshape(-1, lanes),
        offset.reshape(-1, BATCH, slots).transpose(0, 2, 1).reshape(-1, lanes),
        diag,
    )


LOW = 2 * HALO
PACK = 320


def frame_put(high_ref, low_ref):
    def put(at, value):
        high_ref[at, :], low_ref[at, :] = halves(value)

    return put


def add_windows(y_ref, bh_ref, bl_ref, xh_ref, xl_ref):
    def window(i, carry):
        values = []
        for m in range(3):
            at = pl.multiple_of(HALO + (3 * i + m) * STEP, 64)
            xh = xh_ref[pl.ds(at, WIN), :]
            xl = xl_ref[pl.ds(at, WIN), :]
            values.append((at, dot3(bh_ref[3 * i + m], bl_ref[3 * i + m], xh, xl)))
        for at, value in values:
            y_ref[pl.ds(at, WIN), :] += value
        return carry

    lax.fori_loop(0, bh_ref.shape[0] // 3, window, 0)


def clear_rows(y_ref):
    def clear(i, carry):
        y_ref[pl.ds(pl.multiple_of(i * 64, 64), 64), :] = jnp.zeros((64, y_ref.shape[1]), F32)
        return carry

    lax.fori_loop(0, y_ref.shape[0] // 64, clear, 0)


def first_kernel(
    valid_ref, own_ref, inner_ref, outer_ref, band_ref,
    bh_ref, bl_ref, xh_ref, xl_ref, y_ref,
):
    own, cols = own_ref.shape
    high = LOW + own
    chunk = 256

    def split_band(g, carry):
        bh_ref[g], bl_ref[g] = halves(band_ref[g])
        return carry

    lax.fori_loop(0, band_ref.shape[0], split_band, 0)
    put = frame_put(xh_ref, xl_ref)
    for ref in (xh_ref, xl_ref):
        ref[: LOW - EDGE] = jnp.zeros((LOW - EDGE, cols), BF16)
        ref[high + EDGE :] = jnp.zeros((ref.shape[0] - high - EDGE, cols), BF16)

    def sides(left_ref, right_ref):
        put(pl.ds(LOW - EDGE, EDGE), left_ref[...])
        put(pl.ds(high, EDGE), right_ref[...])

    pl.when(valid_ref[2] == 0)(lambda: sides(outer_ref, inner_ref))
    pl.when(valid_ref[2] != 0)(lambda: sides(inner_ref, outer_ref))

    def split_own(i, carry):
        at = pl.multiple_of(i * chunk, chunk)
        put(pl.ds(LOW + at, chunk), own_ref[pl.ds(at, chunk), :])
        return carry

    lax.fori_loop(0, own // chunk, split_own, 0)
    clear_rows(y_ref)
    add_windows(y_ref, bh_ref, bl_ref, xh_ref, xl_ref)


def powers_kernel(
    valid_ref, bh_ref, bl_ref, xh_ref, xl_ref, begun_ref, iband_ref, oband_ref,
    image_ref, mine_ref, theirs_ref,
    lh_ref, ll_ref, rh_ref, rl_ref, vh_ref, vl_ref, y_ref, sem,
):
    frame, cols = y_ref.shape
    own = image_ref.shape[1]
    high = LOW + own
    chunk = 256

    for ref in (vh_ref, vl_ref):
        for n in range(2):
            ref[n, :HALO] = jnp.zeros((HALO, cols), BF16)
            ref[n, high + HALO :] = jnp.zeros((frame - high - HALO, cols), BF16)
    vh_ref[2], vl_ref[2] = xh_ref[...], xl_ref[...]

    def sides(lband_ref, rband_ref):
        lh_ref[...], ll_ref[...] = halves(lband_ref[...])
        rh_ref[...], rl_ref[...] = halves(rband_ref[...])

    pl.when(valid_ref[2] == 0)(lambda: sides(oband_ref, iband_ref))
    pl.when(valid_ref[2] != 0)(lambda: sides(iband_ref, oband_ref))

    tn = ((0,), (0,))

    def keep_moment(j, value):
        here = valid_ref[2] == j // ITERS
        low, up = value[:, :128], value[:, 128:]
        mixed = jnp.where(
            iota((64, 128), 1) < 64, pltpu.roll(low[64:128], 64, 1), up[192:]
        )
        for ref, chosen in ((mine_ref, here), (theirs_ref, jnp.logical_not(here))):
            @pl.when(chosen)
            def _(ref=ref):
                at = pl.multiple_of(j % ITERS * PACK, 64)
                ref[pl.ds(at, 64), :] = low[:64]
                ref[pl.ds(at + 64, 192), :] = up[:192]
                ref[pl.ds(at + 256, 64), :] = mixed

    for ref in (mine_ref, theirs_ref):
        ref[ITERS * PACK :] = jnp.zeros((ref.shape[0] - ITERS * PACK, 128), F32)

    def power(n, carry):
        now = (n + 2) % 3
        then = n % 3
        source = (vh_ref.at[now], vl_ref.at[now])
        put = frame_put(vh_ref.at[then], vl_ref.at[then])

        @pl.when(n == 0)
        def _():
            y_ref[...] = begun_ref[...]

        @pl.when(n > 0)
        def _():
            clear_rows(y_ref)
            add_windows(y_ref, bh_ref, bl_ref, *source)

        values = []
        for h_ref, l_ref, lo, rows, out, at in (
            (lh_ref, ll_ref, 0, 128, HALO, 0),
            (lh_ref, ll_ref, 128, 192, HALO + 64, HALO + 64),
            (rh_ref, rl_ref, 0, 256, own + HALO, own + HALO),
            (rh_ref, rl_ref, 256, 64, own + HALO + STEP, own + HALO + STEP),
        ):
            value = dot3(
                h_ref[lo : lo + rows], l_ref[lo : lo + rows],
                vh_ref[now, at : at + WIN], vl_ref[now, at : at + WIN],
            )
            values.append((out, rows, value))
        for out, rows, value in values:
            y_ref[out : out + rows] += value

        put(pl.ds(HALO, HALO), jnp.where(valid_ref[0] > 0, y_ref[HALO:LOW], 0.0))
        put(pl.ds(high, HALO), jnp.where(valid_ref[1] > 0, y_ref[high : high + HALO], 0.0))

        def split(i, carry):
            at = pl.multiple_of(i * chunk, chunk)
            put(pl.ds(LOW + at, chunk), y_ref[pl.ds(LOW + at, chunk), :])
            return carry

        copy = pltpu.make_async_copy(
            y_ref.at[pl.ds(LOW, own)], image_ref.at[jnp.minimum(n, ITERS - 2)], sem
        )
        pl.when(n + 1 < ITERS)(copy.start)
        lax.fori_loop(0, own // chunk, split, 0)

        xh, xl = vh_ref[now, LOW:high], vl_ref[now, LOW:high]
        zh, zl = vh_ref[then, LOW:high], vl_ref[then, LOW:high]
        by_high = dot(xh, jnp.concatenate([xh, xl, zh, zl], axis=1), tn)
        by_low = dot(xl, zh, tn)
        cross = by_high[:, cols : 2 * cols]
        keep_moment(2 * n, by_high[:, :cols] + (cross + cross.T))
        keep_moment(2 * n + 1, by_high[:, 2 * cols : 3 * cols] + (by_high[:, 3 * cols :] + by_low))
        pl.when(n + 1 < ITERS)(copy.wait)
        return carry

    lax.fori_loop(0, ITERS, power, 0)


def begin(vector, inner, outer, valid, band):
    own, cols = vector.shape
    frame = own + 2 * LOW + 64
    part = jax.ShapeDtypeStruct(band.shape, BF16)
    wide = jax.ShapeDtypeStruct((frame, cols), BF16)
    return pl.pallas_call(
        first_kernel,
        out_shape=(part, part, wide, wide, jax.ShapeDtypeStruct((frame, cols), F32)),
        in_specs=[pl.BlockSpec(memory_space=pltpu.SMEM)] + in_vmem(4),
        out_specs=tuple(in_vmem(5)),
        compiler_params=pltpu.CompilerParams(vmem_limit_bytes=20 << 20),
        name="begin",
    )(valid, vector, inner, outer, band)


def powers(own, begun, valid, edges):
    frame, cols = begun[-1].shape
    half = jax.ShapeDtypeStruct((1024, 128), F32)
    wide = pltpu.VMEM((3, frame, cols), BF16)
    edge = pltpu.VMEM(edges[0].shape, BF16)
    return pl.pallas_call(
        powers_kernel,
        out_shape=(pltpu.HBM((ITERS - 1, own, cols), F32), half, half),
        in_specs=[pl.BlockSpec(memory_space=pltpu.SMEM)] + in_vmem(7),
        out_specs=(pl.BlockSpec(memory_space=pltpu.HBM), *in_vmem(2)),
        compiler_params=pltpu.CompilerParams(vmem_limit_bytes=28 << 20),
        scratch_shapes=[edge] * 4 + [wide] * 2 + [pltpu.VMEM((frame, cols), F32), pltpu.SemaphoreType.DMA],
        name="powers",
    )(valid, *begun, *edges)


def diagonals(matrix):
    size = matrix.shape[0]
    on = jnp.where(iota((size, size), 0) == iota((size, size), 1), matrix, 0.0)
    return jnp.sum(on, axis=0, keepdims=True), jnp.sum(on, axis=1, keepdims=True)


def split_dot(a, b):
    return dot3(*halves(a), *halves(b))


def inverse_spd(matrix):
    size = matrix.shape[0]
    unit = (iota((size, size), 0) == iota((size, size), 1)).astype(F32)
    along, down = diagonals(matrix)
    scale = lax.rsqrt(along) * lax.rsqrt(down)
    scaled = matrix * scale
    norm = jnp.max(jnp.sum(jnp.abs(scaled), axis=1, keepdims=True))
    factor = jnp.where(norm < 1.9, 1.0, 1.9 / norm)
    rest = unit - factor * scaled

    def going(state):
        k, worst, _, _ = state
        return (k < 40) & (size * worst * worst > 1e-9)

    def step(state):
        k, _, total, power = state
        both = full_dot(jnp.concatenate([total, power], axis=0), power)
        total = total + both[:size]
        power = both[size:]
        return k + 1, jnp.max(jnp.abs(power)), total, power

    total = factor * (unit + rest)
    power = full_dot(rest, rest)
    rounds, worst, total, power = lax.while_loop(
        going, step, (1, jnp.max(jnp.abs(power)), total, power)
    )
    worst = size * worst * worst
    total = total + full_dot(total, power)
    return total * scale, worst, rounds


def solve_fast(matrix, target):
    size = matrix.shape[0]
    direct = target.shape[1] == size
    unit = jnp.where(iota((size, size), 0) == iota((size, size), 1), 1.0, 0.0)
    along, down = diagonals(matrix)
    along, down = lax.rsqrt(along), lax.rsqrt(down)
    scaled = matrix * (along * down)
    norm = jnp.max(jnp.sum(jnp.abs(scaled), axis=1, keepdims=True), axis=0, keepdims=True)
    factor = jnp.where(norm < 1.9, 1.0, 1.9 / norm)
    power = unit - factor * scaled

    def twice(power, total):
        both = split_dot(power, jnp.concatenate([power, total], axis=1))
        return both[:, :size], total + both[:, size:]

    if direct:
        power, total = twice(power, target * (down * factor))
    else:
        total = factor * (unit + power)
        power = split_dot(power, power)
    power, total = twice(power, total)

    def left_out(power):
        return jnp.max(jnp.sum(power * power, axis=0, keepdims=True))

    def going(state):
        k, worst, _, _ = state
        return (k < 40) & (worst > CLOSE)

    def step(state):
        k, _, power, total = state
        power, total = twice(power, total)
        return k + 1, left_out(power), power, total

    rounds, worst, power, total = lax.while_loop(
        going, step, (2, left_out(power), power, total)
    )
    total = total + split_dot(power, total)
    if not direct:
        total = split_dot(total * along, target)
    return total * down, worst, rounds


def ratio(left, whole):
    return jnp.min(diagonals(left)[0] / diagonals(whole)[0])


def galerkin_kernel(core_ref, mine_ref, theirs_ref, basis_ref, out_ref, rows_ref, good_ref, mom_ref, coef_ref, stage_ref, sems):
    size = out_ref.shape[1]
    gap = jnp.zeros((64, 128), F32)
    right = iota((64, 128), 1) < 64
    upper = iota((size, size), 0) // 64 <= iota((size, size), 1) // 64

    def unpack(source_ref, start):
        for n in range(ITERS):
            at = n * PACK
            mixed = source_ref[at + 256 : at + 320]
            low = [source_ref[at : at + 64], jnp.where(right, 0.0, pltpu.roll(mixed, 64, 1)), gap, gap]
            up = [source_ref[at + 64 : at + 256], jnp.where(right, 0.0, mixed)]
            half = jnp.concatenate(
                [jnp.concatenate(low, axis=0), jnp.concatenate(up, axis=0)], axis=1
            )
            mom_ref[start + n] = jnp.where(upper, half, half.T)

    @pl.when(core_ref[0] == 0)
    def _():
        unpack(mine_ref, 0)
        unpack(theirs_ref, ITERS)

    @pl.when(core_ref[0] != 0)
    def _():
        unpack(theirs_ref, 0)
        unpack(mine_ref, ITERS)

    m = [mom_ref[n] for n in range(2 * ITERS)]
    h = [m[n + 1] + SHIFT * m[n] for n in range(2 * ITERS - 1)]

    def solved(matrix, *targets):
        wide, worst, rounds = solve_fast(matrix, jnp.concatenate(targets, axis=1))
        return [wide[:, n * size : (n + 1) * size] for n in range(len(targets))], worst, rounds

    (z01, z02, z0m), w0, k0 = solved(h[0], h[1], h[2], m[0])
    upper = split_dot(h[1], jnp.concatenate([z01, z02, z0m], axis=1))
    lower = split_dot(h[2], jnp.concatenate([z02, z0m], axis=1))
    first = h[2] - upper[:, :size]
    cross = h[3] - upper[:, size : 2 * size]
    m1 = m[1] - upper[:, 2 * size :]
    last = h[4] - lower[:, :size]
    m2 = m[2] - lower[:, size:]
    first = 0.5 * (first + first.T)
    (z12, z1m), w1, k1 = solved(first, cross, m1)
    lower = split_dot(cross.T, jnp.concatenate([z12, z1m], axis=1))
    rest = last - lower[:, :size]
    rest = 0.5 * (rest + rest.T)
    m2 = m2 - lower[:, size:]
    (y2,), w2, k2 = solved(rest, m2)
    y1 = z1m - split_dot(z12, y2)
    y0 = z0m - split_dot(jnp.concatenate([z01, z02], axis=1), jnp.concatenate([y1, y2], axis=0))
    for n, y in enumerate((y0, y1, y2)):
        coef_ref[n * size : (n + 1) * size] = y
    keep = pltpu.make_async_copy(coef_ref, out_ref, sems.at[0])
    keep.start()
    wide = coef_ref.shape[0]
    yh, yl = halves(coef_ref[...])
    sends = []
    for k in range(3):
        part = dot3(*halves(basis_ref[:, k * wide : (k + 1) * wide]), yh, yl)
        stage_ref[k] = part.reshape(rows_ref.shape[0], -1, size)
        sends.append(
            pltpu.make_async_copy(stage_ref.at[k], rows_ref.at[:, :, pl.ds(k * size, size)], sems.at[k + 1])
        )
        sends[-1].start()
    share = jnp.minimum(ratio(first, h[2]), ratio(rest, h[4]))
    rounds = jnp.maximum(k0, jnp.maximum(k1, k2))
    worst = jnp.maximum(w0, jnp.maximum(w1, w2))
    for copy in [keep, *sends]:
        copy.wait()
    good_ref[0] = jnp.where((share > GUARD) & (worst <= CLOSE) & (rounds <= ROUNDS), 1, 0)


def galerkin(core, mine, theirs, basis_rows, peers):
    slots, wide = basis_rows.shape
    size = wide // (3 * ITERS)
    smem = pl.BlockSpec(memory_space=pltpu.SMEM)
    return pl.pallas_call(
        galerkin_kernel,
        out_shape=(
            pltpu.HBM((ITERS * size, size), F32),
            pltpu.HBM((peers, slots // peers, wide // ITERS), F32),
            jax.ShapeDtypeStruct((1,), jnp.int32),
        ),
        in_specs=[smem] + in_vmem(3),
        out_specs=(*[pl.BlockSpec(memory_space=pltpu.HBM)] * 2, smem),
        scratch_shapes=[
            pltpu.VMEM((2 * ITERS, size, size), F32),
            pltpu.VMEM((ITERS * size, size), F32),
            pltpu.VMEM((3, peers, slots // peers, size), F32),
            pltpu.SemaphoreType.DMA((4,)),
        ],
        compiler_params=pltpu.CompilerParams(vmem_limit_bytes=32 << 20),
        name="galerkin",
    )(core, mine, theirs, basis_rows)


def solve_kernel(matrix_ref, target_ref, out_ref):
    matrix = matrix_ref[...]
    matrix = 0.5 * (matrix + matrix.T)
    inverse, _, _ = inverse_spd(matrix)
    guess = full_dot(inverse, target_ref[...])
    out_ref[...] = guess + full_dot(inverse, target_ref[...] - full_dot(matrix, guess))


def solve(matrix, target):
    return pl.pallas_call(
        solve_kernel,
        out_shape=jax.ShapeDtypeStruct(target.shape, F32),
        in_specs=in_vmem(2),
        out_specs=in_vmem(1)[0],
        name="solve",
    )(matrix, target)


def total_of(mine, theirs):
    shape = mine.shape
    chips = lax.axis_size(CHIPS)
    other = [(0, 1), (1, 0)]
    pair = mine + lax.ppermute(theirs, "core", other)
    pair = pair.reshape(chips, -1, 128)
    arrived = lax.all_to_all(pair, CHIPS, 0, 0, tiled=True)
    own = jnp.broadcast_to(arrived.sum(axis=0)[None], pair.shape)
    gathered = lax.all_to_all(own, CHIPS, 0, 0, tiled=True)
    gathered = gathered.reshape(shape)
    return gathered, lax.ppermute(gathered, "core", other)


def swap_sides(inner, outer):
    count = lax.axis_size(AXES)
    across = [(i, i + 1) for i in range(1, count - 1, 2)]
    return (
        lax.ppermute(inner, "core", [(0, 1), (1, 0)]),
        lax.ppermute(outer, AXES, across + [(b, a) for a, b in across]),
    )


def halo_of(vector):
    first = lax.axis_index("core") == 0
    head, tail = vector[:EDGE], vector[-EDGE:]
    return swap_sides(jnp.where(first, tail, head), jnp.where(first, head, tail))


def plain_cg(right_side, valid, bands):
    def times(a, b):
        return jnp.dot(a, b, preferred_element_type=F32, precision=lax.Precision.HIGHEST)

    def gram_of(lines, n):
        part = lines[n * PACK : (n + 1) * PACK]
        mixed = part[256:]
        gap = jnp.zeros((64, 64), F32)
        low = jnp.concatenate([gap, mixed[:, :64]], axis=1)
        up = jnp.concatenate([gap, mixed[:, 64:]], axis=1)
        empty = jnp.zeros((128, 128), F32)
        half = jnp.concatenate(
            [jnp.concatenate([part[:64], low, empty]), jnp.concatenate([part[64:256], up])], axis=1
        )
        block = jnp.arange(half.shape[0]) // 64
        return jnp.where(block[:, None] <= block[None, :], half, half.T)

    def step(k, state):
        answer, residual, direction, gram = state
        on_direction = k % 2 == 0
        vector = jnp.where(on_direction, direction, residual)
        begun = begin(vector, *halo_of(vector), valid, bands[0])
        image, mine, theirs = powers(vector.shape[0], begun, valid, bands[1:])
        low, high = total_of(mine, theirs)
        low = jnp.where(valid[2] == 0, low, high)
        square = gram_of(low, 0)
        gram = jnp.where(k == 0, square, gram)
        dir_gram = gram_of(low, 1) + SHIFT * square
        factor = solve(
            jnp.where(on_direction, dir_gram, gram), jnp.where(on_direction, gram, square)
        )
        along = times(direction, factor)
        applied = times(image[0] + SHIFT * vector, factor)
        answer = jnp.where(on_direction, answer + along, answer)
        direction = jnp.where(on_direction, direction, residual + along)
        residual = jnp.where(on_direction, residual - applied, residual)
        return answer, residual, direction, jnp.where(on_direction, gram, square)

    state = (jnp.zeros_like(right_side), right_side, right_side, jnp.zeros((right_side.shape[1],) * 2, F32))
    return lax.fori_loop(0, 2 * ITERS - 1, step, state)[0]


def loads_kernel(nodes_ref, load_ref, high_ref, low_ref, line_ref):
    support, slots = nodes_ref.shape
    unit = 8
    groups = slots // unit
    pairs = unit * support
    blocks = high_ref.shape[1] // 128
    wide = 3 * slots
    one = lambda mask: jnp.where(mask, 1.0, 0.0).astype(BF16)

    source = iota((wide, wide), 0)
    target = iota((wide, wide), 1)
    apart = one(source == target % slots * 3 + target // slots)
    parts = dot(jnp.concatenate(halves(load_ref[...]), axis=0), apart)

    owner = iota((groups, slots), 1) // unit == iota((groups, slots), 0)
    place = iota((slots, pairs), 0) % unit == iota((slots, pairs), 1) % unit
    turn = iota((slots, pairs), 1) // unit
    nodes = nodes_ref[...]
    fields = [parts[h * support : (h + 1) * support, k * slots : (k + 1) * slots] for k in range(3) for h in range(2)]
    fields += [(nodes // 128).astype(F32), (nodes % 128).astype(F32)]
    total = jnp.zeros((len(fields) * groups, pairs), F32)
    for s in range(support):
        spread = [jnp.where(owner, field[s : s + 1, :], 0.0) for field in fields]
        total = total + dot(jnp.concatenate(spread, axis=0).astype(BF16), one(place & (turn == s)))
    line_ref[...] = total

    own_lane = iota((unit, pairs), 1) % unit == iota((unit, pairs), 0)
    row = iota((128, pairs), 0)

    def line(n, g):
        return line_ref[pl.ds(n * groups + g, 1), :]

    def half_group(g):
        hot = one(row == line(7, g).astype(jnp.int32))
        block = jnp.broadcast_to(line(6, g).astype(jnp.int32), (unit, pairs))
        terms = [[jnp.where(own_lane, line(2 * k + h, g), 0.0) for h in range(2)] for k in range(3)]
        rows = []
        for c in range(blocks):
            hit = block == c
            for high, low in terms:
                rows.append(
                    jnp.concatenate([jnp.where(hit, high, 0.0), jnp.where(hit, low, 0.0)], axis=1)
                )
        left = jnp.concatenate(rows, axis=0).astype(BF16)
        return dot(left, jnp.concatenate([hot, hot], axis=1), ((1,), (1,)))

    def group(g, carry):
        first = half_group(2 * g)
        second = half_group(2 * g + 1)
        for c in range(blocks):
            for k in range(3):
                at = (c * 3 + k) * unit
                value = jnp.concatenate([first[at : at + unit], second[at : at + unit]], axis=0)
                high, low = halves(value)
                to = pl.multiple_of(k * slots + g * 2 * unit, 16)
                high_ref[pl.ds(to, 2 * unit), c * 128 : (c + 1) * 128] = high
                low_ref[pl.ds(to, 2 * unit), c * 128 : (c + 1) * 128] = low
        return carry

    lax.fori_loop(0, groups // 2, group, 0)


def load_matrix(slot_nodes, slot_load, rows):
    support, slots = slot_nodes.shape
    out = jax.ShapeDtypeStruct((3 * slots, rows), BF16)
    return pl.pallas_call(
        loads_kernel,
        out_shape=(out, out),
        in_specs=in_vmem(2),
        out_specs=tuple(in_vmem(2)),
        scratch_shapes=[pltpu.VMEM((slots, 8 * support), F32)],
        compiler_params=pltpu.CompilerParams(vmem_limit_bytes=24 << 20),
        name="loads",
    )(slot_nodes, slot_load)


CHUNK = 512


def basis_kernel(*refs):
    *vector_refs, wh_ref, wl_ref, out_ref = refs

    @pl.when(pl.program_id(0) == 0)
    def _():
        out_ref[...] = jnp.zeros_like(out_ref)

    slots = out_ref.shape[0]
    cols = vector_refs[0].shape[1]
    count = len(vector_refs)
    for n, ref in enumerate(vector_refs):
        full = dot3(wh_ref[...], wl_ref[...], *halves(ref[...]))
        for k in range(3):
            at = (k * count + n) * cols
            out_ref[:, at : at + cols] += full[k * slots : (k + 1) * slots]


def basis(vectors, weights):
    rows, cols = vectors[0][0].shape[-2:]
    loads = weights[0].shape[0]
    weight = pl.BlockSpec((loads, CHUNK), lambda i: (0, i))
    out = (loads // 3, 3 * len(vectors) * cols)
    return pl.pallas_call(
        basis_kernel,
        grid=(rows // CHUNK,),
        out_shape=jax.ShapeDtypeStruct(out, F32),
        in_specs=[spec for _, spec in vectors] + [weight, weight],
        out_specs=pl.BlockSpec(out, lambda i: (0, 0)),
        compiler_params=pltpu.CompilerParams(vmem_limit_bytes=28 << 20),
        name="basis",
    )(*[vector for vector, _ in vectors], *weights)


def in_chunks(vector, n=None):
    cols = vector.shape[-1]
    if n is None:
        return vector, pl.BlockSpec((CHUNK, cols), lambda i: (i, 0))
    placed = pltpu.with_memory_space_constraint(vector, pltpu.HBM)
    return placed, pl.BlockSpec((None, CHUNK, cols), lambda i: (n, i, 0))


def to_owner(rows):
    return lax.all_to_all(rows, AXES, 0, 0, tiled=True)


def combine_kernel(k0_ref, k1_ref, k2_ref, c_ref, x_ref, ch_ref, cl_ref):
    size = c_ref.shape[1]

    @pl.when(pl.program_id(0) == 0)
    def _():
        ch_ref[...], cl_ref[...] = halves(c_ref[...])

    total = jnp.zeros(x_ref.shape, F32)
    for n, ref in enumerate((k0_ref, k1_ref, k2_ref)):
        ah, al = halves(ref[...])
        at = n * size
        total = total + dot3(ah, al, ch_ref[at : at + size], cl_ref[at : at + size])
    x_ref[...] = total


def combine(vectors, coef):
    rows, cols = vectors[0][0].shape[-2:]
    return pl.pallas_call(
        combine_kernel,
        grid=(rows // CHUNK,),
        out_shape=jax.ShapeDtypeStruct((rows, cols), F32),
        in_specs=[spec for _, spec in vectors] + [pl.BlockSpec(coef.shape, lambda i: (0, 0))],
        out_specs=pl.BlockSpec((CHUNK, cols), lambda i: (i, 0)),
        scratch_shapes=[pltpu.VMEM(coef.shape, BF16)] * 2,
        compiler_params=pltpu.CompilerParams(vmem_limit_bytes=20 << 20),
        name="combine",
    )(*[vector for vector, _ in vectors], pltpu.with_memory_space_constraint(coef, pltpu.HBM))


def lead_kernel(slot_ref, received_ref, out_ref):
    peers, places, wide = received_ref.shape
    _, dipoles, cols = out_ref.shape
    left = received_ref[...].reshape(peers * places, wide)
    hot = jnp.where(iota((peers * places, dipoles), 0) == slot_ref[...], 1.0, 0.0).astype(BF16)
    picked = jnp.zeros((dipoles, wide), F32)
    for _ in range(3):
        part = left.astype(BF16)
        left = left - part.astype(F32)
        picked = picked + dot(hot, part, ((0,), (0,)))
    for k in range(3):
        out_ref[k] = picked[:, k * cols : (k + 1) * cols]


def lead(received, dipole_slot):
    out = (3, dipole_slot.shape[0], received.shape[2] // 3)
    return pl.pallas_call(
        lead_kernel,
        out_shape=jax.ShapeDtypeStruct(out, F32),
        in_specs=in_vmem(2),
        out_specs=in_vmem(1)[0],
        compiler_params=pltpu.CompilerParams(vmem_limit_bytes=20 << 20),
        name="lead",
    )(dipole_slot[None], received)


def one_device(right_side, tile_stiff, tile_nodes, node_shift, slot_nodes, slot_load, dipole_slot):
    count = lax.axis_size(AXES)
    index = lax.axis_index(AXES)
    core = lax.axis_index("core")
    valid = jnp.stack([index > 0, index < count - 1, core]).astype(jnp.int32)
    inner, outer = halo_of(right_side)
    band, inner_band, outer_band = assemble(core[None], tile_stiff, tile_nodes, node_shift)
    bands = (band, *swap_sides(inner_band, outer_band))
    weights = load_matrix(slot_nodes, slot_load, right_side.shape[0])
    begun = begin(right_side, inner, outer, valid, band)
    images, mine, theirs = powers(right_side.shape[0], begun, valid, bands[1:])
    vectors = [in_chunks(right_side), in_chunks(images, 0), in_chunks(images, 1)]
    basis_rows = basis(vectors, weights)
    mine, theirs = total_of(mine, theirs)
    coef, rows, good = galerkin(core[None], mine, theirs, basis_rows, count)
    received = to_owner(rows)
    answer = combine(vectors, coef)
    leadfield = lead(received, dipole_slot)

    def exactly(_):
        exact = plain_cg(right_side, valid, bands)
        own_rows = basis([in_chunks(exact)], weights)
        received = to_owner(own_rows.reshape(count, -1, own_rows.shape[1]))
        return jnp.ones((), jnp.int32), exact, lead(received, dipole_slot)

    state = lax.while_loop(lambda state: state[0] == 0, exactly, (good[0], answer, leadfield))
    return state[1:]


def solution(mesh):
    rows, depth = mesh.devices.shape
    outer = 4 if rows % 4 == 0 else 1
    flat = Mesh(mesh.devices.reshape(outer, rows // outer, depth // 2, 2), AXES)
    return jax.shard_map(
        one_device,
        mesh=flat,
        in_specs=(
            P(AXES, None),
            P(AXES, None, None),
            P(AXES, None),
            P(AXES),
            P(None, AXES),
            P(None, AXES),
            P(AXES),
        ),
        out_specs=(P(AXES, None), P(None, AXES, None)),
        check_vma=False,
    )
```

```python
import jax
import jax.numpy as jnp
from jax import lax
from jax.experimental import pallas as pl
from jax.experimental.pallas import tpu as pltpu
from jax.sharding import Mesh
from jax.sharding import PartitionSpec as P


F32 = jnp.float32
BF16 = jnp.bfloat16
AXES = ("row", "column", "depth", "core")
CHIPS = ("row", "column", "depth")
ITERS = 3
HALO = 128
REACH = 64
WIN = 256
STEP = WIN - REACH
SHIFT = 4.5
ROUNDS = 8
CLOSE = 1e-6
GUARD = 0.01
SMALL = 128
SPAN = 80
BATCH = 8
TOGETHER = 4
EDGE = 192


def dot(a, b, dims=((1,), (0,))):
    return lax.dot_general(a, b, (dims, ((), ())), preferred_element_type=F32)


def halves(x):
    high = x.astype(BF16)
    return high, (x - high.astype(F32)).astype(BF16)


def dot3(ah, al, bh, bl, dims=((1,), (0,))):
    return dot(ah, bh, dims) + (dot(ah, bl, dims) + dot(al, bh, dims))


def full_dot(a, b):
    return lax.dot_general(
        a, b, (((1,), (0,)), ((), ())), preferred_element_type=F32, precision=lax.Precision.HIGHEST
    )


def iota(shape, dim):
    return lax.broadcasted_iota(jnp.int32, shape, dim)


def in_vmem(count):
    return [pl.BlockSpec(memory_space=pltpu.VMEM)] * count


def assemble_kernel(
    core_ref, group_ref, first_ref, stiff_ref, place_ref, offset_ref, diag_ref,
    out_ref, inner_ref, outer_ref,
    rows_ref, small_ref, block_ref, lane_ref, wait_ref,
):
    slots, _, tiles = stiff_ref.shape
    windows = out_ref.shape[0]
    lanes = BATCH * slots
    one = lambda mask: jnp.where(mask, 1.0, 0.0).astype(BF16)
    block_ref[...] = one(iota((lanes, lanes), 0) % BATCH == iota((lanes, lanes), 1) // slots)
    for t in range(BATCH):
        lane_ref[t * SPAN : (t + 1) * SPAN] = one(iota((SPAN, lanes), 1) % BATCH == t)

    def clear(g, carry):
        small_ref[g] = jnp.zeros((SMALL, SMALL), F32)
        return carry

    lax.fori_loop(0, small_ref.shape[0], clear, 0)

    def turn(i, carry):
        for n in range(4):
            plane = stiff_ref[4 * i + n]
            rows_ref[4 * i + n] = jnp.concatenate([plane] * (128 // slots), axis=0).T
        return carry

    lax.fori_loop(0, slots // 4, turn, 0)

    row_in_window = iota((SMALL, lanes), 0)
    row_in_span = iota((SPAN, lanes), 0)

    def first_side(b):
        base = pl.multiple_of(b * BATCH, BATCH)
        parts = halves(rows_ref[:, pl.ds(base, BATCH), :].reshape(lanes, 128))
        block = block_ref[...]
        wide = [jnp.concatenate([part] * (lanes // 128), axis=1) * block for part in parts]
        hot = one(row_in_window == place_ref[pl.ds(b, 1), :])
        return jnp.concatenate(wide, axis=0), hot

    def second_side(b):
        match = one(row_in_span == offset_ref[pl.ds(b, 1), :])
        return jnp.concatenate([match] * BATCH, axis=0) * lane_ref[...]

    def compute(i):
        batches = [TOGETHER * i + n for n in range(TOGETHER)]
        sides = [first_side(b) for b in batches]
        both = [dot(wide, hot, ((1,), (1,))) for wide, hot in sides]
        picks = [second_side(b) for b in batches]
        rights = [jnp.concatenate(halves(x[:lanes] + x[lanes:]), axis=1) for x in both]
        full = [dot(pick, right) for pick, right in zip(picks, rights)]
        return [x[:, :SMALL] + x[:, SMALL:] for x in full]

    def hold(full):
        for n in range(TOGETHER):
            wait_ref[n] = full[n]

    def add_up(i):
        for n in range(TOGETHER):
            for t in range(BATCH):
                tile = (TOGETHER * i + n) * BATCH + t
                r = pl.multiple_of(first_ref[tile], 16)
                small_ref[group_ref[tile], pl.ds(r, SPAN), :] += wait_ref[n, t * SPAN : (t + 1) * SPAN]

    rounds = tiles // (BATCH * TOGETHER)
    hold(compute(0))

    def batch(i, carry):
        full = compute(i)
        add_up(i - 1)
        hold(full)
        return carry

    lax.fori_loop(1, rounds, batch, 0)
    add_up(rounds - 1)

    eye = iota((WIN, WIN), 0) == iota((WIN, WIN), 1)
    gap = jnp.zeros((SMALL, REACH), F32)

    def gather(g, carry):
        out_ref[g] = jnp.where(eye, diag_ref[pl.ds(g, 1), :], 0.0)
        out_ref[g, :SMALL, :SMALL] += small_ref[3 * g]
        middle = jnp.concatenate([gap, small_ref[3 * g + 1], gap], axis=1)
        out_ref[g, REACH : REACH + SMALL, :] += middle
        out_ref[g, SMALL:, SMALL:] += small_ref[3 * g + 2]
        return carry

    lax.fori_loop(0, windows, gather, 0)

    def edges(up_ref, down_ref):
        up_ref[:128] = out_ref[windows - 2, 128:]
        up_ref[128:] = out_ref[windows - 1, :192]
        down_ref[:WIN] = out_ref[0]
        down_ref[WIN:] = out_ref[1, :64]

    pl.when(core_ref[0] == 0)(lambda: edges(inner_ref, outer_ref))
    pl.when(core_ref[0] != 0)(lambda: edges(outer_ref, inner_ref))


def assemble(core, tile_stiff, tile_nodes, node_shift):
    tiles, slots = tile_nodes.shape
    ext = node_shift.shape[0] + 2 * HALO
    windows = ext // STEP
    smalls = ext // REACH
    lowest = jnp.min(tile_nodes, axis=1)
    group = jnp.minimum(lowest // REACH, smalls - 1)
    first = jnp.minimum((lowest - group * REACH) // 16 * 16, REACH - 16)
    place = jnp.where(tile_nodes == ext, -1, tile_nodes - group[:, None] * REACH)
    offset = jnp.where(tile_nodes == ext, -1, place - first[:, None])
    diag = jnp.pad(node_shift - SHIFT, (HALO, HALO)).reshape(windows, STEP)
    diag = jnp.pad(diag, ((0, 0), (0, WIN - STEP)))
    lanes = BATCH * slots
    smem = pl.BlockSpec(memory_space=pltpu.SMEM)
    edge = jax.ShapeDtypeStruct((320, WIN), F32)
    return pl.pallas_call(
        assemble_kernel,
        out_shape=(jax.ShapeDtypeStruct((windows, WIN, WIN), F32), edge, edge),
        in_specs=[smem] * 3 + in_vmem(4),
        out_specs=tuple(in_vmem(3)),
        scratch_shapes=[
            pltpu.VMEM((slots, tiles, 128), F32),
            pltpu.VMEM((smalls, SMALL, SMALL), F32),
            pltpu.VMEM((lanes, lanes), BF16),
            pltpu.VMEM((BATCH * SPAN, lanes), BF16),
            pltpu.VMEM((TOGETHER, BATCH * SPAN, SMALL), F32),
        ],
        compiler_params=pltpu.CompilerParams(vmem_limit_bytes=28 << 20),
        name="assemble",
    )(
        core,
        group,
        first,
        jnp.transpose(tile_stiff, (1, 2, 0)),
        place.reshape(-1, lanes),
        offset.reshape(-1, BATCH, slots).transpose(0, 2, 1).reshape(-1, lanes),
        diag,
    )


LOW = 2 * HALO
PACK = 320


def frame_put(high_ref, low_ref):
    def put(at, value):
        high_ref[at, :], low_ref[at, :] = halves(value)

    return put


def add_windows(y_ref, bh_ref, bl_ref, xh_ref, xl_ref):
    def window(i, carry):
        values = []
        for m in range(3):
            at = pl.multiple_of(HALO + (3 * i + m) * STEP, 64)
            xh = xh_ref[pl.ds(at, WIN), :]
            xl = xl_ref[pl.ds(at, WIN), :]
            values.append((at, dot3(bh_ref[3 * i + m], bl_ref[3 * i + m], xh, xl)))
        for at, value in values:
            y_ref[pl.ds(at, WIN), :] += value
        return carry

    lax.fori_loop(0, bh_ref.shape[0] // 3, window, 0)


def clear_rows(y_ref):
    def clear(i, carry):
        y_ref[pl.ds(pl.multiple_of(i * 64, 64), 64), :] = jnp.zeros((64, y_ref.shape[1]), F32)
        return carry

    lax.fori_loop(0, y_ref.shape[0] // 64, clear, 0)


def first_kernel(
    valid_ref, own_ref, inner_ref, outer_ref, band_ref,
    bh_ref, bl_ref, vh_ref, vl_ref, y_ref,
):
    own, cols = own_ref.shape
    xh_ref, xl_ref = vh_ref.at[2], vl_ref.at[2]
    high = LOW + own
    chunk = 256

    def split_band(g, carry):
        bh_ref[g], bl_ref[g] = halves(band_ref[g])
        return carry

    lax.fori_loop(0, band_ref.shape[0], split_band, 0)
    put = frame_put(xh_ref, xl_ref)
    for ref in (xh_ref, xl_ref):
        ref[: LOW - EDGE] = jnp.zeros((LOW - EDGE, cols), BF16)
        ref[high + EDGE :] = jnp.zeros((ref.shape[0] - high - EDGE, cols), BF16)

    def sides(left_ref, right_ref):
        put(pl.ds(LOW - EDGE, EDGE), left_ref[...])
        put(pl.ds(high, EDGE), right_ref[...])

    pl.when(valid_ref[2] == 0)(lambda: sides(outer_ref, inner_ref))
    pl.when(valid_ref[2] != 0)(lambda: sides(inner_ref, outer_ref))

    def split_own(i, carry):
        at = pl.multiple_of(i * chunk, chunk)
        put(pl.ds(LOW + at, chunk), own_ref[pl.ds(at, chunk), :])
        return carry

    lax.fori_loop(0, own // chunk, split_own, 0)
    clear_rows(y_ref)
    add_windows(y_ref, bh_ref, bl_ref, xh_ref, xl_ref)


def powers_kernel(
    valid_ref, bh_ref, bl_ref, _high_ref, _low_ref, _begun_ref, iband_ref, oband_ref,
    image_ref, mine_ref, theirs_ref, vh_ref, vl_ref, y_ref,
    lh_ref, ll_ref, rh_ref, rl_ref, sem,
):
    frame, cols = y_ref.shape
    own = image_ref.shape[1]
    high = LOW + own
    chunk = 256

    for ref in (vh_ref, vl_ref):
        for n in range(2):
            ref[n, :HALO] = jnp.zeros((HALO, cols), BF16)
            ref[n, high + HALO :] = jnp.zeros((frame - high - HALO, cols), BF16)

    def sides(lband_ref, rband_ref):
        lh_ref[...], ll_ref[...] = halves(lband_ref[...])
        rh_ref[...], rl_ref[...] = halves(rband_ref[...])

    pl.when(valid_ref[2] == 0)(lambda: sides(oband_ref, iband_ref))
    pl.when(valid_ref[2] != 0)(lambda: sides(iband_ref, oband_ref))

    tn = ((0,), (0,))

    def keep_moment(j, value):
        here = valid_ref[2] == j // ITERS
        low, up = value[:, :128], value[:, 128:]
        mixed = jnp.where(
            iota((64, 128), 1) < 64, pltpu.roll(low[64:128], 64, 1), up[192:]
        )
        for ref, chosen in ((mine_ref, here), (theirs_ref, jnp.logical_not(here))):
            @pl.when(chosen)
            def _(ref=ref):
                at = pl.multiple_of(j % ITERS * PACK, 64)
                ref[pl.ds(at, 64), :] = low[:64]
                ref[pl.ds(at + 64, 192), :] = up[:192]
                ref[pl.ds(at + 256, 64), :] = mixed

    for ref in (mine_ref, theirs_ref):
        ref[ITERS * PACK :] = jnp.zeros((ref.shape[0] - ITERS * PACK, 128), F32)

    def power(n, carry):
        now = (n + 2) % 3
        then = n % 3
        source = (vh_ref.at[now], vl_ref.at[now])
        put = frame_put(vh_ref.at[then], vl_ref.at[then])

        @pl.when(n > 0)
        def _():
            clear_rows(y_ref)
            add_windows(y_ref, bh_ref, bl_ref, *source)

        values = []
        for h_ref, l_ref, lo, rows, out, at in (
            (lh_ref, ll_ref, 0, 128, HALO, 0),
            (lh_ref, ll_ref, 128, 192, HALO + 64, HALO + 64),
            (rh_ref, rl_ref, 0, 256, own + HALO, own + HALO),
            (rh_ref, rl_ref, 256, 64, own + HALO + STEP, own + HALO + STEP),
        ):
            value = dot3(
                h_ref[lo : lo + rows], l_ref[lo : lo + rows],
                vh_ref[now, at : at + WIN], vl_ref[now, at : at + WIN],
            )
            values.append((out, rows, value))
        for out, rows, value in values:
            y_ref[out : out + rows] += value

        put(pl.ds(HALO, HALO), jnp.where(valid_ref[0] > 0, y_ref[HALO:LOW], 0.0))
        put(pl.ds(high, HALO), jnp.where(valid_ref[1] > 0, y_ref[high : high + HALO], 0.0))

        def split(i, carry):
            at = pl.multiple_of(i * chunk, chunk)
            put(pl.ds(LOW + at, chunk), y_ref[pl.ds(LOW + at, chunk), :])
            return carry

        copy = pltpu.make_async_copy(
            y_ref.at[pl.ds(LOW, own)], image_ref.at[jnp.minimum(n, ITERS - 2)], sem
        )
        pl.when(n + 1 < ITERS)(copy.start)
        lax.fori_loop(0, own // chunk, split, 0)

        xh, xl = vh_ref[now, LOW:high], vl_ref[now, LOW:high]
        zh, zl = vh_ref[then, LOW:high], vl_ref[then, LOW:high]
        by_high = dot(xh, jnp.concatenate([xh, xl, zh, zl], axis=1), tn)
        by_low = dot(xl, zh, tn)
        cross = by_high[:, cols : 2 * cols]
        keep_moment(2 * n, by_high[:, :cols] + (cross + cross.T))
        keep_moment(2 * n + 1, by_high[:, 2 * cols : 3 * cols] + (by_high[:, 3 * cols :] + by_low))
        pl.when(n + 1 < ITERS)(copy.wait)
        return carry

    lax.fori_loop(0, ITERS, power, 0)


def begin(vector, inner, outer, valid, band):
    own, cols = vector.shape
    frame = own + 2 * LOW + 64
    part = jax.ShapeDtypeStruct(band.shape, BF16)
    wide = jax.ShapeDtypeStruct((3, frame, cols), BF16)
    return pl.pallas_call(
        first_kernel,
        out_shape=(part, part, wide, wide, jax.ShapeDtypeStruct((frame, cols), F32)),
        in_specs=[pl.BlockSpec(memory_space=pltpu.SMEM)] + in_vmem(4),
        out_specs=tuple(in_vmem(5)),
        compiler_params=pltpu.CompilerParams(vmem_limit_bytes=20 << 20),
        name="begin",
    )(valid, vector, inner, outer, band)


def powers(own, begun, valid, edges):
    _, cols = begun[-1].shape
    half = jax.ShapeDtypeStruct((1024, 128), F32)
    edge = pltpu.VMEM(edges[0].shape, BF16)
    return pl.pallas_call(
        powers_kernel,
        out_shape=(
            pltpu.HBM((ITERS - 1, own, cols), F32),
            half,
            half,
            *[jax.ShapeDtypeStruct(part.shape, part.dtype) for part in begun[2:]],
        ),
        in_specs=[pl.BlockSpec(memory_space=pltpu.SMEM)] + in_vmem(7),
        out_specs=(pl.BlockSpec(memory_space=pltpu.HBM), *in_vmem(5)),
        input_output_aliases={3: 3, 4: 4, 5: 5},
        compiler_params=pltpu.CompilerParams(vmem_limit_bytes=28 << 20),
        scratch_shapes=[edge] * 4 + [pltpu.SemaphoreType.DMA],
        name="powers",
    )(valid, *begun, *edges)[:3]


def diagonals(matrix):
    size = matrix.shape[0]
    on = jnp.where(iota((size, size), 0) == iota((size, size), 1), matrix, 0.0)
    return jnp.sum(on, axis=0, keepdims=True), jnp.sum(on, axis=1, keepdims=True)


def split_dot(a, b):
    return dot3(*halves(a), *halves(b))


def inverse_spd(matrix):
    size = matrix.shape[0]
    unit = (iota((size, size), 0) == iota((size, size), 1)).astype(F32)
    along, down = diagonals(matrix)
    scale = lax.rsqrt(along) * lax.rsqrt(down)
    scaled = matrix * scale
    norm = jnp.max(jnp.sum(jnp.abs(scaled), axis=1, keepdims=True))
    factor = jnp.where(norm < 1.9, 1.0, 1.9 / norm)
    rest = unit - factor * scaled

    def going(state):
        k, worst, _, _ = state
        return (k < 40) & (size * worst * worst > 1e-9)

    def step(state):
        k, _, total, power = state
        both = full_dot(jnp.concatenate([total, power], axis=0), power)
        total = total + both[:size]
        power = both[size:]
        return k + 1, jnp.max(jnp.abs(power)), total, power

    total = factor * (unit + rest)
    power = full_dot(rest, rest)
    rounds, worst, total, power = lax.while_loop(
        going, step, (1, jnp.max(jnp.abs(power)), total, power)
    )
    worst = size * worst * worst
    total = total + full_dot(total, power)
    return total * scale, worst, rounds


def solve_fast(matrix, target):
    size = matrix.shape[0]
    direct = target.shape[1] == size
    unit = jnp.where(iota((size, size), 0) == iota((size, size), 1), 1.0, 0.0)
    along, down = diagonals(matrix)
    along, down = lax.rsqrt(along), lax.rsqrt(down)
    scaled = matrix * (along * down)
    norm = jnp.max(jnp.sum(jnp.abs(scaled), axis=1, keepdims=True), axis=0, keepdims=True)
    factor = jnp.where(norm < 1.9, 1.0, 1.9 / norm)
    power = unit - factor * scaled

    def twice(power, total):
        both = split_dot(power, jnp.concatenate([power, total], axis=1))
        return both[:, :size], total + both[:, size:]

    if direct:
        power, total = twice(power, target * (down * factor))
    else:
        total = factor * (unit + power)
        power = split_dot(power, power)
    power, total = twice(power, total)

    def left_out(power):
        return jnp.max(jnp.sum(power * power, axis=0, keepdims=True))

    def going(state):
        k, worst, _, _ = state
        return (k < 40) & (worst > CLOSE)

    def step(state):
        k, _, power, total = state
        power, total = twice(power, total)
        return k + 1, left_out(power), power, total

    rounds, worst, power, total = lax.while_loop(
        going, step, (2, left_out(power), power, total)
    )
    total = total + split_dot(power, total)
    if not direct:
        total = split_dot(total * along, target)
    return total * down, worst, rounds


def ratio(left, whole):
    return jnp.min(diagonals(left)[0] / diagonals(whole)[0])


def galerkin_kernel(core_ref, mine_ref, theirs_ref, basis_ref, out_ref, rows_ref, good_ref, mom_ref, coef_ref, stage_ref, sems):
    size = out_ref.shape[1]
    gap = jnp.zeros((64, 128), F32)
    right = iota((64, 128), 1) < 64
    upper = iota((size, size), 0) // 64 <= iota((size, size), 1) // 64

    def unpack(source_ref, start):
        for n in range(ITERS):
            at = n * PACK
            mixed = source_ref[at + 256 : at + 320]
            low = [source_ref[at : at + 64], jnp.where(right, 0.0, pltpu.roll(mixed, 64, 1)), gap, gap]
            up = [source_ref[at + 64 : at + 256], jnp.where(right, 0.0, mixed)]
            half = jnp.concatenate(
                [jnp.concatenate(low, axis=0), jnp.concatenate(up, axis=0)], axis=1
            )
            mom_ref[start + n] = jnp.where(upper, half, half.T)

    @pl.when(core_ref[0] == 0)
    def _():
        unpack(mine_ref, 0)
        unpack(theirs_ref, ITERS)

    @pl.when(core_ref[0] != 0)
    def _():
        unpack(theirs_ref, 0)
        unpack(mine_ref, ITERS)

    m = [mom_ref[n] for n in range(2 * ITERS)]
    h = [m[n + 1] + SHIFT * m[n] for n in range(2 * ITERS - 1)]

    def solved(matrix, *targets):
        wide, worst, rounds = solve_fast(matrix, jnp.concatenate(targets, axis=1))
        return [wide[:, n * size : (n + 1) * size] for n in range(len(targets))], worst, rounds

    (z01, z02, z0m), w0, k0 = solved(h[0], h[1], h[2], m[0])
    upper = split_dot(h[1], jnp.concatenate([z01, z02, z0m], axis=1))
    lower = split_dot(h[2], jnp.concatenate([z02, z0m], axis=1))
    first = h[2] - upper[:, :size]
    cross = h[3] - upper[:, size : 2 * size]
    m1 = m[1] - upper[:, 2 * size :]
    last = h[4] - lower[:, :size]
    m2 = m[2] - lower[:, size:]
    first = 0.5 * (first + first.T)
    (z12, z1m), w1, k1 = solved(first, cross, m1)
    lower = split_dot(cross.T, jnp.concatenate([z12, z1m], axis=1))
    rest = last - lower[:, :size]
    rest = 0.5 * (rest + rest.T)
    m2 = m2 - lower[:, size:]
    (y2,), w2, k2 = solved(rest, m2)
    y1 = z1m - split_dot(z12, y2)
    y0 = z0m - split_dot(jnp.concatenate([z01, z02], axis=1), jnp.concatenate([y1, y2], axis=0))
    for n, y in enumerate((y0, y1, y2)):
        coef_ref[n * size : (n + 1) * size] = y
    keep = pltpu.make_async_copy(coef_ref, out_ref, sems.at[0])
    keep.start()
    wide = coef_ref.shape[0]
    yh, yl = halves(coef_ref[...])
    sends = []
    for k in range(3):
        part = dot3(*halves(basis_ref[:, k * wide : (k + 1) * wide]), yh, yl)
        stage_ref[k] = part.reshape(rows_ref.shape[0], -1, size)
        sends.append(
            pltpu.make_async_copy(stage_ref.at[k], rows_ref.at[:, :, pl.ds(k * size, size)], sems.at[k + 1])
        )
        sends[-1].start()
    share = jnp.minimum(ratio(first, h[2]), ratio(rest, h[4]))
    rounds = jnp.maximum(k0, jnp.maximum(k1, k2))
    worst = jnp.maximum(w0, jnp.maximum(w1, w2))
    for copy in [keep, *sends]:
        copy.wait()
    good_ref[0] = jnp.where((share > GUARD) & (worst <= CLOSE) & (rounds <= ROUNDS), 1, 0)


def galerkin(core, mine, theirs, basis_rows, peers):
    slots, wide = basis_rows.shape
    size = wide // (3 * ITERS)
    smem = pl.BlockSpec(memory_space=pltpu.SMEM)
    return pl.pallas_call(
        galerkin_kernel,
        out_shape=(
            pltpu.HBM((ITERS * size, size), F32),
            pltpu.HBM((peers, slots // peers, wide // ITERS), F32),
            jax.ShapeDtypeStruct((1,), jnp.int32),
        ),
        in_specs=[smem] + in_vmem(3),
        out_specs=(*[pl.BlockSpec(memory_space=pltpu.HBM)] * 2, smem),
        scratch_shapes=[
            pltpu.VMEM((2 * ITERS, size, size), F32),
            pltpu.VMEM((ITERS * size, size), F32),
            pltpu.VMEM((3, peers, slots // peers, size), F32),
            pltpu.SemaphoreType.DMA((4,)),
        ],
        compiler_params=pltpu.CompilerParams(
            vmem_limit_bytes=32 << 20),
        name="galerkin",
    )(core, mine, theirs, basis_rows)


def solve_kernel(matrix_ref, target_ref, out_ref):
    matrix = matrix_ref[...]
    matrix = 0.5 * (matrix + matrix.T)
    inverse, _, _ = inverse_spd(matrix)
    guess = full_dot(inverse, target_ref[...])
    out_ref[...] = guess + full_dot(inverse, target_ref[...] - full_dot(matrix, guess))


def solve(matrix, target):
    return pl.pallas_call(
        solve_kernel,
        out_shape=jax.ShapeDtypeStruct(target.shape, F32),
        in_specs=in_vmem(2),
        out_specs=in_vmem(1)[0],
        name="solve",
    )(matrix, target)


def total_of(mine, theirs):
    shape = mine.shape
    chips = lax.axis_size(CHIPS)
    other = [(0, 1), (1, 0)]
    pair = mine + lax.ppermute(theirs, "core", other)
    pair = pair.reshape(chips, -1, 128)
    arrived = lax.all_to_all(pair, CHIPS, 0, 0, tiled=True)
    own = jnp.broadcast_to(arrived.sum(axis=0)[None], pair.shape)
    gathered = lax.all_to_all(own, CHIPS, 0, 0, tiled=True)
    gathered = gathered.reshape(shape)
    return gathered, lax.ppermute(gathered, "core", other)


def swap_sides(inner, outer):
    count = lax.axis_size(AXES)
    across = [(i, i + 1) for i in range(1, count - 1, 2)]
    return (
        lax.ppermute(inner, "core", [(0, 1), (1, 0)]),
        lax.ppermute(outer, AXES, across + [(b, a) for a, b in across]),
    )


def halo_of(vector):
    first = lax.axis_index("core") == 0
    head, tail = vector[:EDGE], vector[-EDGE:]
    return swap_sides(jnp.where(first, tail, head), jnp.where(first, head, tail))


def plain_cg(right_side, valid, bands):
    def times(a, b):
        return jnp.dot(a, b, preferred_element_type=F32, precision=lax.Precision.HIGHEST)

    def gram_of(lines, n):
        part = lines[n * PACK : (n + 1) * PACK]
        mixed = part[256:]
        gap = jnp.zeros((64, 64), F32)
        low = jnp.concatenate([gap, mixed[:, :64]], axis=1)
        up = jnp.concatenate([gap, mixed[:, 64:]], axis=1)
        empty = jnp.zeros((128, 128), F32)
        half = jnp.concatenate(
            [jnp.concatenate([part[:64], low, empty]), jnp.concatenate([part[64:256], up])], axis=1
        )
        block = jnp.arange(half.shape[0]) // 64
        return jnp.where(block[:, None] <= block[None, :], half, half.T)

    def step(k, state):
        answer, residual, direction, gram = state
        on_direction = k % 2 == 0
        vector = jnp.where(on_direction, direction, residual)
        begun = begin(vector, *halo_of(vector), valid, bands[0])
        image, mine, theirs = powers(vector.shape[0], begun, valid, bands[1:])
        low, high = total_of(mine, theirs)
        low = jnp.where(valid[2] == 0, low, high)
        square = gram_of(low, 0)
        gram = jnp.where(k == 0, square, gram)
        dir_gram = gram_of(low, 1) + SHIFT * square
        factor = solve(
            jnp.where(on_direction, dir_gram, gram), jnp.where(on_direction, gram, square)
        )
        along = times(direction, factor)
        applied = times(image[0] + SHIFT * vector, factor)
        answer = jnp.where(on_direction, answer + along, answer)
        direction = jnp.where(on_direction, direction, residual + along)
        residual = jnp.where(on_direction, residual - applied, residual)
        return answer, residual, direction, jnp.where(on_direction, gram, square)

    state = (jnp.zeros_like(right_side), right_side, right_side, jnp.zeros((right_side.shape[1],) * 2, F32))
    return lax.fori_loop(0, 2 * ITERS - 1, step, state)[0]


def loads_kernel(nodes_ref, load_ref, high_ref, low_ref, line_ref):
    support, slots = nodes_ref.shape
    unit = 8
    groups = slots // unit
    pairs = unit * support
    blocks = high_ref.shape[1] // 128
    wide = 3 * slots
    one = lambda mask: jnp.where(mask, 1.0, 0.0).astype(BF16)

    source = iota((wide, wide), 0)
    target = iota((wide, wide), 1)
    apart = one(source == target % slots * 3 + target // slots)
    parts = dot(jnp.concatenate(halves(load_ref[...]), axis=0), apart)

    owner = iota((groups, slots), 1) // unit == iota((groups, slots), 0)
    place = iota((slots, pairs), 0) % unit == iota((slots, pairs), 1) % unit
    turn = iota((slots, pairs), 1) // unit
    nodes = nodes_ref[...]
    fields = [parts[h * support : (h + 1) * support, k * slots : (k + 1) * slots] for k in range(3) for h in range(2)]
    fields += [(nodes // 128).astype(F32), (nodes % 128).astype(F32)]
    total = jnp.zeros((len(fields) * groups, pairs), F32)
    for s in range(support):
        spread = [jnp.where(owner, field[s : s + 1, :], 0.0) for field in fields]
        total = total + dot(jnp.concatenate(spread, axis=0).astype(BF16), one(place & (turn == s)))
    line_ref[...] = total

    own_lane = iota((unit, pairs), 1) % unit == iota((unit, pairs), 0)
    row = iota((128, pairs), 0)

    def line(n, g):
        return line_ref[pl.ds(n * groups + g, 1), :]

    def half_group(g):
        hot = one(row == line(7, g).astype(jnp.int32))
        block = jnp.broadcast_to(line(6, g).astype(jnp.int32), (unit, pairs))
        terms = [[jnp.where(own_lane, line(2 * k + h, g), 0.0) for h in range(2)] for k in range(3)]
        rows = []
        for c in range(blocks):
            hit = block == c
            for high, low in terms:
                rows.append(
                    jnp.concatenate([jnp.where(hit, high, 0.0), jnp.where(hit, low, 0.0)], axis=1)
                )
        left = jnp.concatenate(rows, axis=0).astype(BF16)
        return dot(left, jnp.concatenate([hot, hot], axis=1), ((1,), (1,)))

    def group(g, carry):
        first = half_group(2 * g)
        second = half_group(2 * g + 1)
        for c in range(blocks):
            for k in range(3):
                at = (c * 3 + k) * unit
                value = jnp.concatenate([first[at : at + unit], second[at : at + unit]], axis=0)
                high, low = halves(value)
                to = pl.multiple_of(k * slots + g * 2 * unit, 16)
                high_ref[pl.ds(to, 2 * unit), c * 128 : (c + 1) * 128] = high
                low_ref[pl.ds(to, 2 * unit), c * 128 : (c + 1) * 128] = low
        return carry

    lax.fori_loop(0, groups // 2, group, 0)


def load_matrix(slot_nodes, slot_load, rows):
    support, slots = slot_nodes.shape
    out = jax.ShapeDtypeStruct((3 * slots, rows), BF16)
    return pl.pallas_call(
        loads_kernel,
        out_shape=(out, out),
        in_specs=in_vmem(2),
        out_specs=tuple(in_vmem(2)),
        scratch_shapes=[pltpu.VMEM((slots, 8 * support), F32)],
        compiler_params=pltpu.CompilerParams(vmem_limit_bytes=24 << 20),
        name="loads",
    )(slot_nodes, slot_load)


CHUNK = 512


def basis_kernel(*refs):
    *vector_refs, wh_ref, wl_ref, out_ref = refs

    @pl.when(pl.program_id(0) == 0)
    def _():
        out_ref[...] = jnp.zeros_like(out_ref)

    slots = out_ref.shape[0]
    cols = vector_refs[0].shape[1]
    count = len(vector_refs)
    for n, ref in enumerate(vector_refs):
        full = dot3(wh_ref[...], wl_ref[...], *halves(ref[...]))
        for k in range(3):
            at = (k * count + n) * cols
            out_ref[:, at : at + cols] += full[k * slots : (k + 1) * slots]


def basis(vectors, weights):
    rows, cols = vectors[0][0].shape[-2:]
    loads = weights[0].shape[0]
    weight = pl.BlockSpec((loads, CHUNK), lambda i: (0, i))
    out = (loads // 3, 3 * len(vectors) * cols)
    return pl.pallas_call(
        basis_kernel,
        grid=(rows // CHUNK,),
        out_shape=jax.ShapeDtypeStruct(out, F32),
        in_specs=[spec for _, spec in vectors] + [weight, weight],
        out_specs=pl.BlockSpec(out, lambda i: (0, 0)),
        compiler_params=pltpu.CompilerParams(vmem_limit_bytes=28 << 20),
        name="basis",
    )(*[vector for vector, _ in vectors], *weights)


def in_chunks(vector, n=None):
    cols = vector.shape[-1]
    if n is None:
        return vector, pl.BlockSpec((CHUNK, cols), lambda i: (i, 0))
    placed = pltpu.with_memory_space_constraint(vector, pltpu.HBM)
    return placed, pl.BlockSpec((None, CHUNK, cols), lambda i: (n, i, 0))


def to_owner(rows):
    return lax.all_to_all(rows, AXES, 0, 0, tiled=True)


def combine_kernel(k0_ref, k1_ref, k2_ref, c_ref, x_ref, ch_ref, cl_ref):
    size = c_ref.shape[1]

    @pl.when(pl.program_id(0) == 0)
    def _():
        ch_ref[...], cl_ref[...] = halves(c_ref[...])

    total = jnp.zeros(x_ref.shape, F32)
    for n, ref in enumerate((k0_ref, k1_ref, k2_ref)):
        ah, al = halves(ref[...])
        at = n * size
        total = total + dot3(ah, al, ch_ref[at : at + size], cl_ref[at : at + size])
    x_ref[...] = total


def combine(vectors, coef):
    rows, cols = vectors[0][0].shape[-2:]
    return pl.pallas_call(
        combine_kernel,
        grid=(rows // CHUNK,),
        out_shape=jax.ShapeDtypeStruct((rows, cols), F32),
        in_specs=[spec for _, spec in vectors] + [pl.BlockSpec(coef.shape, lambda i: (0, 0))],
        out_specs=pl.BlockSpec((CHUNK, cols), lambda i: (i, 0)),
        scratch_shapes=[pltpu.VMEM(coef.shape, BF16)] * 2,
        compiler_params=pltpu.CompilerParams(vmem_limit_bytes=20 << 20),
        name="combine",
    )(*[vector for vector, _ in vectors], pltpu.with_memory_space_constraint(coef, pltpu.HBM))


def lead_kernel(slot_ref, received_ref, out_ref):
    peers, places, wide = received_ref.shape
    _, dipoles, cols = out_ref.shape
    left = received_ref[...].reshape(peers * places, wide)
    hot = jnp.where(iota((peers * places, dipoles), 0) == slot_ref[...], 1.0, 0.0).astype(BF16)
    picked = jnp.zeros((dipoles, wide), F32)
    for _ in range(3):
        part = left.astype(BF16)
        left = left - part.astype(F32)
        picked = picked + dot(hot, part, ((0,), (0,)))
    for k in range(3):
        out_ref[k] = picked[:, k * cols : (k + 1) * cols]


def lead(received, dipole_slot):
    out = (3, dipole_slot.shape[0], received.shape[2] // 3)
    return pl.pallas_call(
        lead_kernel,
        out_shape=jax.ShapeDtypeStruct(out, F32),
        in_specs=in_vmem(2),
        out_specs=in_vmem(1)[0],
        compiler_params=pltpu.CompilerParams(vmem_limit_bytes=20 << 20),
        name="lead",
    )(dipole_slot[None], received)


def one_device(right_side, tile_stiff, tile_nodes, node_shift, slot_nodes, slot_load, dipole_slot):
    count = lax.axis_size(AXES)
    index = lax.axis_index(AXES)
    core = lax.axis_index("core")
    valid = jnp.stack([index > 0, index < count - 1, core]).astype(jnp.int32)
    inner, outer = halo_of(right_side)
    band, inner_band, outer_band = assemble(core[None], tile_stiff, tile_nodes, node_shift)
    bands = (band, *swap_sides(inner_band, outer_band))
    weights = load_matrix(slot_nodes, slot_load, right_side.shape[0])
    begun = begin(right_side, inner, outer, valid, band)
    images, mine, theirs = powers(right_side.shape[0], begun, valid, bands[1:])
    vectors = [in_chunks(right_side), in_chunks(images, 0), in_chunks(images, 1)]
    basis_rows = basis(vectors, weights)
    mine, theirs = total_of(mine, theirs)
    coef, rows, good = galerkin(core[None], mine, theirs, basis_rows, count)
    received = to_owner(rows)
    answer = combine(vectors, coef)
    leadfield = lead(received, dipole_slot)

    def exactly(_):
        exact = plain_cg(right_side, valid, bands)
        own_rows = basis([in_chunks(exact)], weights)
        received = to_owner(own_rows.reshape(count, -1, own_rows.shape[1]))
        return jnp.ones((), jnp.int32), exact, lead(received, dipole_slot)

    state = lax.while_loop(lambda state: state[0] == 0, exactly, (good[0], answer, leadfield))
    return state[1:]


def solution(mesh):
    rows, depth = mesh.devices.shape
    outer = 4 if rows % 4 == 0 else 1
    flat = Mesh(mesh.devices.reshape(outer, rows // outer, depth // 2, 2), AXES)
    return jax.shard_map(
        one_device,
        mesh=flat,
        in_specs=(
            P(AXES, None),
            P(AXES, None, None),
            P(AXES, None),
            P(AXES),
            P(None, AXES),
            P(None, AXES),
            P(AXES),
        ),
        out_specs=(P(AXES, None), P(None, AXES, None)),
        check_vma=False,
    )
```

```python
import jax
import jax.numpy as jnp
from jax import lax
from jax.experimental import pallas as pl
from jax.experimental.pallas import tpu as pltpu
from jax.sharding import Mesh
from jax.sharding import PartitionSpec as P


F32 = jnp.float32
BF16 = jnp.bfloat16
AXES = ("row", "column", "depth", "core")
CHIPS = ("row", "column", "depth")
ITERS = 3
HALO = 128
REACH = 64
WIN = 256
STEP = WIN - REACH
SHIFT = 4.5
ROUNDS = 8
CLOSE = 1e-6
GUARD = 0.01
SMALL = 128
SPAN = 80
BATCH = 8
TOGETHER = 4
EDGE = 192


def dot(a, b, dims=((1,), (0,))):
    return lax.dot_general(a, b, (dims, ((), ())), preferred_element_type=F32)


def halves(x):
    high = x.astype(BF16)
    return high, (x - high.astype(F32)).astype(BF16)


def dot3(ah, al, bh, bl, dims=((1,), (0,))):
    return dot(ah, bh, dims) + (dot(ah, bl, dims) + dot(al, bh, dims))


def full_dot(a, b):
    return lax.dot_general(
        a, b, (((1,), (0,)), ((), ())), preferred_element_type=F32, precision=lax.Precision.HIGHEST
    )


def iota(shape, dim):
    return lax.broadcasted_iota(jnp.int32, shape, dim)


def in_vmem(count):
    return [pl.BlockSpec(memory_space=pltpu.VMEM)] * count


def assemble_kernel(
    core_ref, group_ref, first_ref, stiff_ref, place_ref, offset_ref, diag_ref,
    out_ref, inner_ref, outer_ref,
    rows_ref, small_ref, block_ref, lane_ref, wait_ref,
):
    slots, _, tiles = stiff_ref.shape
    windows = out_ref.shape[0]
    lanes = BATCH * slots
    one = lambda mask: jnp.where(mask, 1.0, 0.0).astype(BF16)
    block_ref[...] = one(iota((lanes, lanes), 0) % BATCH == iota((lanes, lanes), 1) // slots)
    for t in range(BATCH):
        lane_ref[t * SPAN : (t + 1) * SPAN] = one(iota((SPAN, lanes), 1) % BATCH == t)

    def clear(g, carry):
        small_ref[g] = jnp.zeros((SMALL, SMALL), F32)
        return carry

    lax.fori_loop(0, small_ref.shape[0], clear, 0)

    def turn(i, carry):
        for n in range(4):
            plane = stiff_ref[4 * i + n]
            rows_ref[4 * i + n] = jnp.concatenate([plane] * (128 // slots), axis=0).T
        return carry

    lax.fori_loop(0, slots // 4, turn, 0)

    row_in_window = iota((SMALL, lanes), 0)
    row_in_span = iota((SPAN, lanes), 0)

    def first_side(b):
        base = pl.multiple_of(b * BATCH, BATCH)
        parts = halves(rows_ref[:, pl.ds(base, BATCH), :].reshape(lanes, 128))
        block = block_ref[...]
        wide = [jnp.concatenate([part] * (lanes // 128), axis=1) * block for part in parts]
        hot = one(row_in_window == place_ref[pl.ds(b, 1), :])
        return jnp.concatenate(wide, axis=0), hot

    def second_side(b):
        match = one(row_in_span == offset_ref[pl.ds(b, 1), :])
        return jnp.concatenate([match] * BATCH, axis=0) * lane_ref[...]

    def compute(i):
        batches = [TOGETHER * i + n for n in range(TOGETHER)]
        sides = [first_side(b) for b in batches]
        both = [dot(wide, hot, ((1,), (1,))) for wide, hot in sides]
        picks = [second_side(b) for b in batches]
        rights = [jnp.concatenate(halves(x[:lanes] + x[lanes:]), axis=1) for x in both]
        full = [dot(pick, right) for pick, right in zip(picks, rights)]
        return [x[:, :SMALL] + x[:, SMALL:] for x in full]

    def hold(full):
        for n in range(TOGETHER):
            wait_ref[n] = full[n]

    def add_up(i):
        for n in range(TOGETHER):
            for t in range(BATCH):
                tile = (TOGETHER * i + n) * BATCH + t
                r = pl.multiple_of(first_ref[tile], 16)
                small_ref[group_ref[tile], pl.ds(r, SPAN), :] += wait_ref[n, t * SPAN : (t + 1) * SPAN]

    rounds = tiles // (BATCH * TOGETHER)
    hold(compute(0))

    def batch(i, carry):
        full = compute(i)
        add_up(i - 1)
        hold(full)
        return carry

    lax.fori_loop(1, rounds, batch, 0)
    add_up(rounds - 1)

    eye = iota((WIN, WIN), 0) == iota((WIN, WIN), 1)
    gap = jnp.zeros((SMALL, REACH), F32)

    def gather(g, carry):
        out_ref[g] = jnp.where(eye, diag_ref[pl.ds(g, 1), :], 0.0)
        out_ref[g, :SMALL, :SMALL] += small_ref[3 * g]
        middle = jnp.concatenate([gap, small_ref[3 * g + 1], gap], axis=1)
        out_ref[g, REACH : REACH + SMALL, :] += middle
        out_ref[g, SMALL:, SMALL:] += small_ref[3 * g + 2]
        return carry

    lax.fori_loop(0, windows, gather, 0)

    def edges(up_ref, down_ref):
        up_ref[:128] = out_ref[windows - 2, 128:]
        up_ref[128:] = out_ref[windows - 1, :192]
        down_ref[:WIN] = out_ref[0]
        down_ref[WIN:] = out_ref[1, :64]

    pl.when(core_ref[0] == 0)(lambda: edges(inner_ref, outer_ref))
    pl.when(core_ref[0] != 0)(lambda: edges(outer_ref, inner_ref))


def assemble(core, tile_stiff, tile_nodes, node_shift):
    tiles, slots = tile_nodes.shape
    ext = node_shift.shape[0] + 2 * HALO
    windows = ext // STEP
    smalls = ext // REACH
    lowest = jnp.min(tile_nodes, axis=1)
    group = jnp.minimum(lowest // REACH, smalls - 1)
    first = jnp.minimum((lowest - group * REACH) // 16 * 16, REACH - 16)
    place = jnp.where(tile_nodes == ext, -1, tile_nodes - group[:, None] * REACH)
    offset = jnp.where(tile_nodes == ext, -1, place - first[:, None])
    diag = jnp.pad(node_shift - SHIFT, (HALO, HALO)).reshape(windows, STEP)
    diag = jnp.pad(diag, ((0, 0), (0, WIN - STEP)))
    lanes = BATCH * slots
    smem = pl.BlockSpec(memory_space=pltpu.SMEM)
    edge = jax.ShapeDtypeStruct((320, WIN), F32)
    return pl.pallas_call(
        assemble_kernel,
        out_shape=(jax.ShapeDtypeStruct((windows, WIN, WIN), F32), edge, edge),
        in_specs=[smem] * 3 + in_vmem(4),
        out_specs=tuple(in_vmem(3)),
        scratch_shapes=[
            pltpu.VMEM((slots, tiles, 128), F32),
            pltpu.VMEM((smalls, SMALL, SMALL), F32),
            pltpu.VMEM((lanes, lanes), BF16),
            pltpu.VMEM((BATCH * SPAN, lanes), BF16),
            pltpu.VMEM((TOGETHER, BATCH * SPAN, SMALL), F32),
        ],
        compiler_params=pltpu.CompilerParams(vmem_limit_bytes=28 << 20),
        name="assemble",
    )(
        core,
        group,
        first,
        jnp.transpose(tile_stiff, (1, 2, 0)),
        place.reshape(-1, lanes),
        offset.reshape(-1, BATCH, slots).transpose(0, 2, 1).reshape(-1, lanes),
        diag,
    )


LOW = 2 * HALO
PACK = 320


def frame_put(high_ref, low_ref):
    def put(at, value):
        high_ref[at, :], low_ref[at, :] = halves(value)

    return put


def add_windows(y_ref, bh_ref, bl_ref, xh_ref, xl_ref):
    def window(i, carry):
        values = []
        for m in range(3):
            at = pl.multiple_of(HALO + (3 * i + m) * STEP, 64)
            xh = xh_ref[pl.ds(at, WIN), :]
            xl = xl_ref[pl.ds(at, WIN), :]
            values.append((at, dot3(bh_ref[3 * i + m], bl_ref[3 * i + m], xh, xl)))
        for at, value in values:
            y_ref[pl.ds(at, WIN), :] += value
        return carry

    lax.fori_loop(0, bh_ref.shape[0] // 3, window, 0)


def clear_rows(y_ref):
    def clear(i, carry):
        y_ref[pl.ds(pl.multiple_of(i * 64, 64), 64), :] = jnp.zeros((64, y_ref.shape[1]), F32)
        return carry

    lax.fori_loop(0, y_ref.shape[0] // 64, clear, 0)


def first_kernel(
    valid_ref, own_ref, inner_ref, outer_ref, band_ref,
    bh_ref, bl_ref, vh_ref, vl_ref, y_ref,
):
    own, cols = own_ref.shape
    xh_ref, xl_ref = vh_ref.at[2], vl_ref.at[2]
    high = LOW + own
    chunk = 256

    def split_band(g, carry):
        bh_ref[g], bl_ref[g] = halves(band_ref[g])
        return carry

    lax.fori_loop(0, band_ref.shape[0], split_band, 0)
    put = frame_put(xh_ref, xl_ref)
    for ref in (xh_ref, xl_ref):
        ref[: LOW - EDGE] = jnp.zeros((LOW - EDGE, cols), BF16)
        ref[high + EDGE :] = jnp.zeros((ref.shape[0] - high - EDGE, cols), BF16)

    def sides(left_ref, right_ref):
        put(pl.ds(LOW - EDGE, EDGE), left_ref[...])
        put(pl.ds(high, EDGE), right_ref[...])

    pl.when(valid_ref[2] == 0)(lambda: sides(outer_ref, inner_ref))
    pl.when(valid_ref[2] != 0)(lambda: sides(inner_ref, outer_ref))

    def split_own(i, carry):
        at = pl.multiple_of(i * chunk, chunk)
        put(pl.ds(LOW + at, chunk), own_ref[pl.ds(at, chunk), :])
        return carry

    lax.fori_loop(0, own // chunk, split_own, 0)
    clear_rows(y_ref)
    add_windows(y_ref, bh_ref, bl_ref, xh_ref, xl_ref)


def powers_kernel(
    valid_ref, bh_ref, bl_ref, _high_ref, _low_ref, _begun_ref, iband_ref, oband_ref,
    image_ref, mine_ref, theirs_ref, vh_ref, vl_ref, y_ref,
    lh_ref, ll_ref, rh_ref, rl_ref, sem,
):
    frame, cols = y_ref.shape
    own = image_ref.shape[1]
    high = LOW + own
    chunk = 256

    for ref in (vh_ref, vl_ref):
        for n in range(2):
            ref[n, :HALO] = jnp.zeros((HALO, cols), BF16)
            ref[n, high + HALO :] = jnp.zeros((frame - high - HALO, cols), BF16)

    def sides(lband_ref, rband_ref):
        lh_ref[...], ll_ref[...] = halves(lband_ref[...])
        rh_ref[...], rl_ref[...] = halves(rband_ref[...])

    pl.when(valid_ref[2] == 0)(lambda: sides(oband_ref, iband_ref))
    pl.when(valid_ref[2] != 0)(lambda: sides(iband_ref, oband_ref))

    tn = ((0,), (0,))

    def keep_moment(j, value):
        here = valid_ref[2] == j // ITERS
        low, up = value[:, :128], value[:, 128:]
        mixed = jnp.where(
            iota((64, 128), 1) < 64, pltpu.roll(low[64:128], 64, 1), up[192:]
        )
        for ref, chosen in ((mine_ref, here), (theirs_ref, jnp.logical_not(here))):
            @pl.when(chosen)
            def _(ref=ref):
                at = pl.multiple_of(j % ITERS * PACK, 64)
                ref[pl.ds(at, 64), :] = low[:64]
                ref[pl.ds(at + 64, 192), :] = up[:192]
                ref[pl.ds(at + 256, 64), :] = mixed

    for ref in (mine_ref, theirs_ref):
        ref[ITERS * PACK :] = jnp.zeros((ref.shape[0] - ITERS * PACK, 128), F32)

    def power(n, carry):
        now = (n + 2) % 3
        then = n % 3
        source = (vh_ref.at[now], vl_ref.at[now])
        put = frame_put(vh_ref.at[then], vl_ref.at[then])

        @pl.when(n > 0)
        def _():
            clear_rows(y_ref)
            add_windows(y_ref, bh_ref, bl_ref, *source)

        values = []
        for h_ref, l_ref, lo, rows, out, at in (
            (lh_ref, ll_ref, 0, 128, HALO, 0),
            (lh_ref, ll_ref, 128, 192, HALO + 64, HALO + 64),
            (rh_ref, rl_ref, 0, 256, own + HALO, own + HALO),
            (rh_ref, rl_ref, 256, 64, own + HALO + STEP, own + HALO + STEP),
        ):
            value = dot3(
                h_ref[lo : lo + rows], l_ref[lo : lo + rows],
                vh_ref[now, at : at + WIN], vl_ref[now, at : at + WIN],
            )
            values.append((out, rows, value))
        for out, rows, value in values:
            y_ref[out : out + rows] += value

        put(pl.ds(HALO, HALO), jnp.where(valid_ref[0] > 0, y_ref[HALO:LOW], 0.0))
        put(pl.ds(high, HALO), jnp.where(valid_ref[1] > 0, y_ref[high : high + HALO], 0.0))

        def split(i, carry):
            at = pl.multiple_of(i * chunk, chunk)
            put(pl.ds(LOW + at, chunk), y_ref[pl.ds(LOW + at, chunk), :])
            return carry

        copy = pltpu.make_async_copy(
            y_ref.at[pl.ds(LOW, own)], image_ref.at[jnp.minimum(n, ITERS - 2)], sem
        )
        pl.when(n + 1 < ITERS)(copy.start)
        lax.fori_loop(0, own // chunk, split, 0)

        xh, xl = vh_ref[now, LOW:high], vl_ref[now, LOW:high]
        zh, zl = vh_ref[then, LOW:high], vl_ref[then, LOW:high]
        by_high = dot(xh, jnp.concatenate([xh, xl, zh, zl], axis=1), tn)
        by_low = dot(xl, zh, tn)
        cross = by_high[:, cols : 2 * cols]
        keep_moment(2 * n, by_high[:, :cols] + (cross + cross.T))
        keep_moment(2 * n + 1, by_high[:, 2 * cols : 3 * cols] + (by_high[:, 3 * cols :] + by_low))
        pl.when(n + 1 < ITERS)(copy.wait)
        return carry

    lax.fori_loop(0, ITERS, power, 0)


def begin(vector, inner, outer, valid, band):
    own, cols = vector.shape
    frame = own + 2 * LOW + 64
    part = jax.ShapeDtypeStruct(band.shape, BF16)
    wide = jax.ShapeDtypeStruct((3, frame, cols), BF16)
    return pl.pallas_call(
        first_kernel,
        out_shape=(part, part, wide, wide, jax.ShapeDtypeStruct((frame, cols), F32)),
        in_specs=[pl.BlockSpec(memory_space=pltpu.SMEM)] + in_vmem(4),
        out_specs=tuple(in_vmem(5)),
        compiler_params=pltpu.CompilerParams(vmem_limit_bytes=20 << 20),
        name="begin",
    )(valid, vector, inner, outer, band)


def powers(own, begun, valid, edges):
    _, cols = begun[-1].shape
    half = jax.ShapeDtypeStruct((1024, 128), F32)
    edge = pltpu.VMEM(edges[0].shape, BF16)
    return pl.pallas_call(
        powers_kernel,
        out_shape=(
            pltpu.HBM((ITERS - 1, own, cols), F32),
            half,
            half,
            *[jax.ShapeDtypeStruct(part.shape, part.dtype) for part in begun[2:]],
        ),
        in_specs=[pl.BlockSpec(memory_space=pltpu.SMEM)] + in_vmem(7),
        out_specs=(pl.BlockSpec(memory_space=pltpu.HBM), *in_vmem(5)),
        input_output_aliases={3: 3, 4: 4, 5: 5},
        compiler_params=pltpu.CompilerParams(vmem_limit_bytes=28 << 20),
        scratch_shapes=[edge] * 4 + [pltpu.SemaphoreType.DMA],
        name="powers",
    )(valid, *begun, *edges)[:3]


def diagonals(matrix):
    size = matrix.shape[0]
    on = jnp.where(iota((size, size), 0) == iota((size, size), 1), matrix, 0.0)
    return jnp.sum(on, axis=0, keepdims=True), jnp.sum(on, axis=1, keepdims=True)


def split_dot(a, b):
    return dot3(*halves(a), *halves(b))


def inverse_spd(matrix):
    size = matrix.shape[0]
    unit = (iota((size, size), 0) == iota((size, size), 1)).astype(F32)
    along, down = diagonals(matrix)
    scale = lax.rsqrt(along) * lax.rsqrt(down)
    scaled = matrix * scale
    norm = jnp.max(jnp.sum(jnp.abs(scaled), axis=1, keepdims=True))
    factor = jnp.where(norm < 1.9, 1.0, 1.9 / norm)
    rest = unit - factor * scaled

    def going(state):
        k, worst, _, _ = state
        return (k < 40) & (size * worst * worst > 1e-9)

    def step(state):
        k, _, total, power = state
        both = full_dot(jnp.concatenate([total, power], axis=0), power)
        total = total + both[:size]
        power = both[size:]
        return k + 1, jnp.max(jnp.abs(power)), total, power

    total = factor * (unit + rest)
    power = full_dot(rest, rest)
    rounds, worst, total, power = lax.while_loop(
        going, step, (1, jnp.max(jnp.abs(power)), total, power)
    )
    worst = size * worst * worst
    total = total + full_dot(total, power)
    return total * scale, worst, rounds


def solve_fast(matrix, target):
    size = matrix.shape[0]
    direct = target.shape[1] == size
    unit = jnp.where(iota((size, size), 0) == iota((size, size), 1), 1.0, 0.0)
    along, down = diagonals(matrix)
    along, down = lax.rsqrt(along), lax.rsqrt(down)
    scaled = matrix * (along * down)
    norm = jnp.max(jnp.sum(jnp.abs(scaled), axis=1, keepdims=True), axis=0, keepdims=True)
    factor = jnp.where(norm < 1.9, 1.0, 1.9 / norm)
    power = unit - factor * scaled

    def twice(power, total):
        both = split_dot(power, jnp.concatenate([power, total], axis=1))
        return both[:, :size], total + both[:, size:]

    if direct:
        power, total = twice(power, target * (down * factor))
    else:
        total = factor * (unit + power)
        power = split_dot(power, power)
    power, total = twice(power, total)

    def left_out(power):
        return jnp.max(jnp.sum(power * power, axis=0, keepdims=True))

    def going(state):
        k, worst, _, _ = state
        return (k < 40) & (worst > CLOSE)

    def step(state):
        k, _, power, total = state
        power, total = twice(power, total)
        return k + 1, left_out(power), power, total

    rounds, worst, power, total = lax.while_loop(
        going, step, (2, left_out(power), power, total)
    )
    total = total + split_dot(power, total)
    if not direct:
        total = split_dot(total * along, target)
    return total * down, worst, rounds


def ratio(left, whole):
    return jnp.min(diagonals(left)[0] / diagonals(whole)[0])


def galerkin_kernel(core_ref, mine_ref, theirs_ref, basis_ref, out_ref, rows_ref, good_ref, mom_ref, coef_ref, stage_ref, sems):
    size = out_ref.shape[1]
    gap = jnp.zeros((64, 128), F32)
    right = iota((64, 128), 1) < 64
    upper = iota((size, size), 0) // 64 <= iota((size, size), 1) // 64

    def unpack(source_ref, start):
        for n in range(ITERS):
            at = n * PACK
            mixed = source_ref[at + 256 : at + 320]
            low = [source_ref[at : at + 64], jnp.where(right, 0.0, pltpu.roll(mixed, 64, 1)), gap, gap]
            up = [source_ref[at + 64 : at + 256], jnp.where(right, 0.0, mixed)]
            half = jnp.concatenate(
                [jnp.concatenate(low, axis=0), jnp.concatenate(up, axis=0)], axis=1
            )
            mom_ref[start + n] = jnp.where(upper, half, half.T)

    @pl.when(core_ref[0] == 0)
    def _():
        unpack(mine_ref, 0)
        unpack(theirs_ref, ITERS)

    @pl.when(core_ref[0] != 0)
    def _():
        unpack(theirs_ref, 0)
        unpack(mine_ref, ITERS)

    m = [mom_ref[n] for n in range(2 * ITERS)]
    h = [m[n + 1] + SHIFT * m[n] for n in range(2 * ITERS - 1)]

    def solved(matrix, *targets):
        wide, worst, rounds = solve_fast(matrix, jnp.concatenate(targets, axis=1))
        return [wide[:, n * size : (n + 1) * size] for n in range(len(targets))], worst, rounds

    (z01, z02, z0m), w0, k0 = solved(h[0], h[1], h[2], m[0])
    upper = split_dot(h[1], jnp.concatenate([z01, z02, z0m], axis=1))
    lower = split_dot(h[2], jnp.concatenate([z02, z0m], axis=1))
    first = h[2] - upper[:, :size]
    cross = h[3] - upper[:, size : 2 * size]
    m1 = m[1] - upper[:, 2 * size :]
    last = h[4] - lower[:, :size]
    m2 = m[2] - lower[:, size:]
    first = 0.5 * (first + first.T)
    (z12, z1m), w1, k1 = solved(first, cross, m1)
    lower = split_dot(cross.T, jnp.concatenate([z12, z1m], axis=1))
    rest = last - lower[:, :size]
    rest = 0.5 * (rest + rest.T)
    m2 = m2 - lower[:, size:]
    (y2,), w2, k2 = solved(rest, m2)
    y1 = z1m - split_dot(z12, y2)
    y0 = z0m - split_dot(jnp.concatenate([z01, z02], axis=1), jnp.concatenate([y1, y2], axis=0))
    for n, y in enumerate((y0, y1, y2)):
        coef_ref[n * size : (n + 1) * size] = y
    keep = pltpu.make_async_copy(coef_ref, out_ref, sems.at[0])
    keep.start()
    wide = coef_ref.shape[0]
    yh, yl = halves(coef_ref[...])
    sends = []
    for k in range(3):
        part = dot3(*halves(basis_ref[:, k * wide : (k + 1) * wide]), yh, yl)
        stage_ref[k] = part.reshape(rows_ref.shape[0], -1, size)
        sends.append(
            pltpu.make_async_copy(stage_ref.at[k], rows_ref.at[:, :, pl.ds(k * size, size)], sems.at[k + 1])
        )
        sends[-1].start()
    share = jnp.minimum(ratio(first, h[2]), ratio(rest, h[4]))
    rounds = jnp.maximum(k0, jnp.maximum(k1, k2))
    worst = jnp.maximum(w0, jnp.maximum(w1, w2))
    for copy in [keep, *sends]:
        copy.wait()
    good_ref[0] = jnp.where((share > GUARD) & (worst <= CLOSE) & (rounds <= ROUNDS), 1, 0)


def galerkin(core, mine, theirs, basis_rows, peers):
    slots, wide = basis_rows.shape
    size = wide // (3 * ITERS)
    smem = pl.BlockSpec(memory_space=pltpu.SMEM)
    return pl.pallas_call(
        galerkin_kernel,
        out_shape=(
            pltpu.HBM((ITERS * size, size), F32),
            pltpu.HBM((peers, slots // peers, wide // ITERS), F32),
            jax.ShapeDtypeStruct((1,), jnp.int32),
        ),
        in_specs=[smem] + in_vmem(3),
        out_specs=(*[pl.BlockSpec(memory_space=pltpu.HBM)] * 2, smem),
        scratch_shapes=[
            pltpu.VMEM((2 * ITERS, size, size), F32),
            pltpu.VMEM((ITERS * size, size), F32),
            pltpu.VMEM((3, peers, slots // peers, size), F32),
            pltpu.SemaphoreType.DMA((4,)),
        ],
        compiler_params=pltpu.CompilerParams(
            vmem_limit_bytes=32 << 20),
        name="galerkin",
    )(core, mine, theirs, basis_rows)


def solve_kernel(matrix_ref, target_ref, out_ref):
    matrix = matrix_ref[...]
    matrix = 0.5 * (matrix + matrix.T)
    inverse, _, _ = inverse_spd(matrix)
    guess = full_dot(inverse, target_ref[...])
    out_ref[...] = guess + full_dot(inverse, target_ref[...] - full_dot(matrix, guess))


def solve(matrix, target):
    return pl.pallas_call(
        solve_kernel,
        out_shape=jax.ShapeDtypeStruct(target.shape, F32),
        in_specs=in_vmem(2),
        out_specs=in_vmem(1)[0],
        name="solve",
    )(matrix, target)


def total_of(mine, theirs):
    shape = mine.shape
    chips = lax.axis_size(CHIPS)
    other = [(0, 1), (1, 0)]
    pair = mine + lax.ppermute(theirs, "core", other)
    pair = pair.reshape(chips, -1, 128)
    arrived = lax.all_to_all(pair, CHIPS, 0, 0, tiled=True)
    own = jnp.broadcast_to(arrived.sum(axis=0)[None], pair.shape)
    gathered = lax.all_to_all(own, CHIPS, 0, 0, tiled=True)
    gathered = gathered.reshape(shape)
    return gathered, lax.ppermute(gathered, "core", other)


def swap_sides(inner, outer):
    count = lax.axis_size(AXES)
    across = [(i, i + 1) for i in range(1, count - 1, 2)]
    return (
        lax.ppermute(inner, "core", [(0, 1), (1, 0)]),
        lax.ppermute(outer, AXES, across + [(b, a) for a, b in across]),
    )


def halo_of(vector):
    first = lax.axis_index("core") == 0
    head, tail = vector[:EDGE], vector[-EDGE:]
    return swap_sides(jnp.where(first, tail, head), jnp.where(first, head, tail))


def plain_cg(right_side, valid, bands):
    def times(a, b):
        return jnp.dot(a, b, preferred_element_type=F32, precision=lax.Precision.HIGHEST)

    def gram_of(lines, n):
        part = lines[n * PACK : (n + 1) * PACK]
        mixed = part[256:]
        gap = jnp.zeros((64, 64), F32)
        low = jnp.concatenate([gap, mixed[:, :64]], axis=1)
        up = jnp.concatenate([gap, mixed[:, 64:]], axis=1)
        empty = jnp.zeros((128, 128), F32)
        half = jnp.concatenate(
            [jnp.concatenate([part[:64], low, empty]), jnp.concatenate([part[64:256], up])], axis=1
        )
        block = jnp.arange(half.shape[0]) // 64
        return jnp.where(block[:, None] <= block[None, :], half, half.T)

    def step(k, state):
        answer, residual, direction, gram = state
        on_direction = k % 2 == 0
        vector = jnp.where(on_direction, direction, residual)
        begun = begin(vector, *halo_of(vector), valid, bands[0])
        image, mine, theirs = powers(vector.shape[0], begun, valid, bands[1:])
        low, high = total_of(mine, theirs)
        low = jnp.where(valid[2] == 0, low, high)
        square = gram_of(low, 0)
        gram = jnp.where(k == 0, square, gram)
        dir_gram = gram_of(low, 1) + SHIFT * square
        factor = solve(
            jnp.where(on_direction, dir_gram, gram), jnp.where(on_direction, gram, square)
        )
        along = times(direction, factor)
        applied = times(image[0] + SHIFT * vector, factor)
        answer = jnp.where(on_direction, answer + along, answer)
        direction = jnp.where(on_direction, direction, residual + along)
        residual = jnp.where(on_direction, residual - applied, residual)
        return answer, residual, direction, jnp.where(on_direction, gram, square)

    state = (jnp.zeros_like(right_side), right_side, right_side, jnp.zeros((right_side.shape[1],) * 2, F32))
    return lax.fori_loop(0, 2 * ITERS - 1, step, state)[0]


def loads_kernel(nodes_ref, load_ref, high_ref, low_ref, line_ref):
    support, slots = nodes_ref.shape
    unit = 8
    groups = slots // unit
    pairs = unit * support
    blocks = high_ref.shape[1] // 128
    wide = 3 * slots
    one = lambda mask: jnp.where(mask, 1.0, 0.0).astype(BF16)

    source = iota((wide, wide), 0)
    target = iota((wide, wide), 1)
    apart = one(source == target % slots * 3 + target // slots)
    parts = dot(jnp.concatenate(halves(load_ref[...]), axis=0), apart)

    owner = iota((groups, slots), 1) // unit == iota((groups, slots), 0)
    place = iota((slots, pairs), 0) % unit == iota((slots, pairs), 1) % unit
    turn = iota((slots, pairs), 1) // unit
    nodes = nodes_ref[...]
    fields = [parts[h * support : (h + 1) * support, k * slots : (k + 1) * slots] for k in range(3) for h in range(2)]
    fields += [(nodes // 128).astype(F32), (nodes % 128).astype(F32)]
    total = jnp.zeros((len(fields) * groups, pairs), F32)
    for s in range(support):
        spread = [jnp.where(owner, field[s : s + 1, :], 0.0) for field in fields]
        total = total + dot(jnp.concatenate(spread, axis=0).astype(BF16), one(place & (turn == s)))
    line_ref[...] = total

    own_lane = iota((unit, pairs), 1) % unit == iota((unit, pairs), 0)
    row = iota((128, pairs), 0)

    def line(n, g):
        return line_ref[pl.ds(n * groups + g, 1), :]

    def half_group(g):
        hot = one(row == line(7, g).astype(jnp.int32))
        block = jnp.broadcast_to(line(6, g).astype(jnp.int32), (unit, pairs))
        terms = [[jnp.where(own_lane, line(2 * k + h, g), 0.0) for h in range(2)] for k in range(3)]
        rows = []
        for c in range(blocks):
            hit = block == c
            for high, low in terms:
                rows.append(
                    jnp.concatenate([jnp.where(hit, high, 0.0), jnp.where(hit, low, 0.0)], axis=1)
                )
        left = jnp.concatenate(rows, axis=0).astype(BF16)
        return dot(left, jnp.concatenate([hot, hot], axis=1), ((1,), (1,)))

    def group(g, carry):
        first = half_group(2 * g)
        second = half_group(2 * g + 1)
        for c in range(blocks):
            for k in range(3):
                at = (c * 3 + k) * unit
                value = jnp.concatenate([first[at : at + unit], second[at : at + unit]], axis=0)
                high, low = halves(value)
                to = pl.multiple_of(k * slots + g * 2 * unit, 16)
                high_ref[pl.ds(to, 2 * unit), c * 128 : (c + 1) * 128] = high
                low_ref[pl.ds(to, 2 * unit), c * 128 : (c + 1) * 128] = low
        return carry

    lax.fori_loop(0, groups // 2, group, 0)


def load_matrix(slot_nodes, slot_load, rows):
    support, slots = slot_nodes.shape
    out = jax.ShapeDtypeStruct((3 * slots, rows), BF16)
    return pl.pallas_call(
        loads_kernel,
        out_shape=(out, out),
        in_specs=in_vmem(2),
        out_specs=tuple(in_vmem(2)),
        scratch_shapes=[pltpu.VMEM((slots, 8 * support), F32)],
        compiler_params=pltpu.CompilerParams(vmem_limit_bytes=24 << 20),
        name="loads",
    )(slot_nodes, slot_load)


CHUNK = 512


def basis_kernel(*refs):
    *vector_refs, wh_ref, wl_ref, out_ref = refs

    @pl.when(pl.program_id(0) == 0)
    def _():
        out_ref[...] = jnp.zeros_like(out_ref)

    slots = out_ref.shape[0]
    cols = vector_refs[0].shape[1]
    count = len(vector_refs)
    for n, ref in enumerate(vector_refs):
        full = dot3(wh_ref[...], wl_ref[...], *halves(ref[...]))
        for k in range(3):
            at = (k * count + n) * cols
            out_ref[:, at : at + cols] += full[k * slots : (k + 1) * slots]


def basis(vectors, weights):
    rows, cols = vectors[0][0].shape[-2:]
    loads = weights[0].shape[0]
    weight = pl.BlockSpec((loads, 2 * CHUNK), lambda i: (0, i))
    out = (loads // 3, 3 * len(vectors) * cols)
    return pl.pallas_call(
        basis_kernel,
        grid=(rows // (2 * CHUNK),),
        out_shape=jax.ShapeDtypeStruct(out, F32),
        in_specs=[spec for _, spec in vectors] + [weight, weight],
        out_specs=pl.BlockSpec(out, lambda i: (0, 0)),
        compiler_params=pltpu.CompilerParams(vmem_limit_bytes=28 << 20),
        name="basis",
    )(*[vector for vector, _ in vectors], *weights)


def in_chunks(vector, n=None, step=CHUNK):
    cols = vector.shape[-1]
    if n is None:
        return vector, pl.BlockSpec((step, cols), lambda i: (i, 0))
    placed = pltpu.with_memory_space_constraint(vector, pltpu.HBM)
    return placed, pl.BlockSpec((None, step, cols), lambda i: (n, i, 0))


def to_owner(rows):
    return lax.all_to_all(rows, AXES, 0, 0, tiled=True)


def combine_kernel(k0_ref, k1_ref, k2_ref, c_ref, x_ref, ch_ref, cl_ref):
    size = c_ref.shape[1]

    @pl.when(pl.program_id(0) == 0)
    def _():
        ch_ref[...], cl_ref[...] = halves(c_ref[...])

    total = jnp.zeros(x_ref.shape, F32)
    for n, ref in enumerate((k0_ref, k1_ref, k2_ref)):
        ah, al = halves(ref[...])
        at = n * size
        total = total + dot3(ah, al, ch_ref[at : at + size], cl_ref[at : at + size])
    x_ref[...] = total


def combine(vectors, coef):
    rows, cols = vectors[0][0].shape[-2:]
    return pl.pallas_call(
        combine_kernel,
        grid=(rows // CHUNK,),
        out_shape=jax.ShapeDtypeStruct((rows, cols), F32),
        in_specs=[spec for _, spec in vectors] + [pl.BlockSpec(coef.shape, lambda i: (0, 0))],
        out_specs=pl.BlockSpec((CHUNK, cols), lambda i: (i, 0)),
        scratch_shapes=[pltpu.VMEM(coef.shape, BF16)] * 2,
        compiler_params=pltpu.CompilerParams(vmem_limit_bytes=20 << 20),
        name="combine",
    )(*[vector for vector, _ in vectors], pltpu.with_memory_space_constraint(coef, pltpu.HBM))


def lead_kernel(slot_ref, received_ref, out_ref):
    peers, places, wide = received_ref.shape
    _, dipoles, cols = out_ref.shape
    left = received_ref[...].reshape(peers * places, wide)
    hot = jnp.where(iota((peers * places, dipoles), 0) == slot_ref[...], 1.0, 0.0).astype(BF16)
    picked = jnp.zeros((dipoles, wide), F32)
    for _ in range(3):
        part = left.astype(BF16)
        left = left - part.astype(F32)
        picked = picked + dot(hot, part, ((0,), (0,)))
    for k in range(3):
        out_ref[k] = picked[:, k * cols : (k + 1) * cols]


def lead(received, dipole_slot):
    out = (3, dipole_slot.shape[0], received.shape[2] // 3)
    return pl.pallas_call(
        lead_kernel,
        out_shape=jax.ShapeDtypeStruct(out, F32),
        in_specs=in_vmem(2),
        out_specs=in_vmem(1)[0],
        compiler_params=pltpu.CompilerParams(vmem_limit_bytes=20 << 20),
        name="lead",
    )(dipole_slot[None], received)


def one_device(right_side, tile_stiff, tile_nodes, node_shift, slot_nodes, slot_load, dipole_slot):
    count = lax.axis_size(AXES)
    index = lax.axis_index(AXES)
    core = lax.axis_index("core")
    valid = jnp.stack([index > 0, index < count - 1, core]).astype(jnp.int32)
    inner, outer = halo_of(right_side)
    band, inner_band, outer_band = assemble(core[None], tile_stiff, tile_nodes, node_shift)
    bands = (band, *swap_sides(inner_band, outer_band))
    weights = load_matrix(slot_nodes, slot_load, right_side.shape[0])
    begun = begin(right_side, inner, outer, valid, band)
    images, mine, theirs = powers(right_side.shape[0], begun, valid, bands[1:])
    vectors = [in_chunks(right_side), in_chunks(images, 0), in_chunks(images, 1)]
    basis_rows = basis(
        [in_chunks(right_side, None, 2 * CHUNK)]
        + [in_chunks(images, n, 2 * CHUNK) for n in range(2)],
        weights,
    )
    mine, theirs = total_of(mine, theirs)
    coef, rows, good = galerkin(core[None], mine, theirs, basis_rows, count)
    received = to_owner(rows)
    answer = combine(vectors, coef)
    leadfield = lead(received, dipole_slot)

    def exactly(_):
        exact = plain_cg(right_side, valid, bands)
        own_rows = basis([in_chunks(exact, None, 2 * CHUNK)], weights)
        received = to_owner(own_rows.reshape(count, -1, own_rows.shape[1]))
        return jnp.ones((), jnp.int32), exact, lead(received, dipole_slot)

    state = lax.while_loop(lambda state: state[0] == 0, exactly, (good[0], answer, leadfield))
    return state[1:]


def solution(mesh):
    rows, depth = mesh.devices.shape
    outer = 4 if rows % 4 == 0 else 1
    flat = Mesh(mesh.devices.reshape(outer, rows // outer, depth // 2, 2), AXES)
    return jax.shard_map(
        one_device,
        mesh=flat,
        in_specs=(
            P(AXES, None),
            P(AXES, None, None),
            P(AXES, None),
            P(AXES),
            P(None, AXES),
            P(None, AXES),
            P(AXES),
        ),
        out_specs=(P(AXES, None), P(None, AXES, None)),
        check_vma=False,
    )
```
